512 devices in a mesh: dp: 32 (over z, y_lo), expert: 16 (over x, y_hi, core).
Axes of the slice: x: 4, y: 8 (y_hi: 2, y_lo: 4; y = y_hi * 4 + y_lo), z: 8, core: 2. Of those that a mesh axis runs over, the one named last changes fastest.
Arguments:
- grad_out: bfloat16 [65536, 2880], P(('dp', 'expert')), may hold values from -256 to 256
- hidden_act: bfloat16 [65536, 4, 360], P(('dp', 'expert')), may hold values from -6 to 6
- gate_weights: bfloat16 [65536, 4], P(('dp', 'expert')), may hold values from 0.099609375 to 0.69921875
- routing: int32 [65536, 4], P(('dp', 'expert')), may hold values from 0 to 15, all different within a row; in each aligned block of 128 rows (0 to 127, 128 to 255, ...) at most 40 rows name the same one
- resp_lengths: int32 [512, 4], P(('dp', 'expert')), may hold values from 1 to 64, 128 in all within a row
- advantage: float32 [512, 4], P(('dp', 'expert')), may hold values from -4 to 4
- w_down: bfloat16 [16, 360, 2880], P('expert', None, 'dp'), may hold values from -0.3125 to 0.3125
Outputs:
- grad_down: float32 [16, 360, 2880], P('expert', None, 'dp')
- grad_hidden: float32 [65536, 4, 360], P(('dp', 'expert'))
- grad_gates: float32 [65536, 4], P(('dp', 'expert'))
The draws below stay inside these ranges and needn't reach their ends.
Inputs may be any that keep to these rules, and one draw needn't show every extreme that they name: `routing`: each token names 4 different experts; within the 128 tokens of one device no expert is named more than 40 times, a bound that some block reaches. `resp_lengths`: the 4 lengths of one device add up to 128; the largest is 64.
All inputs are finite; a program needn't handle non-finite values.
Results may differ from the reference program's by a relative error of at most 0.0041.
Values may be sent and summed in bfloat16 or wider, within the bound.
No kernel may reach another device: no remote copies, remote signals or barrier semaphores. Data moves between devices by JAX's collectives and lax.ppermute only.
A program may use at most 64 MiB of HBM per device.

```python
import math
import jax
import jax.numpy as jnp
import numpy as np
from jax import lax

D = 2880
TOPK = 4
FFW = 360
ROWS = 128
SEQ_DEV = 4
EXPERTS = 16
CAP = 40
LMAX = 64
TOKENS = 65536
N_DP = 32
N_EXPERT = 16


def spiked(entries, own_key, source, target, shards_of, factor):
    owner, partner = [(jnp.arange(entries.shape[dim]) // (entries.shape[dim] // shards_of)).reshape([-1 if axis == dim else 1 for axis in range(entries.ndim)]) for dim in (source, target)]
    chosen = jax.random.permutation(own_key, shards_of)[partner]
    strong = (owner == chosen) | (owner == (partner + shards_of // 2) % shards_of)
    return jnp.where(strong, factor * entries, entries)


def level_of(rng, dims, shards, least, top_value):
    def one(dim, shards_of):
        draws = jax.random.uniform(jax.random.fold_in(jax.random.fold_in(rng, 6), dim), (shards_of,), jnp.float32, least / len(shards), top_value / len(shards))
        return jnp.repeat(jnp.exp(draws), dims[dim] // shards_of).reshape((-1,) + (1,) * (len(dims) - dim - 1))

    level = one(*shards[0])
    for cut in shards[1:]:
        level = level * one(*cut)
    return level


def profile(count, total, most, slope):
    loads = [(1 << 20) // math.isqrt(grade ** slope) + 1 for grade in range(2, count + 1)]
    spare, given = total - most - (count - 1), [1] * (count - 1)
    while spare > 0:
        candidates = [i for i in range(count - 1) if given[i] < most]
        pool, left = sum([loads[i] for i in candidates]), spare
        for i in candidates:
            more = min(most - given[i], max(1, left * loads[i] // pool), spare)
            given[i] = given[i] + more
            spare = spare - more
    return np.array([most] + given)


def ragged(stream_key, amount, total, bound, slope):
    if amount == 2:
        one = jax.random.randint(stream_key, (), max(1, total - bound), min(bound, total - 1) + 1)
        return jnp.stack([one, total - one])
    lengths = jnp.asarray(profile(amount, total, bound, slope), jnp.int32)
    pairs = (amount - 1) // 2
    giver, taker = lengths[1:1 + 2 * pairs:2], lengths[2:2 + 2 * pairs:2]
    margin = jnp.minimum(giver - 1, bound - taker)
    shifted = jax.random.randint(jax.random.fold_in(stream_key, 1), (pairs,), 0, 1 << 20) % (margin + 1)
    lengths = lengths.at[1:1 + 2 * pairs:2].set(giver - shifted).at[2:2 + 2 * pairs:2].set(taker + shifted)
    return lengths[jax.random.permutation(jax.random.fold_in(stream_key, 2), amount)]


def shared_out(rng, own, number, rows, amount, top, reach, skew):
    ranking = jax.random.permutation(rng, amount)
    packed, common = shares(amount, rows * top, reach, skew, True), shares(amount, rows * top, reach, skew, False)
    places = jnp.arange(amount)

    def named(sizes, turn):
        used = int((sizes > 0).sum())
        fixed = max(1, used // 4)
        shifted = fixed + (places - fixed + turn * (used - fixed)) % max(1, amount - fixed)
        return jnp.zeros((amount,), jnp.int32).at[ranking[jnp.where(places < fixed, places, shifted)]].set(jnp.asarray(sizes, jnp.int32))

    sizes = jnp.where(number % 4 == 0, named(packed, number // 4), named(common, number - number // 4 - 1))
    mixed = jax.random.permutation(jax.random.fold_in(own, 3), amount)
    source_of, receiver = mixed[0:amount // 2 * 2:2], mixed[1:amount // 2 * 2:2]
    room = jnp.minimum(sizes[source_of] - 1, reach - sizes[receiver]) // 2
    room = jnp.where((source_of == ranking[0]) | (receiver == ranking[0]) | (sizes[receiver] == 0), 0, jnp.maximum(room, 0))
    shifted = jax.random.randint(jax.random.fold_in(own, 4), (amount // 2,), 0, 1 << 20) % (room + 1)
    sizes = sizes.at[source_of].add(-shifted).at[receiver].add(shifted)
    labels = jnp.searchsorted(jnp.cumsum(sizes), jnp.arange(rows * top), side="right").astype(jnp.int32)
    grid = labels.reshape(top, rows).T
    grid = grid[jax.random.permutation(jax.random.fold_in(own, 1), rows)]
    turn = jax.random.randint(jax.random.fold_in(own, 2), (rows, 1), 0, top)
    return jnp.take_along_axis(grid, (jnp.arange(top)[None, :] + turn) % top, axis=1)


def shares(count, total, limit, slope, full):
    weights = [(1 << 20) // math.isqrt(rank ** slope) + 1 for rank in range(1, count + 1)]
    largest = limit if full else min(limit, max(-(-total // count), total * weights[0] // sum(weights)))
    least = 1 if total - largest >= count - 1 else 0
    given, spare = [largest] + [least] * (count - 1), total - largest - least * (count - 1)
    while spare > 0:
        free = [i for i in range(1, count) if given[i] < largest] or [i for i in range(1, count) if given[i] < limit]
        whole, budget = sum([weights[i] for i in free]), spare
        for i in free:
            more = min(limit - given[i], max(1, budget * weights[i] // whole), spare)
            given[i] = given[i] + more
            spare = spare - more
    return np.array(given)


def normal_values(rng, dims, spread, bound, cuts=(), held_as=jnp.bfloat16):
    level = level_of(rng, dims, cuts, -0.22, 0.18) if cuts else 1.0
    drawn = jax.random.normal(rng, dims, jnp.float32) * spread * level
    return jnp.minimum(jnp.maximum(drawn, -bound), bound).astype(held_as)


def heavy_noise(key, shape, deviation, limit, split, heavy, kind=jnp.bfloat16):
    values = deviation * jax.random.normal(key, shape, jnp.float32)
    if split:
        values = values * level_of(key, shape, split, -0.22, 0.18)
    return jnp.clip(spiked(values, jax.random.fold_in(key, 3), *heavy), -limit, limit).astype(kind)


def setup_inputs(seed: int = 0) -> dict:
    seeds = jax.random.split(jax.random.key(seed), 8)
    grad_out = heavy_noise(seeds[0], (TOKENS, D), 16.0, 256.0, ((0, 512),), (0, 1, 64, 4.0))
    hidden_act = normal_values(seeds[1], (TOKENS, TOPK, FFW), 1.0, 6.0, ((0, 512),))
    gate_weights = jnp.clip(0.099609375 + 0.5996094 * jax.random.uniform(seeds[2], (TOKENS, TOPK), jnp.float32) ** level_of(seeds[2], (TOKENS, TOPK), ((0, 512),), -0.2, 0.2), 0.099609375, 0.69921875).astype(jnp.bfloat16)
    routing_keys = jax.random.split(jax.random.fold_in(seeds[3], 1), TOKENS // ROWS)
    routing_turns = jax.random.permutation(jax.random.fold_in(seeds[3], 3), TOKENS // ROWS)
    routing = jax.vmap(lambda own, number: shared_out(jax.random.fold_in(seeds[3], 2), own, number, ROWS, EXPERTS, TOPK, CAP, 2))(routing_keys, routing_turns).reshape((TOKENS, TOPK))
    resp_lengths = jax.vmap(lambda own: ragged(own, SEQ_DEV, ROWS, LMAX, 2))(jax.random.split(seeds[4], (N_DP * N_EXPERT))).reshape((N_DP * N_EXPERT, SEQ_DEV)).astype(jnp.int32)
    advantage = normal_values(seeds[5], (N_DP * N_EXPERT, SEQ_DEV), 1.0, 4.0, ((0, 512),), jnp.float32)
    w_down = normal_values(seeds[6], (EXPERTS, FFW, D), FFW ** -0.5, 0.3125, ((0, 16), (2, 32)))
    return dict(grad_out=grad_out, hidden_act=hidden_act, gate_weights=gate_weights, routing=routing, resp_lengths=resp_lengths, advantage=advantage, w_down=w_down)


def token_scale(resp_lengths, advantage):
    ends = jnp.cumsum(resp_lengths, axis=1).astype(jnp.int32)
    starts = (ends - resp_lengths).astype(jnp.int32)
    position = jnp.arange(ROWS, dtype=jnp.int32)
    inside = (position[None, :, None] >= starts[:, None, :]) & (position[None, :, None] < ends[:, None, :])
    ratio = advantage / resp_lengths.astype(advantage.dtype)
    return jnp.sum(jnp.where(inside, ratio[:, None, :], jnp.zeros((), advantage.dtype)), axis=2).reshape(-1)


def reference(grad_out, hidden_act, gate_weights, routing, resp_lengths, advantage, w_down):
    ftype = advantage.dtype
    scale = token_scale(resp_lengths, advantage)
    cotan = (scale[:, None] * grad_out.astype(ftype)).astype(jnp.bfloat16)
    items = TOKENS * TOPK
    dest = routing.reshape(-1).astype(jnp.int32)
    order = jnp.argsort(dest, stable=True).astype(jnp.int32)
    counts = jnp.sum((dest[:, None] == jnp.arange(EXPERTS, dtype=jnp.int32)[None, :]).astype(jnp.int32), axis=0).astype(jnp.int32)
    firsts = (jnp.cumsum(counts) - counts).astype(jnp.int32)
    padded = min(items, N_DP * N_EXPERT * CAP)
    order_pad = jnp.concatenate([order, jnp.full((padded,), items, jnp.int32)])
    hidden = hidden_act.reshape(items, FFW)
    gates = gate_weights.reshape(items)

    def per_expert(expert_id):
        index = lax.dynamic_slice_in_dim(order_pad, firsts[expert_id], padded)
        valid = jnp.arange(padded, dtype=jnp.int32) < counts[expert_id]
        index = jnp.where(valid, index, items).astype(jnp.int32)
        safe = jnp.minimum(index, items - 1).astype(jnp.int32)
        cot_rows = jnp.where(valid[:, None], cotan[safe // TOPK].astype(ftype), jnp.zeros((), ftype))
        hid_rows = jnp.where(valid[:, None], hidden[safe].astype(ftype), jnp.zeros((), ftype))
        gate_rows = gates[safe].astype(ftype)
        gated = (gate_rows[:, None] * cot_rows).astype(jnp.bfloat16)
        gated = lax.optimization_barrier(gated).astype(ftype)
        weight = w_down[expert_id].astype(ftype)
        dweight = jnp.dot(hid_rows.T, gated)
        back = jnp.dot(cot_rows, weight.T)
        dhid = gate_rows[:, None] * back
        output = jnp.dot(hid_rows, weight)
        dgate = jnp.sum(cot_rows * output, axis=1)
        return dweight, dhid, dgate, index

    grad_down, dhid, dgate, index = lax.map(per_expert, jnp.arange(EXPERTS, dtype=jnp.int32))
    flat_index = index.reshape(-1)
    grad_hidden = jnp.zeros((items, FFW), ftype).at[flat_index].set(dhid.reshape(-1, FFW), mode="drop")
    grad_gates = jnp.zeros((items,), ftype).at[flat_index].set(dgate.reshape(-1), mode="drop")
    return grad_down, grad_hidden.reshape(TOKENS, TOPK, FFW), grad_gates.reshape(TOKENS, TOPK)
```

```python
import functools

import jax
import jax.numpy as jnp
from jax import lax
from jax.experimental import pallas as pl
from jax.experimental.pallas import tpu as pltpu
from jax.sharding import Mesh, PartitionSpec as P

BF = jnp.bfloat16
F32 = jnp.float32
NT = (((1,), (1,)), ((), ()))
TN = (((0,), (0,)), ((), ()))
NN = (((1,), (0,)), ((), ()))
ROWS, D, TOPK, FFW, NEXP, CAP, NDP = 128, 2880, 4, 360, 16, 40, 32
OWN = D // NDP
PAD = 96
WIDE = NDP * PAD
HALF = NEXP // 2
HSLOT = HALF * CAP
VMEM = pl.BlockSpec(memory_space=pltpu.VMEM)
SMEM = pl.BlockSpec(memory_space=pltpu.SMEM)


def params(mib=40):
    return pltpu.CompilerParams(vmem_limit_bytes=mib << 20)


def prep_kernel(yh_ref, len_ref, adv_ref, g_ref, r_ref, cot_ref, pm_ref, scr):
    pos = lax.broadcasted_iota(jnp.int32, (8, ROWS), 1)
    start = jnp.int32(0)
    scale = jnp.zeros((8, ROWS), F32)
    for s in range(4):
        n = len_ref[0, s]
        ratio = jnp.full((8, ROWS), adv_ref[0, s], F32) / jnp.full((8, ROWS), n, jnp.int32).astype(F32)
        scale = jnp.where((pos >= start) & (pos < start + n), ratio, scale)
        start = start + n
    scr[0:D] = g_ref[...].astype(F32) * scale[0:1]
    scr[D:] = jnp.zeros((8, ROWS), F32)
    keep = lax.broadcasted_iota(jnp.int32, (PAD, ROWS), 0) < OWN
    for d in range(NDP):
        block = scr[d * OWN : d * OWN + PAD]
        cot_ref[d * PAD : (d + 1) * PAD] = jnp.where(keep, block, 0.0).astype(BF)
    row = lax.broadcasted_iota(jnp.int32, (NEXP, ROWS), 0)
    eid = ((row >> 1) & 3) * 4 + (row >> 3) * 2 + (row & 1)
    hit = r_ref[0:1] == eid
    for k in range(1, TOPK):
        hit = hit | (r_ref[k : k + 1] == eid)
    a = lax.broadcasted_iota(jnp.int32, (ROWS, ROWS), 0)
    b = lax.broadcasted_iota(jnp.int32, (ROWS, ROWS), 1)
    before = (a < b).astype(F32).astype(BF)
    rank = lax.dot_general(hit.astype(F32).astype(BF), before, NN, preferred_element_type=F32)
    place = jnp.where(hit, rank, -1.0)
    pm_ref[...] = place
    other = jnp.where(yh_ref[0] == 0, place[HALF:], place[:HALF])
    cot_ref[WIDE:] = jnp.concatenate([other, jnp.zeros((HALF, ROWS), F32)], axis=0).astype(BF)


def prep(yh, lens, adv, gt, rt):
    return pl.pallas_call(
        prep_kernel,
        in_specs=[SMEM, SMEM, SMEM, VMEM, VMEM],
        out_specs=[VMEM, VMEM],
        out_shape=[jax.ShapeDtypeStruct((WIDE + 16, ROWS), BF), jax.ShapeDtypeStruct((NEXP, ROWS), F32)],
        scratch_shapes=[pltpu.VMEM((D + 8, ROWS), F32)],
        compiler_params=params(),
        name="prep",
    )(yh, lens, adv, gt, rt)


def slot_onehot(place, n):
    c = lax.broadcasted_iota(jnp.int32, (n, CAP, ROWS), 1).astype(F32)
    return (place[:, None, :] == c).astype(F32).reshape(n * CAP, ROWS)


def select_kernel(yh_ref, cot_ref, pm_ref, out_ref):
    place = jnp.where(yh_ref[0] == 0, pm_ref[:HALF], pm_ref[HALF:])
    s = slot_onehot(place, HALF).astype(BF)
    step = 768
    for i in range(0, WIDE, step):
        out_ref[:, i : i + step] = lax.dot_general(
            s, cot_ref[i : i + step], NT, preferred_element_type=F32
        ).astype(BF)


def select_own(yh, cot, pm):
    return pl.pallas_call(
        select_kernel,
        in_specs=[SMEM, VMEM, VMEM],
        out_specs=VMEM,
        out_shape=jax.ShapeDtypeStruct((HSLOT, WIDE), BF),
        compiler_params=params(),
        name="select_own",
    )(yh, cot, pm)


def forward_kernel(cot_ref, out_ref):
    place = cot_ref[WIDE:].astype(F32)[:HALF]
    s = slot_onehot(place, HALF).astype(BF)
    step = 768
    for i in range(0, WIDE, step):
        out_ref[:, i : i + step] = lax.dot_general(
            s, cot_ref[i : i + step], NT, preferred_element_type=F32
        ).astype(BF)


def select_partner(cot):
    return pl.pallas_call(
        forward_kernel,
        in_specs=[VMEM],
        out_specs=VMEM,
        out_shape=jax.ShapeDtypeStruct((HSLOT, WIDE), BF),
        compiler_params=params(),
        name="select_partner",
    )(cot)


def picks(pm_ref, r_ref):
    row = lax.broadcasted_iota(jnp.int32, (NEXP, ROWS), 0)
    eid = ((row >> 1) & 3) * 4 + (row >> 3) * 2 + (row & 1)
    place = pm_ref[...]
    return [
        slot_onehot(jnp.where(r_ref[k : k + 1] == eid, place, -1.0), NEXP).astype(BF)
        for k in range(TOPK)
    ]


def hid_kernel(h_ref, gate_ref, pm_ref, r_ref, out_ref):
    acc = jnp.zeros((NEXP * CAP, FFW), F32)
    gate = gate_ref[...].astype(F32)
    for k, s in enumerate(picks(pm_ref, r_ref)):
        hs = (h_ref[k].astype(F32) * gate[k : k + 1]).astype(BF)
        acc = acc + lax.dot_general(s, hs, NT, preferred_element_type=F32)
    out_ref[...] = acc.astype(BF)


def send_hidden(ht, gt, pm, rt):
    return pl.pallas_call(
        hid_kernel,
        in_specs=[VMEM] * 4,
        out_specs=VMEM,
        out_shape=jax.ShapeDtypeStruct((NEXP * CAP, FFW), BF),
        compiler_params=params(),
        name="send_hidden",
    )(ht, gt, pm, rt)


def term_kernel(yh_ref, own_ref, par_ref, h_ref, out_ref):
    yh = yh_ref[0]
    acc = lax.dot_general(own_ref[...], h_ref[yh], TN, preferred_element_type=F32)
    acc = acc + lax.dot_general(par_ref[...], h_ref[1 - yh], TN, preferred_element_type=F32)
    out_ref[...] = acc.astype(BF)


def grad_term(yh, own, par, hid):
    step = 768
    return pl.pallas_call(
        term_kernel,
        grid=(WIDE // step,),
        in_specs=[
            SMEM,
            pl.BlockSpec((HSLOT, step), lambda i: (0, i)),
            pl.BlockSpec((HSLOT, step), lambda i: (0, i)),
            pl.BlockSpec((2, HSLOT, FFW), lambda i: (0, 0, 0)),
        ],
        out_specs=pl.BlockSpec((step, FFW), lambda i: (i, 0)),
        out_shape=jax.ShapeDtypeStruct((WIDE, FFW), BF),
        compiler_params=params(),
        name="grad_term",
    )(yh, own, par, hid)


def back_kernel(yh_ref, own_ref, par_ref, w_ref, out_ref):
    yh = yh_ref[0]
    w = w_ref[...]
    out_ref[yh] = lax.dot_general(own_ref[...], w, NN, preferred_element_type=F32).astype(BF)
    out_ref[1 - yh] = lax.dot_general(par_ref[...], w, NN, preferred_element_type=F32).astype(BF)


def back_product(yh, own, par, w):
    return pl.pallas_call(
        back_kernel,
        in_specs=[SMEM, VMEM, VMEM, VMEM],
        out_specs=VMEM,
        out_shape=jax.ShapeDtypeStruct((2, HSLOT, FFW), BF),
        compiler_params=params(),
        name="back_product",
    )(yh, own, par, w)


def sum_kernel(x_ref, out_ref):
    acc = x_ref[0].astype(F32)
    for d in range(1, NDP):
        acc = acc + x_ref[d].astype(F32)
    out_ref[...] = acc[:OWN]


def sum_terms(x):
    return pl.pallas_call(
        sum_kernel,
        in_specs=[VMEM],
        out_specs=VMEM,
        out_shape=jax.ShapeDtypeStruct((OWN, FFW), F32),
        compiler_params=params(),
        name="sum_terms",
    )(x)


def home_kernel(x_ref, h_ref, gate_ref, pm_ref, r_ref, gh_ref, gg_ref):
    x = x_ref[...]
    gate = gate_ref[...].astype(F32)
    for k, s in enumerate(picks(pm_ref, r_ref)):
        back = lax.dot_general(x, s, TN, preferred_element_type=F32)
        gh_ref[k] = back * gate[k : k + 1]
        gg_ref[k : k + 1] = jnp.sum(back * h_ref[k].astype(F32), axis=0, keepdims=True)


def bring_home(x, ht, gt, pm, rt):
    return pl.pallas_call(
        home_kernel,
        in_specs=[VMEM] * 5,
        out_specs=[VMEM, VMEM],
        out_shape=[
            jax.ShapeDtypeStruct((TOPK, FFW, ROWS), F32),
            jax.ShapeDtypeStruct((TOPK, ROWS), F32),
        ],
        compiler_params=params(),
        name="bring_home",
    )(x, ht, gt, pm, rt)


def local(grad_out, hidden_act, gate_weights, routing, resp_lengths, advantage, w_down):
    yh = lax.axis_index("yh").reshape(1).astype(jnp.int32)
    gt = grad_out.T
    ht = jnp.transpose(hidden_act, (1, 2, 0))
    gates = gate_weights.T
    rt = routing.T

    wt = jnp.pad(w_down[0].T, ((0, PAD - OWN), (0, 0)))
    w4 = lax.all_gather(wt, "yl", axis=0, tiled=True)
    weight = lax.all_gather(w4, "z", axis=0, tiled=True)

    cot, pm = prep(yh, resp_lengths, advantage, gt, rt)
    cot_par = lax.ppermute(cot, "yh", [(0, 1), (1, 0)])
    own = select_own(yh, cot, pm)
    own = lax.all_to_all(
        own.reshape(HALF, CAP, WIDE), ("x", "c"), split_axis=0, concat_axis=0, tiled=True
    ).reshape(HSLOT, WIDE)
    hid = send_hidden(ht, gates, pm, rt)
    hid = lax.all_to_all(
        hid.reshape(NEXP, CAP, FFW), ("yh", "x", "c"), split_axis=0, concat_axis=0, tiled=True
    ).reshape(2, HSLOT, FFW)
    par = select_partner(cot_par)
    par = lax.all_to_all(
        par.reshape(HALF, CAP, WIDE), ("x", "c"), split_axis=0, concat_axis=0, tiled=True
    ).reshape(HSLOT, WIDE)

    term = grad_term(yh, own, par, hid)
    terms = lax.all_to_all(
        term.reshape(NDP, PAD, FFW), ("z", "yl"), split_axis=0, concat_axis=0, tiled=True
    )
    back = back_product(yh, own, par, weight)
    back = lax.all_to_all(
        back.reshape(NEXP, CAP, FFW), ("yh", "x", "c"), split_axis=0, concat_axis=0, tiled=True
    ).reshape(NEXP * CAP, FFW)
    gh, gg = bring_home(back, ht, gates, pm, rt)
    gd = sum_terms(terms)
    return gd.T[None], jnp.transpose(gh, (2, 0, 1)), gg.T


def solution(mesh):
    fine = Mesh(mesh.devices.reshape(8, 4, 4, 2, 2), ("z", "yl", "x", "yh", "c"))
    every = ("z", "yl", "x", "yh", "c")
    rows2 = P(every, None)
    rows3 = P(every, None, None)
    cols = P(("x", "yh", "c"), None, ("z", "yl"))
    return jax.shard_map(
        local,
        mesh=fine,
        in_specs=(rows2, rows3, rows2, rows2, rows2, rows2, cols),
        out_specs=(cols, rows3, rows2),
        check_vma=False,
    )
```

```python
import jax
import jax.numpy as jnp
from jax import lax
from jax.experimental import pallas as pl
from jax.experimental.pallas import tpu as pltpu
from jax.sharding import Mesh, PartitionSpec as P

BF = jnp.bfloat16
F32 = jnp.float32
I32 = jnp.int32
NT = (((1,), (1,)), ((), ()))
TN = (((0,), (0,)), ((), ()))
NN = (((1,), (0,)), ((), ()))
ROWS, D, TOPK, FFW, NEXP, CAP = 128, 2880, 4, 360, 16, 40
NZ, NY, NX = 8, 4, 4
NDP = NZ * NY
OWN = D // NDP
PAD = 96
WIDE = NDP * PAD
HALF = NEXP // 2
HSLOT = HALF * CAP
HW = 384
COVER = 50_000_000_000
NC = 1
CY = NY // NC
CW = WIDE // NC
BLK = CY * PAD
VMEM = pl.BlockSpec(memory_space=pltpu.VMEM)
SMEM = pl.BlockSpec(memory_space=pltpu.SMEM)
ANY = pl.BlockSpec(memory_space=pltpu.HBM)


def call(body, name, ins, outs, scratch=(), mib=14, weight=None):
    outs = [jax.ShapeDtypeStruct(*o) for o in outs]
    return pl.pallas_call(
        body,
        in_specs=list(ins),
        out_specs=[VMEM] * len(outs),
        out_shape=outs,
        scratch_shapes=list(scratch),
        compiler_params=pltpu.CompilerParams(vmem_limit_bytes=mib << 20),
        name=name,
        cost_estimate=weight and pl.CostEstimate(flops=weight, transcendentals=0, bytes_accessed=0),
    )


def expert_ids():
    row = lax.broadcasted_iota(I32, (NEXP, ROWS), 0)
    return ((row >> 1) & 3) * 4 + (row >> 3) * 2 + (row & 1)


def slot_onehot(place, n):
    c = lax.broadcasted_iota(I32, (n, CAP, ROWS), 1).astype(F32)
    return (place[:, None, :] == c).astype(F32).reshape(n * CAP, ROWS)


def prep_kernel(pos_ref, len_hbm, adv_hbm, g_hbm, r_hbm, *refs):
    cots, (pm_ref, other_ref, g_ref, r_ref, len_ref, adv_ref, scr, sems) = refs[:NC], refs[NC:]
    pairs = [(g_hbm, g_ref), (r_hbm, r_ref), (len_hbm, len_ref), (adv_hbm, adv_ref)]
    copies = [pltpu.make_async_copy(a, b, sems.at[i]) for i, (a, b) in enumerate(pairs)]
    for c in copies:
        c.start()
    for c in copies[1:]:
        c.wait()
    eid = expert_ids()
    hit = r_ref[0:1] == eid
    for k in range(1, TOPK):
        hit = hit | (r_ref[k : k + 1] == eid)
    a = lax.broadcasted_iota(I32, (ROWS, ROWS), 0)
    b = lax.broadcasted_iota(I32, (ROWS, ROWS), 1)
    before = (a < b).astype(F32).astype(BF)
    rank = lax.dot_general(hit.astype(F32).astype(BF), before, NN, preferred_element_type=F32)
    place = jnp.where(hit, rank, -1.0)
    pm_ref[...] = place
    other_ref[...] = jnp.where(pos_ref[2] == 0, place[HALF:], place[:HALF])
    pos = lax.broadcasted_iota(I32, (8, ROWS), 1)
    start = jnp.int32(0)
    scale = jnp.zeros((8, ROWS), F32)
    for s in range(4):
        n = len_ref[0, s]
        ratio = jnp.full((8, ROWS), adv_ref[0, s], F32) / jnp.full((8, ROWS), n, I32).astype(F32)
        scale = jnp.where((pos >= start) & (pos < start + n), ratio, scale)
        start = start + n
    copies[0].wait()
    scr[0:D] = g_ref[...].astype(F32) * scale[0:1]
    scr[D:] = jnp.zeros((8, ROWS), F32)
    keep = lax.broadcasted_iota(I32, (PAD, ROWS), 0) < OWN
    for d in range(NDP):
        z, y = d // NY, d % NY
        block = scr[d * OWN : d * OWN + PAD]
        at = (z * CY + y % CY) * PAD
        cots[y // CY][at : at + PAD] = jnp.where(keep, block, 0.0).astype(BF)


def prep(pos, lens, adv, gt, rt):
    outs = [((CW, ROWS), BF)] * NC + [((NEXP, ROWS), F32), ((HALF, ROWS), F32)]
    scratch = [
        pltpu.VMEM((D, ROWS), BF),
        pltpu.VMEM((TOPK, ROWS), I32),
        pltpu.SMEM((1, 4), I32),
        pltpu.SMEM((1, 4), F32),
        pltpu.VMEM((D + 8, ROWS), F32),
        pltpu.SemaphoreType.DMA((4,)),
    ]
    res = call(prep_kernel, "prep", [SMEM] + [ANY] * 4, outs, scratch)(pos, lens, adv, gt, rt)
    return res[:NC], res[NC], res[NC + 1]


def spread(s, cot_ref, out_ref, at):
    step = 768
    for i in range(0, CW, step):
        out_ref[:, at + i : at + i + step] = lax.dot_general(
            s, cot_ref[i : i + step], NT, preferred_element_type=F32
        ).astype(BF)


def hidden_rows(h_ref, gate_ref, r_ref, place, eid):
    n = place.shape[0]
    acc = jnp.zeros((n * CAP, HW), F32)
    for k in range(TOPK):
        s = slot_onehot(jnp.where(r_ref[k : k + 1] == eid, place, -1.0), n).astype(BF)
        rows = jnp.concatenate(
            [h_ref[k], gate_ref[k : k + 1], jnp.zeros((HW - FFW - 1, ROWS), BF)], axis=0
        )
        acc = acc + lax.dot_general(s, rows, NT, preferred_element_type=F32)
    return acc.astype(BF)


def other_kernel(pos_ref, h_ref, gate_ref, r_ref, pm_ref, out_ref):
    first = pos_ref[2] == 0
    eid = expert_ids()
    place = jnp.where(first, pm_ref[HALF:], pm_ref[:HALF])
    out_ref[...] = hidden_rows(h_ref, gate_ref, r_ref, place, jnp.where(first, eid[HALF:], eid[:HALF]))


def own_kernel(pos_ref, h_ref, gate_ref, r_ref, pm_ref, *refs):
    cots, out_ref = refs[:NC], refs[NC]
    first = pos_ref[2] == 0
    eid = expert_ids()
    place = jnp.where(first, pm_ref[:HALF], pm_ref[HALF:])
    s = slot_onehot(place, HALF).astype(BF)
    for i, cot_ref in enumerate(cots):
        spread(s, cot_ref, out_ref, i * CW)
    out_ref[:, WIDE:] = hidden_rows(
        h_ref, gate_ref, r_ref, place, jnp.where(first, eid[:HALF], eid[HALF:])
    )


def partner_kernel(cot_ref, place_ref, h_ref, _, out_ref):
    spread(slot_onehot(place_ref[...], HALF).astype(BF), cot_ref, out_ref, 0)
    out_ref[:, CW:] = h_ref[...]


def term_kernel(js, rounded, n_after=0):
    def body(pos_ref, own_ref, par_ref, *outs):
        outs = outs[len(outs) - len(js) :]
        hid = [own_ref[:, WIDE:], par_ref[:, CW:]]
        gate = [h[:, FFW : FFW + 1].astype(F32) for h in hid]
        hid = [h[:, :FFW] for h in hid]
        for j, out_ref in zip(js, outs):
            at = pl.multiple_of(((pos_ref[0] + j) % NZ) * BLK, BLK)
            acc = jnp.zeros((BLK, FFW), F32)
            for ref, h, g in zip((own_ref, par_ref), hid, gate):
                gated = (ref[:, pl.ds(at, BLK)].astype(F32) * g).astype(BF)
                acc = acc + lax.dot_general(gated, h, TN, preferred_element_type=F32)
            out_ref[...] = acc.astype(out_ref.dtype)

    dtype = BF if rounded else F32
    return call(
        body, "grad_term", [SMEM, VMEM, VMEM] + [ANY] * n_after, [((BLK, FFW), dtype)] * len(js)
    )


def step_kernel(*refs):
    n = len(refs) // 3
    for x_ref, t_ref, out_ref in zip(refs[:n], refs[n : 2 * n], refs[-n:]):
        out_ref[...] = (x_ref[...].astype(F32) + t_ref[...]).astype(BF)


def ring_step(xs, ts, after=()):
    n, m = len(xs), len(after)

    def body(*refs):
        step_kernel(*refs[: 2 * n], *refs[2 * n + m :])

    ins = [VMEM] * (2 * n) + [ANY] * m
    return call(body, "ring_step", ins, [((BLK, FFW), BF)] * n)(*xs, *ts, *after)


def z_kernel(pos_ref, t_ref, a_ref, b_ref, keep_ref, *outs):
    for j in range(NY):
        at = pl.multiple_of(((pos_ref[1] + j) % NY) * PAD, PAD)
        rows = pl.ds(at, PAD)
        v = t_ref[rows] + (a_ref[rows].astype(F32) + b_ref[rows].astype(F32))
        if j == 0:
            keep_ref[...] = v
        else:
            outs[j - 1][...] = v.astype(BF)


def y_kernel(t_ref, a_ref, b_ref, c_ref, out_ref):
    v = (t_ref[...] + a_ref[...].astype(F32)) + (b_ref[...].astype(F32) + c_ref[...].astype(F32))
    out_ref[...] = v[:OWN]


def pad_kernel(w_ref, out_ref):
    out_ref[...] = jnp.zeros((PAD, HW), BF)
    out_ref[:OWN, :FFW] = w_ref[...]


def weight_kernel(pos_ref, *refs):
    out_ref = refs[NY]
    for j in range(NY):
        y = (pos_ref[1] + NY - j) % NY
        for z in range(NZ):
            out_ref[z, y] = refs[j][z * PAD : (z + 1) * PAD]


def back_kernel(pos_ref, own_ref, par_ref, w_ref, _, out_ref):
    yh = pos_ref[2]
    w = w_ref[:, :FFW]
    out_ref[yh] = lax.dot_general(
        own_ref[:, :WIDE], w, NN, preferred_element_type=F32
    ).astype(BF)
    out_ref[1 - yh] = lax.dot_general(
        par_ref[:, :WIDE], w, NN, preferred_element_type=F32
    ).astype(BF)


def home_kernel(x_ref, h_ref, gate_ref, pm_ref, r_ref, gh_ref, gg_ref):
    x = x_ref[...]
    gate = gate_ref[...].astype(F32)
    eid = expert_ids()
    place = pm_ref[...]
    for k in range(TOPK):
        s = slot_onehot(jnp.where(r_ref[k : k + 1] == eid, place, -1.0), NEXP).astype(BF)
        back = lax.dot_general(x, s, TN, preferred_element_type=F32)
        gh_ref[k] = back * gate[k : k + 1]
        gg_ref[k : k + 1] = jnp.sum(back * h_ref[k].astype(F32), axis=0, keepdims=True)


def shift(x, axis, n, by):
    return lax.ppermute(x, axis, [(i, (i + by) % n) for i in range(n)])


def exchange(x, axes):
    return lax.all_to_all(x, axes, split_axis=0, concat_axis=0, tiled=True)


def local(grad_out, hidden_act, gate_weights, routing, resp_lengths, advantage, w_down):
    pos = jnp.stack([lax.axis_index(a).astype(I32) for a in ("z", "yl", "yh")])
    gt = grad_out.T
    ht = jnp.transpose(hidden_act, (1, 2, 0))
    gates = gate_weights.T
    rt = routing.T

    wt = call(pad_kernel, "weight_pad", [VMEM], [((PAD, HW), BF)])(w_down[0].T)[0]
    wz = lax.all_gather(wt, "z", axis=0, tiled=True)
    cots, pm, other = prep(pos, resp_lengths, advantage, gt, rt)
    cot_par = shift(cots[0], "yh", 2, 1)
    place_par = shift(other, "yh", 2, 1)
    hid_par = call(
        other_kernel, "send_other", [SMEM] + [VMEM] * 4, [((HSLOT, HW), BF)], weight=COVER
    )(
        pos, ht, gates, rt, pm
    )[0]
    hid_par = shift(hid_par, "yh", 2, 1)
    own = call(
        own_kernel, "send_own", [SMEM] + [VMEM] * (4 + NC), [((HSLOT, WIDE + HW), BF)], weight=COVER
    )(pos, ht, gates, rt, pm, *cots)[0]
    own = exchange(own.reshape(HALF, CAP, WIDE + HW), ("x", "c")).reshape(HSLOT, WIDE + HW)

    par = call(partner_kernel, "send_partner", [VMEM] * 3 + [ANY], [((HSLOT, CW + HW), BF)])(
        cot_par, place_par, hid_par, wz
    )[0]
    parts = [wz] + [shift(wz, "yl", NY, j) for j in range(1, NY)]
    weight = call(weight_kernel, "weight_part", [SMEM] + [VMEM] * NY, [((NZ, NY, PAD, HW), BF)])(
        pos, *parts
    )[0].reshape(WIDE, HW)
    par = exchange(par.reshape(HALF, CAP, CW + HW), ("x", "c")).reshape(HSLOT, CW + HW)

    up, down = term_kernel((4, 5), True, NY - 1)(pos, own, par, *parts[1:])
    t3, t6, t2, t7, t1, t0 = term_kernel((3, 6, 2, 7, 1, 0), False)(pos, own, par)
    up, down = shift(up, "z", NZ, 1), shift(down, "z", NZ, -1)
    up, down = ring_step((up, down), (t3, t6))
    back = call(back_kernel, "back_product", [SMEM] + [VMEM] * 3 + [ANY], [((2, HSLOT, FFW), BF)])(
        pos, own, par, weight, up
    )[0]
    up, down = shift(up, "z", NZ, 1), shift(down, "z", NZ, -1)
    up, down = ring_step((up, down), (t2, t7), (back,))
    up, down = shift(up, "z", NZ, 1), shift(down, "z", NZ, -1)
    up = shift(ring_step((up,), (t1,))[0], "z", NZ, 1)
    kept, s1, s2, s3 = call(
        z_kernel, "z_sum", [SMEM] + [VMEM] * 3, [((PAD, FFW), F32)] + [((PAD, FFW), BF)] * 3
    )(pos, t0, up, down)
    got = [shift(s, "yl", NY, j + 1) for j, s in enumerate((s1, s2, s3))]
    gd = call(y_kernel, "y_sum", [VMEM] * 4, [((OWN, FFW), F32)])(kept, *got)[0]

    back = exchange(back.reshape(NEXP, CAP, FFW), ("yh", "x", "c")).reshape(NEXP * CAP, FFW)
    gh, gg = call(
        home_kernel,
        "bring_home",
        [VMEM] * 5,
        [((TOPK, FFW, ROWS), F32), ((TOPK, ROWS), F32)],
    )(back, ht, gates, pm, rt)
    return gd.T[None], jnp.transpose(gh, (2, 0, 1)), gg.T


def solution(mesh):
    every = ("z", "yl", "x", "yh", "c")
    fine = Mesh(mesh.devices.reshape(NZ, NY, NX, 2, 2), every)
    rows2 = P(every, None)
    rows3 = P(every, None, None)
    cols = P(("x", "yh", "c"), None, ("z", "yl"))
    return jax.shard_map(
        local,
        mesh=fine,
        in_specs=(rows2, rows3, rows2, rows2, rows2, rows2, cols),
        out_specs=(cols, rows3, rows2),
        check_vma=False,
    )
```

```python
import jax
import jax.numpy as jnp
from jax import lax
from jax.experimental import pallas as pl
from jax.experimental.pallas import tpu as pltpu
from jax.sharding import Mesh, PartitionSpec as P

BF = jnp.bfloat16
F32 = jnp.float32
I32 = jnp.int32
NT = (((1,), (1,)), ((), ()))
TN = (((0,), (0,)), ((), ()))
NN = (((1,), (0,)), ((), ()))
ROWS, D, TOPK, FFW, NEXP, CAP = 128, 2880, 4, 360, 16, 40
NZ, NY, NX = 8, 4, 4
NDP = NZ * NY
OWN = D // NDP
PAD = 96
WIDE = NDP * PAD
HALF = NEXP // 2
HSLOT = HALF * CAP
HW = 384
COVER = 50_000_000_000
BLK = NY * PAD
PART = PAD // 2
VMEM = pl.BlockSpec(memory_space=pltpu.VMEM)
SMEM = pl.BlockSpec(memory_space=pltpu.SMEM)
ANY = pl.BlockSpec(memory_space=pltpu.HBM)


def call(body, name, ins, outs, scratch=(), mib=14, weight=None):
    outs = [jax.ShapeDtypeStruct(*o) for o in outs]
    return pl.pallas_call(
        body,
        in_specs=list(ins),
        out_specs=[VMEM] * len(outs),
        out_shape=outs,
        scratch_shapes=list(scratch),
        compiler_params=pltpu.CompilerParams(vmem_limit_bytes=mib << 20),
        name=name,
        cost_estimate=weight and pl.CostEstimate(flops=weight, transcendentals=0, bytes_accessed=0),
    )


def expert_ids():
    row = lax.broadcasted_iota(I32, (NEXP, ROWS), 0)
    return ((row >> 1) & 3) * 4 + (row >> 3) * 2 + (row & 1)


def slot_onehot(place, n):
    c = lax.broadcasted_iota(I32, (n, CAP, ROWS), 1).astype(F32)
    return (place[:, None, :] == c).astype(F32).reshape(n * CAP, ROWS)


def prep_kernel(pos_ref, len_hbm, adv_hbm, g_hbm, r_hbm, cot_ref, pm_ref, *refs):
    g_ref, r_ref, len_ref, adv_ref, scr, sems = refs
    pairs = [(g_hbm, g_ref), (r_hbm, r_ref), (len_hbm, len_ref), (adv_hbm, adv_ref)]
    copies = [pltpu.make_async_copy(a, b, sems.at[i]) for i, (a, b) in enumerate(pairs)]
    for c in copies:
        c.start()
    for c in copies[1:]:
        c.wait()
    eid = expert_ids()
    hit = r_ref[0:1] == eid
    for k in range(1, TOPK):
        hit = hit | (r_ref[k : k + 1] == eid)
    a = lax.broadcasted_iota(I32, (ROWS, ROWS), 0)
    b = lax.broadcasted_iota(I32, (ROWS, ROWS), 1)
    before = (a < b).astype(F32).astype(BF)
    rank = lax.dot_general(hit.astype(F32).astype(BF), before, NN, preferred_element_type=F32)
    place = jnp.where(hit, rank, -1.0)
    pm_ref[...] = place
    other = jnp.where(pos_ref[2] == 0, place[HALF:], place[:HALF])
    cot_ref[WIDE:] = jnp.concatenate([other, jnp.zeros((HALF, ROWS), F32)], axis=0).astype(BF)
    pos = lax.broadcasted_iota(I32, (8, ROWS), 1)
    start = jnp.int32(0)
    scale = jnp.zeros((8, ROWS), F32)
    for s in range(4):
        n = len_ref[0, s]
        ratio = jnp.full((8, ROWS), adv_ref[0, s], F32) / jnp.full((8, ROWS), n, I32).astype(F32)
        scale = jnp.where((pos >= start) & (pos < start + n), ratio, scale)
        start = start + n
    copies[0].wait()
    scr[0:D] = g_ref[...].astype(F32) * scale[0:1]
    scr[D:] = jnp.zeros((8, ROWS), F32)
    keep = lax.broadcasted_iota(I32, (PAD, ROWS), 0) < OWN
    for d in range(NDP):
        block = scr[d * OWN : d * OWN + PAD]
        cot_ref[d * PAD : (d + 1) * PAD] = jnp.where(keep, block, 0.0).astype(BF)


def prep(pos, lens, adv, gt, rt):
    outs = [((WIDE + 16, ROWS), BF), ((NEXP, ROWS), F32)]
    scratch = [
        pltpu.VMEM((D, ROWS), BF),
        pltpu.VMEM((TOPK, ROWS), I32),
        pltpu.SMEM((1, 4), I32),
        pltpu.SMEM((1, 4), F32),
        pltpu.VMEM((D + 8, ROWS), F32),
        pltpu.SemaphoreType.DMA((4,)),
    ]
    args = [pltpu.with_memory_space_constraint(v, pltpu.HBM) for v in (lens, adv, gt, rt)]
    return call(prep_kernel, "prep", [SMEM] + [ANY] * 4, outs, scratch)(pos, *args)


def spread(s, cot_ref, out_ref):
    step = 768
    for i in range(0, WIDE, step):
        out_ref[:, i : i + step] = lax.dot_general(
            s, cot_ref[i : i + step], NT, preferred_element_type=F32
        ).astype(BF)


def hidden_rows(h_ref, gate_ref, r_ref, place, eid):
    n = place.shape[0]
    acc = jnp.zeros((n * CAP, HW), F32)
    for k in range(TOPK):
        s = slot_onehot(jnp.where(r_ref[k : k + 1] == eid, place, -1.0), n).astype(BF)
        rows = jnp.concatenate(
            [h_ref[k], gate_ref[k : k + 1], jnp.zeros((HW - FFW - 1, ROWS), BF)], axis=0
        )
        acc = acc + lax.dot_general(s, rows, NT, preferred_element_type=F32)
    return acc.astype(BF)


def other_kernel(pos_ref, h_ref, gate_ref, r_ref, pm_ref, out_ref):
    first = pos_ref[2] == 0
    eid = expert_ids()
    place = jnp.where(first, pm_ref[HALF:], pm_ref[:HALF])
    out_ref[...] = hidden_rows(h_ref, gate_ref, r_ref, place, jnp.where(first, eid[HALF:], eid[:HALF]))


def own_kernel(pos_ref, h_ref, gate_ref, r_ref, pm_ref, cot_ref, out_ref):
    first = pos_ref[2] == 0
    eid = expert_ids()
    place = jnp.where(first, pm_ref[:HALF], pm_ref[HALF:])
    spread(slot_onehot(place, HALF).astype(BF), cot_ref, out_ref)
    out_ref[:, WIDE:] = hidden_rows(
        h_ref, gate_ref, r_ref, place, jnp.where(first, eid[:HALF], eid[HALF:])
    )


def partner_kernel(cot_ref, h_ref, out_ref):
    place = cot_ref[WIDE:].astype(F32)[:HALF]
    spread(slot_onehot(place, HALF).astype(BF), cot_ref, out_ref)
    out_ref[:, WIDE:] = h_ref[...]


def term_kernel(pos_ref, own_ref, par_ref, hown_ref, hpar_ref, z_ref, keep_ref, a_ref, b_ref, c_ref, scr):
    acc = jnp.zeros((BLK, FFW), F32)
    for ref, h in ((own_ref, hown_ref), (par_ref, hpar_ref)):
        gate = h[:, FFW : FFW + 1].astype(F32)
        gated = (ref[...].astype(F32) * gate).astype(BF)
        acc = acc + lax.dot_general(gated, h[:, :FFW], TN, preferred_element_type=F32)
    scr[...] = acc
    for y in range(NY):
        z_ref[0, y] = acc[y * PAD : y * PAD + PART].astype(BF)
    for j, out_ref in enumerate((keep_ref, a_ref, b_ref, c_ref)):
        at = pl.multiple_of(((pos_ref[1] + j) % NY) * PAD + PART, 16)
        out_ref[0] = scr[pl.ds(at, PART)].astype(out_ref.dtype)


def grad_term(pos, own, par):
    cols = pl.BlockSpec((HSLOT, BLK), lambda z: (0, z))
    hid = pl.BlockSpec((HSLOT, HW), lambda z: (0, WIDE // HW))
    row = pl.BlockSpec((1, PART, FFW), lambda z: (z, 0, 0))
    return pl.pallas_call(
        term_kernel,
        grid=(NZ,),
        in_specs=[SMEM, cols, cols, hid, hid],
        out_specs=[pl.BlockSpec((1, NY, PART, FFW), lambda z: (z, 0, 0, 0))] + [row] * NY,
        out_shape=[jax.ShapeDtypeStruct((NZ, NY, PART, FFW), BF)]
        + [jax.ShapeDtypeStruct((NZ, PART, FFW), F32)]
        + [jax.ShapeDtypeStruct((NZ, PART, FFW), BF)] * (NY - 1),
        scratch_shapes=[pltpu.VMEM((BLK, FFW), F32)],
        compiler_params=pltpu.CompilerParams(vmem_limit_bytes=14 << 20),
        name="grad_term",
    )(pos, own, par, own, par)


def y_sum_kernel(keep_ref, a_ref, b_ref, c_ref, *refs):
    out_ref = refs[-1]
    for z in range(NZ):
        v = keep_ref[z] + a_ref[z].astype(F32)
        out_ref[z] = (v + (b_ref[z].astype(F32) + c_ref[z].astype(F32))).astype(BF)


def z_sum_kernel(pos_ref, x_ref, keep_ref, *outs):
    for j in range(NY):
        y = (pos_ref[1] + j) % NY
        v = x_ref[0, y].astype(F32)
        for z in range(1, NZ):
            v = v + x_ref[z, y].astype(F32)
        if j == 0:
            keep_ref[...] = v
        else:
            outs[j - 1][...] = v.astype(BF)


def last_kernel(keep_ref, a_ref, b_ref, c_ref, x_ref, out_ref):
    v = keep_ref[...] + a_ref[...].astype(F32)
    out_ref[:PART] = v + (b_ref[...].astype(F32) + c_ref[...].astype(F32))
    v = x_ref[0].astype(F32)
    for z in range(1, NZ):
        v = v + x_ref[z].astype(F32)
    out_ref[PART:] = v[: OWN - PART]


def pad_kernel(w_ref, _, out_ref):
    out_ref[...] = jnp.zeros((PAD, HW), BF)
    out_ref[:OWN, :FFW] = w_ref[...]


def weight_kernel(pos_ref, *refs):
    out_ref = refs[NY]
    for j in range(NY):
        out_ref[(pos_ref[1] + NY - j) % NY] = refs[j][...]


def peer(pos_ref, r, sign):
    dx, dc = r // 2, r % 2
    return ((pos_ref[3] + NX + sign * dx) % NX) * 2 + (pos_ref[4] + dc) % 2


def back_kernel(pos_ref, own_ref, par_ref, w_ref, *refs):
    outs, scr = refs[:HALF], refs[HALF]
    w = w_ref[:, :FFW]
    for i, ref in enumerate((own_ref, par_ref)):
        scr[...] = lax.dot_general(ref[:, :WIDE], w, NN, preferred_element_type=F32)
        for r, out_ref in enumerate(outs):
            at = pl.multiple_of(peer(pos_ref, r, 1) * CAP, 8)
            out_ref[i] = scr[pl.ds(at, CAP)].astype(BF)


def stack_kernel(*refs):
    for r in range(HALF):
        refs[HALF][r] = refs[r][1]


def home_kernel(pos_ref, h_ref, gate_ref, pm_ref, r_ref, other_ref, *refs):
    owns, gh_ref, gg_ref = refs[:HALF], refs[HALF], refs[HALF + 1]
    gate = gate_ref[...].astype(F32)
    c = lax.broadcasted_iota(I32, (CAP, ROWS), 0).astype(F32)
    yh = pos_ref[2]
    pieces, places, ids = [], [], []
    for half in range(2):
        side = yh if half == 0 else 1 - yh
        for r in range(HALF):
            i = peer(pos_ref, r, -1)
            pieces.append((owns[r][0] if half == 0 else other_ref[r]).astype(F32))
            places.append(pm_ref[pl.ds(side * HALF + i, 1)])
            ids.append((i // 2) * 4 + side * 2 + i % 2)
    x = jnp.concatenate(pieces, axis=0).astype(BF)
    for k in range(TOPK):
        rk = r_ref[k : k + 1]
        rows = [
            (jnp.where(rk == e, p, -1.0) == c).astype(F32) for p, e in zip(places, ids)
        ]
        s = jnp.concatenate(rows, axis=0).astype(BF)
        back = lax.dot_general(x, s, TN, preferred_element_type=F32)
        gh_ref[k] = back * gate[k : k + 1]
        gg_ref[k : k + 1] = jnp.sum(back * h_ref[k].astype(F32), axis=0, keepdims=True)


def shift(x, axis, n, by):
    return lax.ppermute(x, axis, [(i, (i + by) % n) for i in range(n)])


def to_peer(x, r):
    dx, dc = r // 2, r % 2
    if r == 0:
        return x
    pairs = [(i, ((i // 2 + dx) % NX) * 2 + (i + dc) % 2) for i in range(HALF)]
    return lax.ppermute(x, ("x", "c"), pairs)


def exchange(x, axes):
    return lax.all_to_all(x, axes, split_axis=0, concat_axis=0, tiled=True)


def local(grad_out, hidden_act, gate_weights, routing, resp_lengths, advantage, w_down):
    pos = jnp.stack([lax.axis_index(a).astype(I32) for a in ("z", "yl", "yh", "x", "c")])
    gt = grad_out.T
    ht = jnp.transpose(hidden_act, (1, 2, 0))
    gates = gate_weights.T
    rt = routing.T

    cot, pm = prep(pos, resp_lengths, advantage, gt, rt)
    cot_par = shift(cot, "yh", 2, 1)
    hid_par = call(
        other_kernel, "send_other", [SMEM] + [VMEM] * 4, [((HSLOT, HW), BF)], weight=COVER
    )(pos, ht, gates, rt, pm)[0]
    hid_par = shift(hid_par, "yh", 2, 1)
    own = call(
        own_kernel, "send_own", [SMEM] + [VMEM] * 5, [((HSLOT, WIDE + HW), BF)], weight=COVER
    )(pos, ht, gates, rt, pm, cot)[0]
    wt = call(pad_kernel, "weight_pad", [VMEM, ANY], [((PAD, HW), BF)])(w_down[0].T, pm)[0]
    own = exchange(own.reshape(HALF, CAP, WIDE + HW), ("x", "c")).reshape(HSLOT, WIDE + HW)

    parts = [wt] + [shift(wt, "yl", NY, j) for j in range(1, NY)]
    weight = call(weight_kernel, "weight_part", [SMEM] + [VMEM] * NY, [((NY, PAD, HW), BF)])(
        pos, *parts
    )[0].reshape(NY * PAD, HW)
    weight = lax.all_gather(weight, "z", axis=0, tiled=True)

    par = call(partner_kernel, "send_partner", [VMEM] * 2, [((HSLOT, WIDE + HW), BF)])(
        cot_par, hid_par
    )[0]
    par = exchange(par.reshape(HALF, CAP, WIDE + HW), ("x", "c")).reshape(HSLOT, WIDE + HW)

    zs, keep, *ys = grad_term(pos, own, par)
    zs = exchange(zs, "z")
    ys = [shift(y, "yl", NY, j + 1) for j, y in enumerate(ys)]
    backs = call(
        back_kernel,
        "back_product",
        [SMEM] + [VMEM] * 3,
        [((2, CAP, FFW), BF)] * HALF,
        [pltpu.VMEM((HSLOT, FFW), F32)],
    )(pos, own, par, weight)
    backs = [to_peer(b, r) for r, b in enumerate(backs)]
    ys = call(
        y_sum_kernel, "y_sum", [VMEM] * NY + [ANY] * 5, [((NZ, PART, FFW), BF)]
    )(keep, *ys, *backs[1:6])[0]
    ys = exchange(ys, "z")
    keep, *zs = call(
        z_sum_kernel,
        "z_sum",
        [SMEM, VMEM],
        [((PART, FFW), F32)] + [((PART, FFW), BF)] * (NY - 1),
    )(pos, zs)
    zs = [shift(z, "yl", NY, j + 1) for j, z in enumerate(zs)]
    gd = call(last_kernel, "last_sum", [VMEM] * (NY + 1), [((OWN, FFW), F32)])(keep, *zs, ys)[0]

    other = call(stack_kernel, "stack_other", [VMEM] * HALF, [((HALF, CAP, FFW), BF)])(*backs)[0]
    other = shift(other, "yh", 2, 1)
    gh, gg = call(
        home_kernel,
        "bring_home",
        [SMEM] + [VMEM] * (5 + HALF),
        [((TOPK, FFW, ROWS), F32), ((TOPK, ROWS), F32)],
    )(pos, ht, gates, pm, rt, other, *backs)
    return gd.T[None], jnp.transpose(gh, (2, 0, 1)), gg.T


def solution(mesh):
    every = ("z", "yl", "x", "yh", "c")
    fine = Mesh(mesh.devices.reshape(NZ, NY, NX, 2, 2), every)
    rows2 = P(every, None)
    rows3 = P(every, None, None)
    cols = P(("x", "yh", "c"), None, ("z", "yl"))
    return jax.shard_map(
        local,
        mesh=fine,
        in_specs=(rows2, rows3, rows2, rows2, rows2, rows2, cols),
        out_specs=(cols, rows3, rows2),
        check_vma=False,
    )
```

```python
import jax
import jax.numpy as jnp
from jax import lax
from jax.experimental import pallas as pl
from jax.experimental.pallas import tpu as pltpu
from jax.sharding import Mesh, PartitionSpec as P

BF = jnp.bfloat16
F32 = jnp.float32
I32 = jnp.int32
NT = (((1,), (1,)), ((), ()))
TN = (((0,), (0,)), ((), ()))
NN = (((1,), (0,)), ((), ()))
ROWS, D, TOPK, FFW, NEXP, CAP = 128, 2880, 4, 360, 16, 40
NZ, NY, NX = 8, 4, 4
NDP = NZ * NY
OWN = D // NDP
PAD = 96
WIDE = NDP * PAD
HALF = NEXP // 2
HSLOT = HALF * CAP
STEP = 768
SPREAD = [
    pltpu.VMEM((HALF * CAP, WIDE + 384), BF),
    pltpu.SemaphoreType.DMA((WIDE // STEP + 1,)),
]
HW = 384
COVER = 50_000_000_000
BLK = NY * PAD
VMEM = pl.BlockSpec(memory_space=pltpu.VMEM)
SMEM = pl.BlockSpec(memory_space=pltpu.SMEM)
ANY = pl.BlockSpec(memory_space=pltpu.HBM)


def call(body, name, ins, outs, scratch=(), mib=14, weight=None, where=None):
    outs = [(pltpu.HBM if where else jax.ShapeDtypeStruct)(*o) for o in outs]
    return pl.pallas_call(
        body,
        in_specs=list(ins),
        out_specs=[where or VMEM] * len(outs),
        out_shape=outs,
        scratch_shapes=list(scratch),
        compiler_params=pltpu.CompilerParams(vmem_limit_bytes=mib << 20),
        name=name,
        cost_estimate=weight and pl.CostEstimate(flops=weight, transcendentals=0, bytes_accessed=0),
    )


def expert_ids():
    row = lax.broadcasted_iota(I32, (NEXP, ROWS), 0)
    return ((row >> 1) & 3) * 4 + (row >> 3) * 2 + (row & 1)


def slot_onehot(place, n):
    c = lax.broadcasted_iota(I32, (n, CAP, ROWS), 1).astype(F32)
    return (place[:, None, :] == c).astype(F32).reshape(n * CAP, ROWS)


def prep_kernel(pos_ref, len_hbm, adv_hbm, g_hbm, r_hbm, cot_ref, pm_ref, *refs):
    g_ref, r_ref, len_ref, adv_ref, scr, sems = refs
    pairs = [(g_hbm, g_ref), (r_hbm, r_ref), (len_hbm, len_ref), (adv_hbm, adv_ref)]
    copies = [pltpu.make_async_copy(a, b, sems.at[i]) for i, (a, b) in enumerate(pairs)]
    for c in copies:
        c.start()
    for c in copies[1:]:
        c.wait()
    eid = expert_ids()
    hit = r_ref[0:1] == eid
    for k in range(1, TOPK):
        hit = hit | (r_ref[k : k + 1] == eid)
    a = lax.broadcasted_iota(I32, (ROWS, ROWS), 0)
    b = lax.broadcasted_iota(I32, (ROWS, ROWS), 1)
    before = (a < b).astype(F32).astype(BF)
    rank = lax.dot_general(hit.astype(F32).astype(BF), before, NN, preferred_element_type=F32)
    place = jnp.where(hit, rank, -1.0)
    pm_ref[...] = place
    other = jnp.where(pos_ref[2] == 0, place[HALF:], place[:HALF])
    cot_ref[WIDE:] = jnp.concatenate([other, jnp.zeros((HALF, ROWS), F32)], axis=0).astype(BF)
    pos = lax.broadcasted_iota(I32, (8, ROWS), 1)
    start = jnp.int32(0)
    scale = jnp.zeros((8, ROWS), F32)
    for s in range(4):
        n = len_ref[0, s]
        ratio = jnp.full((8, ROWS), adv_ref[0, s], F32) / jnp.full((8, ROWS), n, I32).astype(F32)
        scale = jnp.where((pos >= start) & (pos < start + n), ratio, scale)
        start = start + n
    copies[0].wait()
    scr[0:D] = g_ref[...].astype(F32) * scale[0:1]
    scr[D:] = jnp.zeros((8, ROWS), F32)
    keep = lax.broadcasted_iota(I32, (PAD, ROWS), 0) < OWN
    for d in range(NDP):
        block = scr[d * OWN : d * OWN + PAD]
        cot_ref[d * PAD : (d + 1) * PAD] = jnp.where(keep, block, 0.0).astype(BF)


def prep(pos, lens, adv, gt, rt):
    outs = [((WIDE + 16, ROWS), BF), ((NEXP, ROWS), F32)]
    scratch = [
        pltpu.VMEM((D, ROWS), BF),
        pltpu.VMEM((TOPK, ROWS), I32),
        pltpu.SMEM((1, 4), I32),
        pltpu.SMEM((1, 4), F32),
        pltpu.VMEM((D + 8, ROWS), F32),
        pltpu.SemaphoreType.DMA((4,)),
    ]
    args = [pltpu.with_memory_space_constraint(v, pltpu.HBM) for v in (lens, adv, gt, rt)]
    return call(prep_kernel, "prep", [SMEM] + [ANY] * 4, outs, scratch)(pos, *args)


def spread(s, cot_ref, scr, out_hbm, sems):
    copies = []
    for n, i in enumerate(range(0, WIDE, STEP)):
        cols = pl.ds(i, STEP)
        scr[:, cols] = lax.dot_general(
            s, cot_ref[i : i + STEP], NT, preferred_element_type=F32
        ).astype(BF)
        copies.append(pltpu.make_async_copy(scr.at[:, cols], out_hbm.at[:, cols], sems.at[n]))
        copies[-1].start()
    return copies


def finish(rows, copies, scr, out_hbm, sems):
    cols = pl.ds(WIDE, HW)
    scr[:, cols] = rows
    copies.append(pltpu.make_async_copy(scr.at[:, cols], out_hbm.at[:, cols], sems.at[WIDE // STEP]))
    copies[-1].start()
    for c in copies:
        c.wait()


def hidden_rows(h_ref, gate_ref, r_ref, place, eid):
    n = place.shape[0]
    acc = jnp.zeros((n * CAP, HW), F32)
    for k in range(TOPK):
        s = slot_onehot(jnp.where(r_ref[k : k + 1] == eid, place, -1.0), n).astype(BF)
        rows = jnp.concatenate(
            [h_ref[k], gate_ref[k : k + 1], jnp.zeros((HW - FFW - 1, ROWS), BF)], axis=0
        )
        acc = acc + lax.dot_general(s, rows, NT, preferred_element_type=F32)
    return acc.astype(BF)


def other_kernel(pos_ref, h_ref, gate_ref, r_ref, pm_ref, out_ref):
    first = pos_ref[2] == 0
    eid = expert_ids()
    place = jnp.where(first, pm_ref[HALF:], pm_ref[:HALF])
    out_ref[...] = hidden_rows(h_ref, gate_ref, r_ref, place, jnp.where(first, eid[HALF:], eid[:HALF]))


def own_kernel(pos_ref, h_hbm, gate_hbm, r_hbm, pm_ref, cot_ref, out_hbm, *refs):
    h_ref, gate_ref, r_ref, sem_in, scr, sems = refs
    pairs = [(h_hbm, h_ref), (gate_hbm, gate_ref), (r_hbm, r_ref)]
    loads = [pltpu.make_async_copy(a, b, sem_in.at[i]) for i, (a, b) in enumerate(pairs)]
    for c in loads:
        c.start()
    first = pos_ref[2] == 0
    eid = expert_ids()
    place = jnp.where(first, pm_ref[:HALF], pm_ref[HALF:])
    copies = spread(slot_onehot(place, HALF).astype(BF), cot_ref, scr, out_hbm, sems)
    for c in loads:
        c.wait()
    rows = hidden_rows(h_ref, gate_ref, r_ref, place, jnp.where(first, eid[:HALF], eid[HALF:]))
    finish(rows, copies, scr, out_hbm, sems)


def partner_kernel(cot_ref, h_ref, _, out_hbm, scr, sems):
    place = cot_ref[WIDE:].astype(F32)[:HALF]
    copies = spread(slot_onehot(place, HALF).astype(BF), cot_ref, scr, out_hbm, sems)
    finish(h_ref[...], copies, scr, out_hbm, sems)


def term_kernel(own_ref, par_ref, out_hbm, scr, sems):
    hid = [ref[:, WIDE:] for ref in (own_ref, par_ref)]
    gate = [h[:, FFW : FFW + 1].astype(F32) for h in hid]
    copies = []
    for z in range(NZ):
        acc = jnp.zeros((BLK, FFW), F32)
        for ref, h, g in zip((own_ref, par_ref), hid, gate):
            gated = (ref[:, z * BLK : (z + 1) * BLK].astype(F32) * g).astype(BF)
            acc = acc + lax.dot_general(gated, h[:, :FFW], TN, preferred_element_type=F32)
        rows = pl.ds(z * BLK, BLK)
        scr[rows] = acc.astype(BF)
        copies.append(pltpu.make_async_copy(scr.at[rows], out_hbm.at[rows], sems.at[z]))
        copies[-1].start()
    for c in copies:
        c.wait()


def sum_kernel(x_ref, _, out_ref):
    v = x_ref[0].astype(F32)
    for d in range(1, NDP):
        v = v + x_ref[d].astype(F32)
    out_ref[...] = v[:OWN]


def pad_kernel(w_ref, _, out_ref):
    out_ref[...] = jnp.zeros((PAD, HW), BF)
    out_ref[:OWN, :FFW] = w_ref[...]


def weight_kernel(pos_ref, *refs):
    out_ref = refs[NY]
    for j in range(NY):
        out_ref[(pos_ref[1] + NY - j) % NY] = refs[j][...]


def peer(pos_ref, r, sign):
    dx, dc = r // 2, r % 2
    return ((pos_ref[3] + NX + sign * dx) % NX) * 2 + (pos_ref[4] + dc) % 2


def back_kernel(pos_ref, own_ref, par_ref, w_ref, *refs):
    outs, scr = refs[:HALF], refs[HALF]
    w = w_ref[:, :FFW]
    for i, ref in enumerate((own_ref, par_ref)):
        scr[...] = lax.dot_general(ref[:, :WIDE], w, NN, preferred_element_type=F32)
        for r, out_ref in enumerate(outs):
            at = pl.multiple_of(peer(pos_ref, r, 1) * CAP, 8)
            out_ref[i] = scr[pl.ds(at, CAP)].astype(BF)


def stack_kernel(*refs):
    for r in range(HALF):
        refs[HALF][r] = refs[r][1]


def home_kernel(pos_ref, h_ref, gate_ref, pm_ref, r_ref, other_ref, *refs):
    owns, gh_ref, gg_ref = refs[:HALF], refs[HALF], refs[HALF + 1]
    gate = gate_ref[...].astype(F32)
    c = lax.broadcasted_iota(I32, (CAP, ROWS), 0).astype(F32)
    yh = pos_ref[2]
    pieces, places, ids = [], [], []
    for half in range(2):
        side = yh if half == 0 else 1 - yh
        for r in range(HALF):
            i = peer(pos_ref, r, -1)
            pieces.append((owns[r][0] if half == 0 else other_ref[r]).astype(F32))
            places.append(pm_ref[pl.ds(side * HALF + i, 1)])
            ids.append((i // 2) * 4 + side * 2 + i % 2)
    x = jnp.concatenate(pieces, axis=0).astype(BF)
    for k in range(TOPK):
        rk = r_ref[k : k + 1]
        rows = [
            (jnp.where(rk == e, p, -1.0) == c).astype(F32) for p, e in zip(places, ids)
        ]
        s = jnp.concatenate(rows, axis=0).astype(BF)
        back = lax.dot_general(x, s, TN, preferred_element_type=F32)
        gh_ref[k] = back * gate[k : k + 1]
        gg_ref[k : k + 1] = jnp.sum(back * h_ref[k].astype(F32), axis=0, keepdims=True)


def shift(x, axis, n, by):
    return lax.ppermute(x, axis, [(i, (i + by) % n) for i in range(n)])


def to_peer(x, r):
    dx, dc = r // 2, r % 2
    if r == 0:
        return x
    pairs = [(i, ((i // 2 + dx) % NX) * 2 + (i + dc) % 2) for i in range(HALF)]
    return lax.ppermute(x, ("x", "c"), pairs)


def exchange(x, axes):
    return lax.all_to_all(x, axes, split_axis=0, concat_axis=0, tiled=True)


def local(grad_out, hidden_act, gate_weights, routing, resp_lengths, advantage, w_down):
    pos = jnp.stack([lax.axis_index(a).astype(I32) for a in ("z", "yl", "yh", "x", "c")])
    gt = grad_out.T
    ht = jnp.transpose(hidden_act, (1, 2, 0))
    gates = gate_weights.T
    rt = routing.T

    cot, pm = prep(pos, resp_lengths, advantage, gt, rt)
    cot_par = shift(cot, "yh", 2, 1)
    hid_par = call(
        other_kernel, "send_other", [SMEM] + [VMEM] * 4, [((HSLOT, HW), BF)], weight=COVER
    )(pos, ht, gates, rt, pm)[0]
    hid_par = shift(hid_par, "yh", 2, 1)
    own = call(
        own_kernel,
        "send_own",
        [SMEM] + [ANY] * 3 + [VMEM] * 2,
        [((HSLOT, WIDE + HW), BF)],
        [
            pltpu.VMEM((TOPK, FFW, ROWS), BF),
            pltpu.VMEM((TOPK, ROWS), BF),
            pltpu.VMEM((TOPK, ROWS), I32),
            pltpu.SemaphoreType.DMA((3,)),
        ]
        + SPREAD,
        where=ANY,
    )(pos, *(pltpu.with_memory_space_constraint(v, pltpu.HBM) for v in (ht, gates, rt)), pm, cot)[0]
    wt = call(pad_kernel, "weight_pad", [VMEM, ANY], [((PAD, HW), BF)])(w_down[0].T, pm)[0]
    own = exchange(own.reshape(HALF, CAP, WIDE + HW), ("x", "c")).reshape(HSLOT, WIDE + HW)

    parts = [wt] + [shift(wt, "yl", NY, j) for j in range(1, NY)]
    weight = call(weight_kernel, "weight_part", [SMEM] + [VMEM] * NY, [((NY, PAD, HW), BF)])(
        pos, *parts
    )[0].reshape(NY * PAD, HW)

    par = call(partner_kernel, "send_partner", [VMEM] * 2 + [ANY], [((HSLOT, WIDE + HW), BF)], SPREAD, where=ANY)(
        cot_par, hid_par, weight
    )[0]
    par = exchange(par.reshape(HALF, CAP, WIDE + HW), ("x", "c")).reshape(HSLOT, WIDE + HW)

    weight = lax.all_gather(weight, "z", axis=0, tiled=True)

    terms = call(
        term_kernel,
        "grad_term",
        [VMEM] * 2,
        [((WIDE, FFW), BF)],
        [pltpu.VMEM((WIDE, FFW), BF), pltpu.SemaphoreType.DMA((NZ,))],
        mib=20,
        where=ANY,
    )(own, par)[0].reshape(NDP, PAD, FFW)
    terms = exchange(terms, ("z", "yl"))

    backs = call(
        back_kernel,
        "back_product",
        [SMEM] + [VMEM] * 3,
        [((2, CAP, FFW), BF)] * HALF,
        [pltpu.VMEM((HSLOT, FFW), F32)],
    )(pos, own, par, weight)
    backs = [to_peer(b, r) for r, b in enumerate(backs)]
    other = call(stack_kernel, "stack_other", [VMEM] * HALF, [((HALF, CAP, FFW), BF)])(*backs)[0]
    other = shift(other, "yh", 2, 1)
    gh, gg = call(
        home_kernel,
        "bring_home",
        [SMEM] + [VMEM] * (5 + HALF),
        [((TOPK, FFW, ROWS), F32), ((TOPK, ROWS), F32)],
    )(pos, ht, gates, pm, rt, other, *backs)
    gd = call(sum_kernel, "sum_terms", [VMEM, ANY], [((OWN, FFW), F32)])(terms, gg)[0]
    return gd.T[None], jnp.transpose(gh, (2, 0, 1)), gg.T


def solution(mesh):
    every = ("z", "yl", "x", "yh", "c")
    fine = Mesh(mesh.devices.reshape(NZ, NY, NX, 2, 2), every)
    rows2 = P(every, None)
    rows3 = P(every, None, None)
    cols = P(("x", "yh", "c"), None, ("z", "yl"))
    return jax.shard_map(
        local,
        mesh=fine,
        in_specs=(rows2, rows3, rows2, rows2, rows2, rows2, cols),
        out_specs=(cols, rows3, rows2),
        check_vma=False,
    )
```

```python
import jax
import jax.numpy as jnp
from jax import lax
from jax.experimental import pallas as pl
from jax.experimental.pallas import tpu as pltpu
from jax.sharding import Mesh, PartitionSpec as P

BF = jnp.bfloat16
F32 = jnp.float32
I32 = jnp.int32
NT = (((1,), (1,)), ((), ()))
TN = (((0,), (0,)), ((), ()))
NN = (((1,), (0,)), ((), ()))
ROWS, D, TOPK, FFW, NEXP, CAP = 128, 2880, 4, 360, 16, 40
NZ, NY, NX = 8, 4, 4
NDP = NZ * NY
OWN = D // NDP
PAD = 96
WIDE = NDP * PAD
HALF = NEXP // 2
HSLOT = HALF * CAP
STEP = 768
SPREAD = [
    pltpu.VMEM((HALF * CAP, WIDE + 384), BF),
    pltpu.SemaphoreType.DMA((WIDE // STEP + 1,)),
]
HW = 384
NAG = 1
COVER = 50_000_000_000
BLK = NY * PAD
VMEM = pl.BlockSpec(memory_space=pltpu.VMEM)
SMEM = pl.BlockSpec(memory_space=pltpu.SMEM)
ANY = pl.BlockSpec(memory_space=pltpu.HBM)


def call(body, name, ins, outs, scratch=(), mib=14, weight=None, where=None):
    outs = [(pltpu.HBM if where else jax.ShapeDtypeStruct)(*o) for o in outs]
    return pl.pallas_call(
        body,
        in_specs=list(ins),
        out_specs=[where or VMEM] * len(outs),
        out_shape=outs,
        scratch_shapes=list(scratch),
        compiler_params=pltpu.CompilerParams(vmem_limit_bytes=mib << 20),
        name=name,
        cost_estimate=weight and pl.CostEstimate(flops=weight, transcendentals=0, bytes_accessed=0),
    )


def expert_ids():
    row = lax.broadcasted_iota(I32, (NEXP, ROWS), 0)
    return ((row >> 1) & 3) * 4 + (row >> 3) * 2 + (row & 1)


def slot_onehot(place, n):
    c = lax.broadcasted_iota(I32, (n, CAP, ROWS), 1).astype(F32)
    return (place[:, None, :] == c).astype(F32).reshape(n * CAP, ROWS)


def prep_kernel(pos_ref, len_hbm, adv_hbm, g_hbm, r_hbm, _, cot_ref, pm_ref, *refs):
    g_ref, r_ref, len_ref, adv_ref, scr, sems = refs
    pairs = [(g_hbm, g_ref), (r_hbm, r_ref), (len_hbm, len_ref), (adv_hbm, adv_ref)]
    copies = [pltpu.make_async_copy(a, b, sems.at[i]) for i, (a, b) in enumerate(pairs)]
    for c in copies:
        c.start()
    for c in copies[1:]:
        c.wait()
    eid = expert_ids()
    hit = r_ref[0:1] == eid
    for k in range(1, TOPK):
        hit = hit | (r_ref[k : k + 1] == eid)
    a = lax.broadcasted_iota(I32, (ROWS, ROWS), 0)
    b = lax.broadcasted_iota(I32, (ROWS, ROWS), 1)
    before = (a < b).astype(F32).astype(BF)
    rank = lax.dot_general(hit.astype(F32).astype(BF), before, NN, preferred_element_type=F32)
    place = jnp.where(hit, rank, -1.0)
    pm_ref[...] = place
    other = jnp.where(pos_ref[2] == 0, place[HALF:], place[:HALF])
    cot_ref[WIDE:] = jnp.concatenate([other, jnp.zeros((HALF, ROWS), F32)], axis=0).astype(BF)
    pos = lax.broadcasted_iota(I32, (8, ROWS), 1)
    start = jnp.int32(0)
    scale = jnp.zeros((8, ROWS), F32)
    for s in range(4):
        n = len_ref[0, s]
        ratio = jnp.full((8, ROWS), adv_ref[0, s], F32) / jnp.full((8, ROWS), n, I32).astype(F32)
        scale = jnp.where((pos >= start) & (pos < start + n), ratio, scale)
        start = start + n
    copies[0].wait()
    scr[0:D] = g_ref[...].astype(F32) * scale[0:1]
    scr[D:] = jnp.zeros((8, ROWS), F32)
    keep = lax.broadcasted_iota(I32, (PAD, ROWS), 0) < OWN
    for d in range(NDP):
        block = scr[d * OWN : d * OWN + PAD]
        cot_ref[d * PAD : (d + 1) * PAD] = jnp.where(keep, block, 0.0).astype(BF)


def prep(pos, lens, adv, gt, rt, first):
    outs = [((WIDE + 16, ROWS), BF), ((NEXP, ROWS), F32)]
    scratch = [
        pltpu.VMEM((D, ROWS), BF),
        pltpu.VMEM((TOPK, ROWS), I32),
        pltpu.SMEM((1, 4), I32),
        pltpu.SMEM((1, 4), F32),
        pltpu.VMEM((D + 8, ROWS), F32),
        pltpu.SemaphoreType.DMA((4,)),
    ]
    args = [pltpu.with_memory_space_constraint(v, pltpu.HBM) for v in (lens, adv, gt, rt)]
    return call(prep_kernel, "prep", [SMEM] + [ANY] * 5, outs, scratch)(pos, *args, first)


def spread(s, cot_ref, scr, out_hbm, sems):
    copies = []
    for n, i in enumerate(range(0, WIDE, STEP)):
        cols = pl.ds(i, STEP)
        scr[:, cols] = lax.dot_general(
            s, cot_ref[i : i + STEP], NT, preferred_element_type=F32
        ).astype(BF)
        copies.append(pltpu.make_async_copy(scr.at[:, cols], out_hbm.at[:, cols], sems.at[n]))
        copies[-1].start()
    return copies


def finish(rows, copies, scr, out_hbm, sems):
    cols = pl.ds(WIDE, HW)
    scr[:, cols] = rows
    copies.append(pltpu.make_async_copy(scr.at[:, cols], out_hbm.at[:, cols], sems.at[WIDE // STEP]))
    copies[-1].start()
    for c in copies:
        c.wait()


def hidden_rows(h_ref, gate_ref, r_ref, place, eid):
    n = place.shape[0]
    acc = jnp.zeros((n * CAP, HW), F32)
    for k in range(TOPK):
        s = slot_onehot(jnp.where(r_ref[k : k + 1] == eid, place, -1.0), n).astype(BF)
        rows = jnp.concatenate(
            [h_ref[k], gate_ref[k : k + 1], jnp.zeros((HW - FFW - 1, ROWS), BF)], axis=0
        )
        acc = acc + lax.dot_general(s, rows, NT, preferred_element_type=F32)
    return acc.astype(BF)


def other_kernel(pos_ref, h_ref, gate_ref, r_ref, pm_ref, out_ref):
    first = pos_ref[2] == 0
    eid = expert_ids()
    place = jnp.where(first, pm_ref[HALF:], pm_ref[:HALF])
    out_ref[...] = hidden_rows(h_ref, gate_ref, r_ref, place, jnp.where(first, eid[HALF:], eid[:HALF]))


def own_kernel(pos_ref, h_hbm, gate_hbm, r_hbm, pm_ref, cot_ref, out_hbm, *refs):
    h_ref, gate_ref, r_ref, sem_in, scr, sems = refs
    pairs = [(h_hbm, h_ref), (gate_hbm, gate_ref), (r_hbm, r_ref)]
    loads = [pltpu.make_async_copy(a, b, sem_in.at[i]) for i, (a, b) in enumerate(pairs)]
    for c in loads:
        c.start()
    first = pos_ref[2] == 0
    eid = expert_ids()
    place = jnp.where(first, pm_ref[:HALF], pm_ref[HALF:])
    copies = spread(slot_onehot(place, HALF).astype(BF), cot_ref, scr, out_hbm, sems)
    for c in loads:
        c.wait()
    rows = hidden_rows(h_ref, gate_ref, r_ref, place, jnp.where(first, eid[:HALF], eid[HALF:]))
    finish(rows, copies, scr, out_hbm, sems)


def partner_kernel(cot_ref, h_ref, out_hbm, scr, sems):
    place = cot_ref[WIDE:].astype(F32)[:HALF]
    copies = spread(slot_onehot(place, HALF).astype(BF), cot_ref, scr, out_hbm, sems)
    finish(h_ref[...], copies, scr, out_hbm, sems)


def term_kernel(own_ref, par_ref, *refs):
    out_hbm, scr, sems = refs[-3:]
    hid = [ref[:, WIDE:] for ref in (own_ref, par_ref)]
    gate = [h[:, FFW : FFW + 1].astype(F32) for h in hid]
    copies = []
    for z in range(NZ):
        acc = jnp.zeros((BLK, FFW), F32)
        for ref, h, g in zip((own_ref, par_ref), hid, gate):
            gated = (ref[:, z * BLK : (z + 1) * BLK].astype(F32) * g).astype(BF)
            acc = acc + lax.dot_general(gated, h[:, :FFW], TN, preferred_element_type=F32)
        rows = pl.ds(z * BLK, BLK)
        scr[rows] = acc.astype(BF)
        copies.append(pltpu.make_async_copy(scr.at[rows], out_hbm.at[rows], sems.at[z]))
        copies[-1].start()
    for c in copies:
        c.wait()


def sum_kernel(x_ref, _, out_ref):
    v = x_ref[0].astype(F32)
    for d in range(1, NDP):
        v = v + x_ref[d].astype(F32)
    out_ref[...] = v[:OWN]


def pad_kernel(w_ref, out_ref):
    out_ref[...] = jnp.zeros((PAD, HW), BF)
    out_ref[:OWN, :FFW] = w_ref[...]


def weight_kernel(pos_ref, *refs):
    out_ref = refs[NY]
    for j in range(NY):
        out_ref[(pos_ref[1] + NY - j) % NY] = refs[j][...]


def peer(pos_ref, r, sign):
    dx, dc = r // 2, r % 2
    return ((pos_ref[3] + NX + sign * dx) % NX) * 2 + (pos_ref[4] + dc) % 2


def back_kernel(pos_ref, own_ref, par_ref, *refs):
    ws, outs, scr = refs[:NAG], refs[NAG : NAG + HALF], refs[NAG + HALF]
    n = BLK // NAG
    w = jnp.concatenate(
        [ref[z * n : (z + 1) * n, :FFW] for z in range(NZ) for ref in ws], axis=0
    )
    for i, ref in enumerate((own_ref, par_ref)):
        scr[...] = lax.dot_general(ref[:, :WIDE], w, NN, preferred_element_type=F32)
        for r, out_ref in enumerate(outs):
            at = pl.multiple_of(peer(pos_ref, r, 1) * CAP, 8)
            out_ref[i] = scr[pl.ds(at, CAP)].astype(BF)


def stack_kernel(*refs):
    for r in range(HALF):
        refs[HALF][r] = refs[r][1]


def home_kernel(pos_ref, h_ref, gate_ref, pm_ref, r_ref, other_ref, *refs):
    owns, gh_ref, gg_ref = refs[:HALF], refs[HALF], refs[HALF + 1]
    gate = gate_ref[...].astype(F32)
    c = lax.broadcasted_iota(I32, (CAP, ROWS), 0).astype(F32)
    yh = pos_ref[2]
    pieces, places, ids = [], [], []
    for half in range(2):
        side = yh if half == 0 else 1 - yh
        for r in range(HALF):
            i = peer(pos_ref, r, -1)
            pieces.append((owns[r][0] if half == 0 else other_ref[r]).astype(F32))
            places.append(pm_ref[pl.ds(side * HALF + i, 1)])
            ids.append((i // 2) * 4 + side * 2 + i % 2)
    x = jnp.concatenate(pieces, axis=0).astype(BF)
    for k in range(TOPK):
        rk = r_ref[k : k + 1]
        rows = [
            (jnp.where(rk == e, p, -1.0) == c).astype(F32) for p, e in zip(places, ids)
        ]
        s = jnp.concatenate(rows, axis=0).astype(BF)
        back = lax.dot_general(x, s, TN, preferred_element_type=F32)
        gh_ref[k] = back * gate[k : k + 1]
        gg_ref[k : k + 1] = jnp.sum(back * h_ref[k].astype(F32), axis=0, keepdims=True)


def shift(x, axis, n, by):
    return lax.ppermute(x, axis, [(i, (i + by) % n) for i in range(n)])


def to_peer(x, r):
    dx, dc = r // 2, r % 2
    if r == 0:
        return x
    pairs = [(i, ((i // 2 + dx) % NX) * 2 + (i + dc) % 2) for i in range(HALF)]
    return lax.ppermute(x, ("x", "c"), pairs)


def exchange(x, axes):
    return lax.all_to_all(x, axes, split_axis=0, concat_axis=0, tiled=True)


def local(grad_out, hidden_act, gate_weights, routing, resp_lengths, advantage, w_down):
    pos = jnp.stack([lax.axis_index(a).astype(I32) for a in ("z", "yl", "yh", "x", "c")])
    gt = grad_out.T
    ht = jnp.transpose(hidden_act, (1, 2, 0))
    gates = gate_weights.T
    rt = routing.T

    wt = call(pad_kernel, "weight_pad", [VMEM], [((PAD, HW), BF)])(w_down[0].T)[0]
    parts = [wt] + [shift(wt, "yl", NY, j) for j in range(1, NY)]
    w4 = call(weight_kernel, "weight_part", [SMEM] + [VMEM] * NY, [((NY, PAD, HW), BF)])(
        pos, *parts
    )[0].reshape(NY * PAD, HW)
    weight = []
    for i in range(NAG):
        piece = w4[i * (BLK // NAG) : (i + 1) * (BLK // NAG)]
        if weight:
            piece, _ = lax.optimization_barrier((piece, weight[-1]))
        weight.append(lax.all_gather(piece, "z", axis=0, tiled=True))

    cot, pm = prep(pos, resp_lengths, advantage, gt, rt, w4)
    cot_par = shift(cot, "yh", 2, 1)
    hid_par = call(
        other_kernel, "send_other", [SMEM] + [VMEM] * 4, [((HSLOT, HW), BF)], weight=COVER
    )(pos, ht, gates, rt, pm)[0]
    hid_par = shift(hid_par, "yh", 2, 1)
    own = call(
        own_kernel,
        "send_own",
        [SMEM] + [ANY] * 3 + [VMEM] * 2,
        [((HSLOT, WIDE + HW), BF)],
        [
            pltpu.VMEM((TOPK, FFW, ROWS), BF),
            pltpu.VMEM((TOPK, ROWS), BF),
            pltpu.VMEM((TOPK, ROWS), I32),
            pltpu.SemaphoreType.DMA((3,)),
        ]
        + SPREAD,
        where=ANY,
    )(pos, *(pltpu.with_memory_space_constraint(v, pltpu.HBM) for v in (ht, gates, rt)), pm, cot)[0]
    own = exchange(own.reshape(HALF, CAP, WIDE + HW), ("x", "c")).reshape(HSLOT, WIDE + HW)

    par = call(partner_kernel, "send_partner", [VMEM] * 2, [((HSLOT, WIDE + HW), BF)], SPREAD, where=ANY)(
        cot_par, hid_par
    )[0]
    par = exchange(par.reshape(HALF, CAP, WIDE + HW), ("x", "c")).reshape(HSLOT, WIDE + HW)

    terms = call(
        term_kernel,
        "grad_term",
        [VMEM] * 2 + [ANY] * NAG,
        [((WIDE, FFW), BF)],
        [pltpu.VMEM((WIDE, FFW), BF), pltpu.SemaphoreType.DMA((NZ,))],
        mib=20,
        where=ANY,
    )(own, par, *weight)[0].reshape(NDP, PAD, FFW)
    terms = exchange(terms, ("z", "yl"))

    backs = call(
        back_kernel,
        "back_product",
        [SMEM] + [VMEM] * (2 + NAG),
        [((2, CAP, FFW), BF)] * HALF,
        [pltpu.VMEM((HSLOT, FFW), F32)],
        mib=20,
    )(pos, own, par, *weight)
    backs = [to_peer(b, r) for r, b in enumerate(backs)]
    other = call(stack_kernel, "stack_other", [VMEM] * HALF, [((HALF, CAP, FFW), BF)])(*backs)[0]
    other = shift(other, "yh", 2, 1)
    gh, gg = call(
        home_kernel,
        "bring_home",
        [SMEM] + [VMEM] * (5 + HALF),
        [((TOPK, FFW, ROWS), F32), ((TOPK, ROWS), F32)],
    )(pos, ht, gates, pm, rt, other, *backs)
    gd = call(sum_kernel, "sum_terms", [VMEM, ANY], [((OWN, FFW), F32)])(terms, gg)[0]
    return gd.T[None], jnp.transpose(gh, (2, 0, 1)), gg.T


def solution(mesh):
    every = ("z", "yl", "x", "yh", "c")
    fine = Mesh(mesh.devices.reshape(NZ, NY, NX, 2, 2), every)
    rows2 = P(every, None)
    rows3 = P(every, None, None)
    cols = P(("x", "yh", "c"), None, ("z", "yl"))
    return jax.shard_map(
        local,
        mesh=fine,
        in_specs=(rows2, rows3, rows2, rows2, rows2, rows2, cols),
        out_specs=(cols, rows3, rows2),
        check_vma=False,
    )
```

```python
import jax
import jax.numpy as jnp
from jax import lax
from jax.experimental import pallas as pl
from jax.experimental.pallas import tpu as pltpu
from jax.sharding import Mesh, PartitionSpec as P

BF = jnp.bfloat16
F32 = jnp.float32
I32 = jnp.int32
NT = (((1,), (1,)), ((), ()))
TN = (((0,), (0,)), ((), ()))
NN = (((1,), (0,)), ((), ()))
ROWS, D, TOPK, FFW, NEXP, CAP = 128, 2880, 4, 360, 16, 40
NZ, NY, NX = 8, 4, 4
NDP = NZ * NY
OWN = D // NDP
PAD = 96
WIDE = NDP * PAD
HALF = NEXP // 2
HSLOT = HALF * CAP
STEP = 768
HW = 384
COVER = 50_000_000_000
BLK = NY * PAD
CW = WIDE // 2
def spread_scratch(width):
    return [pltpu.VMEM((HSLOT, width), BF), pltpu.SemaphoreType.DMA((WIDE // STEP + 1,))]


VMEM = pl.BlockSpec(memory_space=pltpu.VMEM)
SMEM = pl.BlockSpec(memory_space=pltpu.SMEM)
ANY = pl.BlockSpec(memory_space=pltpu.HBM)


def call(body, name, ins, outs, scratch=(), mib=14, weight=None, where=None):
    outs = [(pltpu.HBM if where else jax.ShapeDtypeStruct)(*o) for o in outs]
    return pl.pallas_call(
        body,
        in_specs=list(ins),
        out_specs=[where or VMEM] * len(outs),
        out_shape=outs,
        scratch_shapes=list(scratch),
        compiler_params=pltpu.CompilerParams(vmem_limit_bytes=mib << 20),
        name=name,
        cost_estimate=weight and pl.CostEstimate(flops=weight, transcendentals=0, bytes_accessed=0),
    )


def expert_ids():
    row = lax.broadcasted_iota(I32, (NEXP, ROWS), 0)
    return ((row >> 1) & 3) * 4 + (row >> 3) * 2 + (row & 1)


def slot_onehot(place, n):
    c = lax.broadcasted_iota(I32, (n, CAP, ROWS), 1).astype(F32)
    return (place[:, None, :] == c).astype(F32).reshape(n * CAP, ROWS)


def prep_kernel(pos_ref, len_hbm, adv_hbm, g_hbm, r_hbm, low_ref, high_ref, pm_ref, *refs):
    g_ref, r_ref, len_ref, adv_ref, scr, sems = refs
    pairs = [(g_hbm, g_ref), (r_hbm, r_ref), (len_hbm, len_ref), (adv_hbm, adv_ref)]
    copies = [pltpu.make_async_copy(a, b, sems.at[i]) for i, (a, b) in enumerate(pairs)]
    for c in copies:
        c.start()
    for c in copies[1:]:
        c.wait()
    eid = expert_ids()
    hit = r_ref[0:1] == eid
    for k in range(1, TOPK):
        hit = hit | (r_ref[k : k + 1] == eid)
    a = lax.broadcasted_iota(I32, (ROWS, ROWS), 0)
    b = lax.broadcasted_iota(I32, (ROWS, ROWS), 1)
    before = (a < b).astype(F32).astype(BF)
    rank = lax.dot_general(hit.astype(F32).astype(BF), before, NN, preferred_element_type=F32)
    place = jnp.where(hit, rank, -1.0)
    pm_ref[...] = place
    other = jnp.where(pos_ref[2] == 0, place[HALF:], place[:HALF])
    low_ref[CW:] = jnp.concatenate([other, jnp.zeros((HALF, ROWS), F32)], axis=0).astype(BF)
    pos = lax.broadcasted_iota(I32, (8, ROWS), 1)
    start = jnp.int32(0)
    scale = jnp.zeros((8, ROWS), F32)
    for s in range(4):
        n = len_ref[0, s]
        ratio = jnp.full((8, ROWS), adv_ref[0, s], F32) / jnp.full((8, ROWS), n, I32).astype(F32)
        scale = jnp.where((pos >= start) & (pos < start + n), ratio, scale)
        start = start + n
    copies[0].wait()
    scr[0:D] = g_ref[...].astype(F32) * scale[0:1]
    scr[D:] = jnp.zeros((8, ROWS), F32)
    keep = lax.broadcasted_iota(I32, (PAD, ROWS), 0) < OWN
    for d in range(NDP):
        block = scr[d * OWN : d * OWN + PAD]
        cot_ref, at = (low_ref, d * PAD) if d < NDP // 2 else (high_ref, d * PAD - CW)
        cot_ref[at : at + PAD] = jnp.where(keep, block, 0.0).astype(BF)


def prep(pos, lens, adv, gt, rt):
    outs = [((CW + 16, ROWS), BF), ((CW, ROWS), BF), ((NEXP, ROWS), F32)]
    scratch = [
        pltpu.VMEM((D, ROWS), BF),
        pltpu.VMEM((TOPK, ROWS), I32),
        pltpu.SMEM((1, 4), I32),
        pltpu.SMEM((1, 4), F32),
        pltpu.VMEM((D + 8, ROWS), F32),
        pltpu.SemaphoreType.DMA((4,)),
    ]
    args = [pltpu.with_memory_space_constraint(v, pltpu.HBM) for v in (lens, adv, gt, rt)]
    return call(prep_kernel, "prep", [SMEM] + [ANY] * 4, outs, scratch)(pos, *args)


def send(copies, scr, out_hbm, at, n, sems):
    cols = pl.ds(at, n)
    copies.append(pltpu.make_async_copy(scr.at[:, cols], out_hbm.at[:, cols], sems.at[len(copies)]))
    copies[-1].start()


def spread(s, cots, scr, out_hbm, sems):
    copies = []
    for n, cot_ref in enumerate(cots):
        for i in range(0, CW, STEP):
            at = n * CW + i
            scr[:, at : at + STEP] = lax.dot_general(
                s, cot_ref[i : i + STEP], NT, preferred_element_type=F32
            ).astype(BF)
            send(copies, scr, out_hbm, at, STEP, sems)
    return copies


def hidden_rows(h_ref, gate_ref, r_ref, place, eid):
    n = place.shape[0]
    acc = jnp.zeros((n * CAP, HW), F32)
    for k in range(TOPK):
        s = slot_onehot(jnp.where(r_ref[k : k + 1] == eid, place, -1.0), n).astype(BF)
        rows = jnp.concatenate(
            [h_ref[k], gate_ref[k : k + 1], jnp.zeros((HW - FFW - 1, ROWS), BF)], axis=0
        )
        acc = acc + lax.dot_general(s, rows, NT, preferred_element_type=F32)
    return acc.astype(BF)


def other_kernel(pos_ref, h_ref, gate_ref, r_ref, pm_ref, _, out_ref):
    first = pos_ref[2] == 0
    eid = expert_ids()
    place = jnp.where(first, pm_ref[HALF:], pm_ref[:HALF])
    out_ref[...] = hidden_rows(h_ref, gate_ref, r_ref, place, jnp.where(first, eid[HALF:], eid[:HALF]))


def own_kernel(pos_ref, h_hbm, gate_hbm, r_hbm, pm_ref, low_ref, high_ref, out_hbm, *refs):
    h_ref, gate_ref, r_ref, sem_in, scr, sems = refs
    pairs = [(h_hbm, h_ref), (gate_hbm, gate_ref), (r_hbm, r_ref)]
    loads = [pltpu.make_async_copy(a, b, sem_in.at[i]) for i, (a, b) in enumerate(pairs)]
    for c in loads:
        c.start()
    first = pos_ref[2] == 0
    eid = expert_ids()
    place = jnp.where(first, pm_ref[:HALF], pm_ref[HALF:])
    copies = spread(slot_onehot(place, HALF).astype(BF), (low_ref, high_ref), scr, out_hbm, sems)
    for c in loads:
        c.wait()
    scr[:, WIDE:] = hidden_rows(
        h_ref, gate_ref, r_ref, place, jnp.where(first, eid[:HALF], eid[HALF:])
    )
    send(copies, scr, out_hbm, WIDE, HW, sems)
    for c in copies:
        c.wait()


def low_kernel(cot_ref, h_ref, out_hbm, scr, sems):
    place = cot_ref[CW:].astype(F32)[:HALF]
    copies = spread(slot_onehot(place, HALF).astype(BF), (cot_ref,), scr, out_hbm, sems)
    scr[:, CW:] = h_ref[...]
    send(copies, scr, out_hbm, CW, HW, sems)
    for c in copies:
        c.wait()


def high_kernel(cot_ref, pm_ref, out_hbm, scr, sems):
    place = pm_ref[CW:].astype(F32)[:HALF]
    for c in spread(slot_onehot(place, HALF).astype(BF), (cot_ref,), scr, out_hbm, sems):
        c.wait()


def term_kernel(own_ref, low_ref, high_ref, _, out_hbm, scr, sems):
    hid = [own_ref[:, WIDE:], low_ref[:, CW:]]
    gate = [h[:, FFW : FFW + 1].astype(F32) for h in hid]
    copies = []
    for z in range(NZ):
        acc = jnp.zeros((BLK, FFW), F32)
        at = z * BLK
        cots = [own_ref[:, at : at + BLK]]
        cots.append(low_ref[:, at : at + BLK] if at < CW else high_ref[:, at - CW : at - CW + BLK])
        for cot, h, g in zip(cots, hid, gate):
            gated = (cot.astype(F32) * g).astype(BF)
            acc = acc + lax.dot_general(gated, h[:, :FFW], TN, preferred_element_type=F32)
        rows = pl.ds(at, BLK)
        scr[rows] = acc.astype(BF)
        copies.append(pltpu.make_async_copy(scr.at[rows], out_hbm.at[rows], sems.at[z]))
        copies[-1].start()
    for c in copies:
        c.wait()


def sum_kernel(x_ref, _, out_ref):
    v = x_ref[0].astype(F32)
    for d in range(1, NDP):
        v = v + x_ref[d].astype(F32)
    out_ref[...] = v[:OWN]


def pad_kernel(w_ref, out_ref):
    out_ref[...] = jnp.zeros((PAD, HW), BF)
    out_ref[:OWN, :FFW] = w_ref[...]


def merge_kernel(bit):
    def body(pos_ref, mine_ref, other_ref, out_ref):
        i = (pos_ref[1] >> bit) & 1
        n = mine_ref.shape[0]
        out_ref[pl.ds(pl.multiple_of(i * n, n), n)] = mine_ref[...]
        out_ref[pl.ds(pl.multiple_of((1 - i) * n, n), n)] = other_ref[...]

    return body


def peer(pos_ref, r, sign):
    dx, dc = r // 2, r % 2
    return ((pos_ref[3] + NX + sign * dx) % NX) * 2 + (pos_ref[4] + dc) % 2


def back_kernel(pos_ref, own_ref, low_ref, high_ref, w_ref, *refs):
    outs, scr = refs[:HALF], refs[HALF]
    for i in range(2):
        parts = (own_ref[:, :CW], own_ref[:, CW:WIDE]) if i == 0 else (low_ref[:, :CW], high_ref[...])
        acc = lax.dot_general(parts[0], w_ref[:CW, :FFW], NN, preferred_element_type=F32)
        scr[...] = acc + lax.dot_general(
            parts[1], w_ref[CW:, :FFW], NN, preferred_element_type=F32
        )
        for r, out_ref in enumerate(outs):
            at = pl.multiple_of(peer(pos_ref, r, 1) * CAP, 8)
            out_ref[i] = scr[pl.ds(at, CAP)].astype(BF)


def stack_kernel(*refs):
    for r in range(HALF):
        refs[HALF][r] = refs[r][1]


def home_kernel(pos_ref, h_ref, gate_ref, pm_ref, r_ref, other_ref, *refs):
    owns, gh_ref, gg_ref = refs[:HALF], refs[HALF], refs[HALF + 1]
    gate = gate_ref[...].astype(F32)
    c = lax.broadcasted_iota(I32, (CAP, ROWS), 0).astype(F32)
    yh = pos_ref[2]
    pieces, places, ids = [], [], []
    for half in range(2):
        side = yh if half == 0 else 1 - yh
        for r in range(HALF):
            i = peer(pos_ref, r, -1)
            pieces.append((owns[r][0] if half == 0 else other_ref[r]).astype(F32))
            places.append(pm_ref[pl.ds(side * HALF + i, 1)])
            ids.append((i // 2) * 4 + side * 2 + i % 2)
    x = jnp.concatenate(pieces, axis=0).astype(BF)
    for k in range(TOPK):
        rk = r_ref[k : k + 1]
        rows = [
            (jnp.where(rk == e, p, -1.0) == c).astype(F32) for p, e in zip(places, ids)
        ]
        s = jnp.concatenate(rows, axis=0).astype(BF)
        back = lax.dot_general(x, s, TN, preferred_element_type=F32)
        gh_ref[k] = back * gate[k : k + 1]
        gg_ref[k : k + 1] = jnp.sum(back * h_ref[k].astype(F32), axis=0, keepdims=True)


def shift(x, axis, n, by):
    return lax.ppermute(x, axis, [(i, (i + by) % n) for i in range(n)])


def to_peer(x, r):
    dx, dc = r // 2, r % 2
    if r == 0:
        return x
    pairs = [(i, ((i // 2 + dx) % NX) * 2 + (i + dc) % 2) for i in range(HALF)]
    return lax.ppermute(x, ("x", "c"), pairs)


def exchange(x, axes):
    return lax.all_to_all(x, axes, split_axis=0, concat_axis=0, tiled=True)


def local(grad_out, hidden_act, gate_weights, routing, resp_lengths, advantage, w_down):
    pos = jnp.stack([lax.axis_index(a).astype(I32) for a in ("z", "yl", "yh", "x", "c")])
    gt = grad_out.T
    ht = jnp.transpose(hidden_act, (1, 2, 0))
    gates = gate_weights.T
    rt = routing.T

    weight = call(pad_kernel, "weight_pad", [VMEM], [((PAD, HW), BF)])(w_down[0].T)[0]
    for bit in range(2):
        other = lax.ppermute(weight, "yl", [(i, i ^ (1 << bit)) for i in range(NY)])
        weight = call(
            merge_kernel(bit), "weight_pair", [SMEM] + [VMEM] * 2, [((2 * weight.shape[0], HW), BF)]
        )(pos, weight, other)[0]
    pair = weight
    weight = lax.all_gather(weight, "z", axis=0, tiled=True)

    low, high, pm = prep(pos, resp_lengths, advantage, gt, rt)
    low_out, high_out, _ = lax.optimization_barrier((low, high, pair))
    low_par = shift(low_out, "yh", 2, 1)
    high_par = shift(high_out, "yh", 2, 1)
    own = call(
        own_kernel,
        "send_own",
        [SMEM] + [ANY] * 3 + [VMEM] * 3,
        [((HSLOT, WIDE + HW), BF)],
        [
            pltpu.VMEM((TOPK, FFW, ROWS), BF),
            pltpu.VMEM((TOPK, ROWS), BF),
            pltpu.VMEM((TOPK, ROWS), I32),
            pltpu.SemaphoreType.DMA((3,)),
        ]
        + spread_scratch(WIDE + HW),
        where=ANY,
    )(pos, *(pltpu.with_memory_space_constraint(v, pltpu.HBM) for v in (ht, gates, rt)), pm, low, high)[0]
    hid_par = call(
        other_kernel, "send_other", [SMEM] + [VMEM] * 4 + [ANY], [((HSLOT, HW), BF)]
    )(pos, ht, gates, rt, pm, pltpu.with_memory_space_constraint(own, pltpu.HBM))[0]
    hid_par = shift(hid_par, "yh", 2, 1)
    own = exchange(own.reshape(HALF, CAP, WIDE + HW), ("x", "c")).reshape(HSLOT, WIDE + HW)

    def forward(x, after):
        width = x.shape[1]
        x, _ = lax.optimization_barrier((x, after))
        return exchange(x.reshape(HALF, CAP, width), ("x", "c")).reshape(HSLOT, width)

    par_low = call(
        low_kernel,
        "send_low",
        [VMEM] * 2,
        [((HSLOT, CW + HW), BF)],
        spread_scratch(CW + HW),
        where=ANY,
        weight=COVER,
    )(low_par, hid_par)[0]
    par_low = forward(par_low, own)
    par_high = call(
        high_kernel,
        "send_high",
        [VMEM] * 2,
        [((HSLOT, CW), BF)],
        spread_scratch(CW),
        where=ANY,
        weight=COVER,
    )(high_par, low_par)[0]
    par_high = forward(par_high, par_low)

    terms = call(
        term_kernel,
        "grad_term",
        [VMEM] * 3 + [ANY],
        [((WIDE, FFW), BF)],
        [pltpu.VMEM((WIDE, FFW), BF), pltpu.SemaphoreType.DMA((NZ,))],
        mib=20,
        where=ANY,
    )(own, par_low, par_high, pltpu.with_memory_space_constraint(weight, pltpu.HBM))[0]
    terms = exchange(terms.reshape(NDP, PAD, FFW), ("z", "yl"))

    backs = call(
        back_kernel,
        "back_product",
        [SMEM] + [VMEM] * 4,
        [((2, CAP, FFW), BF)] * HALF,
        [pltpu.VMEM((HSLOT, FFW), F32)],
        mib=20,
    )(pos, own, par_low, par_high, weight)
    backs = [to_peer(b, r) for r, b in enumerate(backs)]
    other = call(stack_kernel, "stack_other", [VMEM] * HALF, [((HALF, CAP, FFW), BF)])(*backs)[0]
    other = shift(other, "yh", 2, 1)
    gh, gg = call(
        home_kernel,
        "bring_home",
        [SMEM] + [VMEM] * (5 + HALF),
        [((TOPK, FFW, ROWS), F32), ((TOPK, ROWS), F32)],
    )(pos, ht, gates, pm, rt, other, *backs)
    gd = call(sum_kernel, "sum_terms", [VMEM, ANY], [((OWN, FFW), F32)])(terms, gg)[0]
    return gd.T[None], jnp.transpose(gh, (2, 0, 1)), gg.T


def solution(mesh):
    every = ("z", "yl", "x", "yh", "c")
    fine = Mesh(mesh.devices.reshape(NZ, NY, NX, 2, 2), every)
    rows2 = P(every, None)
    rows3 = P(every, None, None)
    cols = P(("x", "yh", "c"), None, ("z", "yl"))
    return jax.shard_map(
        local,
        mesh=fine,
        in_specs=(rows2, rows3, rows2, rows2, rows2, rows2, cols),
        out_specs=(cols, rows3, rows2),
        check_vma=False,
    )
```

```python
import jax
import jax.numpy as jnp
from jax import lax
from jax.experimental import pallas as pl
from jax.experimental.pallas import tpu as pltpu
from jax.sharding import Mesh, PartitionSpec as P

BF = jnp.bfloat16
F32 = jnp.float32
I32 = jnp.int32
NT = (((1,), (1,)), ((), ()))
TN = (((0,), (0,)), ((), ()))
NN = (((1,), (0,)), ((), ()))
ROWS, D, TOPK, FFW, NEXP, CAP = 128, 2880, 4, 360, 16, 40
NZ, NY, NX = 8, 4, 4
NDP = NZ * NY
OWN = D // NDP
PAD = 96
WIDE = NDP * PAD
HALF = NEXP // 2
HSLOT = HALF * CAP
STEP = 768
HW = 384
COVER_LOW = 10_000_000_000
COVER = 50_000_000_000
BLK = NY * PAD
CW = WIDE // 2
def spread_scratch(width):
    return [pltpu.VMEM((HSLOT, width), BF), pltpu.SemaphoreType.DMA((WIDE // STEP + 1,))]


VMEM = pl.BlockSpec(memory_space=pltpu.VMEM)
SMEM = pl.BlockSpec(memory_space=pltpu.SMEM)
ANY = pl.BlockSpec(memory_space=pltpu.HBM)


def call(body, name, ins, outs, scratch=(), mib=14, weight=None, where=None):
    outs = [(pltpu.HBM if where else jax.ShapeDtypeStruct)(*o) for o in outs]
    return pl.pallas_call(
        body,
        in_specs=list(ins),
        out_specs=[where or VMEM] * len(outs),
        out_shape=outs,
        scratch_shapes=list(scratch),
        compiler_params=pltpu.CompilerParams(vmem_limit_bytes=mib << 20),
        name=name,
        cost_estimate=weight and pl.CostEstimate(flops=weight, transcendentals=0, bytes_accessed=0),
    )


def expert_ids():
    row = lax.broadcasted_iota(I32, (NEXP, ROWS), 0)
    return ((row >> 1) & 3) * 4 + (row >> 3) * 2 + (row & 1)


def slot_onehot(place, n):
    c = lax.broadcasted_iota(I32, (n, CAP, ROWS), 1).astype(F32)
    return (place[:, None, :] == c).astype(F32).reshape(n * CAP, ROWS)


def prep_kernel(pos_ref, len_hbm, adv_hbm, g_hbm, r_hbm, low_ref, high_ref, pm_ref, *refs):
    g_ref, r_ref, len_ref, adv_ref, scr, sems = refs
    pairs = [(g_hbm, g_ref), (r_hbm, r_ref), (len_hbm, len_ref), (adv_hbm, adv_ref)]
    copies = [pltpu.make_async_copy(a, b, sems.at[i]) for i, (a, b) in enumerate(pairs)]
    for c in copies:
        c.start()
    for c in copies[1:]:
        c.wait()
    eid = expert_ids()
    hit = r_ref[0:1] == eid
    for k in range(1, TOPK):
        hit = hit | (r_ref[k : k + 1] == eid)
    a = lax.broadcasted_iota(I32, (ROWS, ROWS), 0)
    b = lax.broadcasted_iota(I32, (ROWS, ROWS), 1)
    before = (a < b).astype(F32).astype(BF)
    rank = lax.dot_general(hit.astype(F32).astype(BF), before, NN, preferred_element_type=F32)
    place = jnp.where(hit, rank, -1.0)
    pm_ref[...] = place
    other = jnp.where(pos_ref[2] == 0, place[HALF:], place[:HALF])
    low_ref[CW:] = jnp.concatenate([other, jnp.zeros((HALF, ROWS), F32)], axis=0).astype(BF)
    pos = lax.broadcasted_iota(I32, (8, ROWS), 1)
    start = jnp.int32(0)
    scale = jnp.zeros((8, ROWS), F32)
    for s in range(4):
        n = len_ref[0, s]
        ratio = jnp.full((8, ROWS), adv_ref[0, s], F32) / jnp.full((8, ROWS), n, I32).astype(F32)
        scale = jnp.where((pos >= start) & (pos < start + n), ratio, scale)
        start = start + n
    copies[0].wait()
    scr[0:D] = g_ref[...].astype(F32) * scale[0:1]
    scr[D:] = jnp.zeros((8, ROWS), F32)
    keep = lax.broadcasted_iota(I32, (PAD, ROWS), 0) < OWN
    for d in range(NDP):
        block = scr[d * OWN : d * OWN + PAD]
        cot_ref, at = (low_ref, d * PAD) if d < NDP // 2 else (high_ref, d * PAD - CW)
        cot_ref[at : at + PAD] = jnp.where(keep, block, 0.0).astype(BF)


def prep(pos, lens, adv, gt, rt):
    outs = [((CW + 16, ROWS), BF), ((CW, ROWS), BF), ((NEXP, ROWS), F32)]
    scratch = [
        pltpu.VMEM((D, ROWS), BF),
        pltpu.VMEM((TOPK, ROWS), I32),
        pltpu.SMEM((1, 4), I32),
        pltpu.SMEM((1, 4), F32),
        pltpu.VMEM((D + 8, ROWS), F32),
        pltpu.SemaphoreType.DMA((4,)),
    ]
    args = [pltpu.with_memory_space_constraint(v, pltpu.HBM) for v in (lens, adv, gt, rt)]
    return call(prep_kernel, "prep", [SMEM] + [ANY] * 4, outs, scratch)(pos, *args)


def send(copies, scr, out_hbm, at, n, sems):
    cols = pl.ds(at, n)
    copies.append(pltpu.make_async_copy(scr.at[:, cols], out_hbm.at[:, cols], sems.at[len(copies)]))
    copies[-1].start()


def spread(s, cots, scr, out_hbm, sems):
    copies = []
    for n, cot_ref in enumerate(cots):
        for i in range(0, CW, STEP):
            at = n * CW + i
            scr[:, at : at + STEP] = lax.dot_general(
                s, cot_ref[i : i + STEP], NT, preferred_element_type=F32
            ).astype(BF)
            send(copies, scr, out_hbm, at, STEP, sems)
    return copies


def hidden_rows(h_ref, gate_ref, r_ref, place, eid):
    n = place.shape[0]
    acc = jnp.zeros((n * CAP, HW), F32)
    for k in range(TOPK):
        s = slot_onehot(jnp.where(r_ref[k : k + 1] == eid, place, -1.0), n).astype(BF)
        rows = jnp.concatenate(
            [h_ref[k], gate_ref[k : k + 1], jnp.zeros((HW - FFW - 1, ROWS), BF)], axis=0
        )
        acc = acc + lax.dot_general(s, rows, NT, preferred_element_type=F32)
    return acc.astype(BF)


def other_kernel(pos_ref, h_ref, gate_ref, r_ref, pm_ref, out_ref):
    first = pos_ref[2] == 0
    eid = expert_ids()
    place = jnp.where(first, pm_ref[HALF:], pm_ref[:HALF])
    out_ref[...] = hidden_rows(h_ref, gate_ref, r_ref, place, jnp.where(first, eid[HALF:], eid[:HALF]))


def own_kernel(pos_ref, h_hbm, gate_hbm, r_hbm, pm_ref, low_ref, high_ref, out_hbm, *refs):
    h_ref, gate_ref, r_ref, sem_in, scr, sems = refs
    pairs = [(h_hbm, h_ref), (gate_hbm, gate_ref), (r_hbm, r_ref)]
    loads = [pltpu.make_async_copy(a, b, sem_in.at[i]) for i, (a, b) in enumerate(pairs)]
    for c in loads:
        c.start()
    first = pos_ref[2] == 0
    eid = expert_ids()
    place = jnp.where(first, pm_ref[:HALF], pm_ref[HALF:])
    copies = spread(slot_onehot(place, HALF).astype(BF), (low_ref, high_ref), scr, out_hbm, sems)
    for c in loads:
        c.wait()
    scr[:, WIDE:] = hidden_rows(
        h_ref, gate_ref, r_ref, place, jnp.where(first, eid[:HALF], eid[HALF:])
    )
    send(copies, scr, out_hbm, WIDE, HW, sems)
    for c in copies:
        c.wait()


def low_kernel(cot_ref, h_ref, out_hbm, scr, sems):
    place = cot_ref[CW:].astype(F32)[:HALF]
    copies = spread(slot_onehot(place, HALF).astype(BF), (cot_ref,), scr, out_hbm, sems)
    scr[:, CW:] = h_ref[...]
    send(copies, scr, out_hbm, CW, HW, sems)
    for c in copies:
        c.wait()


def high_kernel(cot_ref, pm_ref, out_hbm, scr, sems):
    place = pm_ref[CW:].astype(F32)[:HALF]
    for c in spread(slot_onehot(place, HALF).astype(BF), (cot_ref,), scr, out_hbm, sems):
        c.wait()


def term_kernel(own_ref, low_ref, high_ref, _, out_hbm, scr, sems):
    hid = [own_ref[:, WIDE:], low_ref[:, CW:]]
    gate = [h[:, FFW : FFW + 1].astype(F32) for h in hid]
    copies = []
    for z in range(NZ):
        acc = jnp.zeros((BLK, FFW), F32)
        at = z * BLK
        cots = [own_ref[:, at : at + BLK]]
        cots.append(low_ref[:, at : at + BLK] if at < CW else high_ref[:, at - CW : at - CW + BLK])
        for cot, h, g in zip(cots, hid, gate):
            gated = (cot.astype(F32) * g).astype(BF)
            acc = acc + lax.dot_general(gated, h[:, :FFW], TN, preferred_element_type=F32)
        rows = pl.ds(at, BLK)
        scr[rows] = acc.astype(BF)
        copies.append(pltpu.make_async_copy(scr.at[rows], out_hbm.at[rows], sems.at[z]))
        copies[-1].start()
    for c in copies:
        c.wait()


def sum_kernel(x_ref, _, out_ref):
    v = x_ref[0].astype(F32)
    for d in range(1, NDP):
        v = v + x_ref[d].astype(F32)
    out_ref[...] = v[:OWN]


def pad_kernel(w_ref, out_ref):
    out_ref[...] = jnp.zeros((PAD, HW), BF)
    out_ref[:OWN, :FFW] = w_ref[...]


def merge_kernel(bit):
    def body(pos_ref, mine_ref, other_ref, *refs):
        out_ref = refs[-1]
        i = (pos_ref[1] >> bit) & 1
        n = mine_ref.shape[0]
        out_ref[pl.ds(pl.multiple_of(i * n, n), n)] = mine_ref[...]
        out_ref[pl.ds(pl.multiple_of((1 - i) * n, n), n)] = other_ref[...]

    return body


def peer(pos_ref, r, sign):
    dx, dc = r // 2, r % 2
    return ((pos_ref[3] + NX + sign * dx) % NX) * 2 + (pos_ref[4] + dc) % 2


def back_kernel(pos_ref, own_ref, low_ref, high_ref, w_ref, *refs):
    outs, scr = refs[:HALF], refs[HALF]
    for i in range(2):
        parts = (own_ref[:, :CW], own_ref[:, CW:WIDE]) if i == 0 else (low_ref[:, :CW], high_ref[...])
        acc = lax.dot_general(parts[0], w_ref[:CW, :FFW], NN, preferred_element_type=F32)
        scr[...] = acc + lax.dot_general(
            parts[1], w_ref[CW:, :FFW], NN, preferred_element_type=F32
        )
        for r, out_ref in enumerate(outs):
            at = pl.multiple_of(peer(pos_ref, r, 1) * CAP, 8)
            out_ref[i] = scr[pl.ds(at, CAP)].astype(BF)


def stack_kernel(*refs):
    for r in range(HALF):
        refs[HALF][r] = refs[r][1]


def home_kernel(pos_ref, h_ref, gate_ref, pm_ref, r_ref, other_ref, *refs):
    owns, gh_ref, gg_ref = refs[:HALF], refs[HALF], refs[HALF + 1]
    gate = gate_ref[...].astype(F32)
    c = lax.broadcasted_iota(I32, (CAP, ROWS), 0).astype(F32)
    yh = pos_ref[2]
    pieces, places, ids = [], [], []
    for half in range(2):
        side = yh if half == 0 else 1 - yh
        for r in range(HALF):
            i = peer(pos_ref, r, -1)
            pieces.append((owns[r][0] if half == 0 else other_ref[r]).astype(F32))
            places.append(pm_ref[pl.ds(side * HALF + i, 1)])
            ids.append((i // 2) * 4 + side * 2 + i % 2)
    x = jnp.concatenate(pieces, axis=0).astype(BF)
    for k in range(TOPK):
        rk = r_ref[k : k + 1]
        rows = [
            (jnp.where(rk == e, p, -1.0) == c).astype(F32) for p, e in zip(places, ids)
        ]
        s = jnp.concatenate(rows, axis=0).astype(BF)
        back = lax.dot_general(x, s, TN, preferred_element_type=F32)
        gh_ref[k] = back * gate[k : k + 1]
        gg_ref[k : k + 1] = jnp.sum(back * h_ref[k].astype(F32), axis=0, keepdims=True)


def shift(x, axis, n, by):
    return lax.ppermute(x, axis, [(i, (i + by) % n) for i in range(n)])


def to_peer(x, r):
    dx, dc = r // 2, r % 2
    if r == 0:
        return x
    pairs = [(i, ((i // 2 + dx) % NX) * 2 + (i + dc) % 2) for i in range(HALF)]
    return lax.ppermute(x, ("x", "c"), pairs)


def exchange(x, axes):
    return lax.all_to_all(x, axes, split_axis=0, concat_axis=0, tiled=True)


def local(grad_out, hidden_act, gate_weights, routing, resp_lengths, advantage, w_down):
    pos = jnp.stack([lax.axis_index(a).astype(I32) for a in ("z", "yl", "yh", "x", "c")])
    gt = grad_out.T
    ht = jnp.transpose(hidden_act, (1, 2, 0))
    gates = gate_weights.T
    rt = routing.T

    low, high, pm = prep(pos, resp_lengths, advantage, gt, rt)
    own = call(
        own_kernel,
        "send_own",
        [SMEM] + [ANY] * 3 + [VMEM] * 3,
        [((HSLOT, WIDE + HW), BF)],
        [
            pltpu.VMEM((TOPK, FFW, ROWS), BF),
            pltpu.VMEM((TOPK, ROWS), BF),
            pltpu.VMEM((TOPK, ROWS), I32),
            pltpu.SemaphoreType.DMA((3,)),
        ]
        + spread_scratch(WIDE + HW),
        where=ANY,
    )(pos, *(pltpu.with_memory_space_constraint(v, pltpu.HBM) for v in (ht, gates, rt)), pm, low, high)[0]

    weight = call(pad_kernel, "weight_pad", [VMEM], [((PAD, HW), BF)])(w_down[0].T)[0]
    ready = pltpu.with_memory_space_constraint(own, pltpu.HBM)
    for bit in range(2):
        other = lax.ppermute(weight, "yl", [(i, i ^ (1 << bit)) for i in range(NY)])
        weight = call(
            merge_kernel(bit),
            "weight_pair",
            [SMEM] + [VMEM] * 2 + [ANY],
            [((2 * weight.shape[0], HW), BF)],
        )(pos, weight, other, ready)[0]
    pair = weight
    weight = lax.all_gather(weight, "z", axis=0, tiled=True)

    low_out, high_out, pm_out, _ = lax.optimization_barrier((low, high, pm, pair))
    low_par = shift(low_out, "yh", 2, 1)
    high_par = shift(high_out, "yh", 2, 1)
    hid_par = call(other_kernel, "send_other", [SMEM] + [VMEM] * 4, [((HSLOT, HW), BF)])(
        pos, ht, gates, rt, pm_out
    )[0]
    hid_par = shift(hid_par, "yh", 2, 1)
    own = exchange(own.reshape(HALF, CAP, WIDE + HW), ("x", "c")).reshape(HSLOT, WIDE + HW)

    def forward(x, after):
        width = x.shape[1]
        x, _ = lax.optimization_barrier((x, after))
        return exchange(x.reshape(HALF, CAP, width), ("x", "c")).reshape(HSLOT, width)

    par_low = call(
        low_kernel,
        "send_low",
        [VMEM] * 2,
        [((HSLOT, CW + HW), BF)],
        spread_scratch(CW + HW),
        where=ANY,
        weight=COVER_LOW,
    )(low_par, hid_par)[0]
    par_low = forward(par_low, own)
    par_high = call(
        high_kernel,
        "send_high",
        [VMEM] * 2,
        [((HSLOT, CW), BF)],
        spread_scratch(CW),
        where=ANY,
        weight=COVER,
    )(high_par, low_par)[0]
    par_high = forward(par_high, par_low)

    terms = call(
        term_kernel,
        "grad_term",
        [VMEM] * 3 + [ANY],
        [((WIDE, FFW), BF)],
        [pltpu.VMEM((WIDE, FFW), BF), pltpu.SemaphoreType.DMA((NZ,))],
        mib=20,
        where=ANY,
    )(own, par_low, par_high, pltpu.with_memory_space_constraint(weight, pltpu.HBM))[0]
    terms = exchange(terms.reshape(NDP, PAD, FFW), ("z", "yl"))

    backs = call(
        back_kernel,
        "back_product",
        [SMEM] + [VMEM] * 4,
        [((2, CAP, FFW), BF)] * HALF,
        [pltpu.VMEM((HSLOT, FFW), F32)],
        mib=20,
    )(pos, own, par_low, par_high, weight)
    backs = [to_peer(b, r) for r, b in enumerate(backs)]
    other = call(stack_kernel, "stack_other", [VMEM] * HALF, [((HALF, CAP, FFW), BF)])(*backs)[0]
    other = shift(other, "yh", 2, 1)
    gh, gg = call(
        home_kernel,
        "bring_home",
        [SMEM] + [VMEM] * (5 + HALF),
        [((TOPK, FFW, ROWS), F32), ((TOPK, ROWS), F32)],
    )(pos, ht, gates, pm, rt, other, *backs)
    gd = call(sum_kernel, "sum_terms", [VMEM, ANY], [((OWN, FFW), F32)])(terms, gg)[0]
    return gd.T[None], jnp.transpose(gh, (2, 0, 1)), gg.T


def solution(mesh):
    every = ("z", "yl", "x", "yh", "c")
    fine = Mesh(mesh.devices.reshape(NZ, NY, NX, 2, 2), every)
    rows2 = P(every, None)
    rows3 = P(every, None, None)
    cols = P(("x", "yh", "c"), None, ("z", "yl"))
    return jax.shard_map(
        local,
        mesh=fine,
        in_specs=(rows2, rows3, rows2, rows2, rows2, rows2, cols),
        out_specs=(cols, rows3, rows2),
        check_vma=False,
    )
```

```python
import jax
import jax.numpy as jnp
from jax import lax
from jax.experimental import pallas as pl
from jax.experimental.pallas import tpu as pltpu
from jax.sharding import Mesh, PartitionSpec as P

BF = jnp.bfloat16
F32 = jnp.float32
I32 = jnp.int32
NT = (((1,), (1,)), ((), ()))
TN = (((0,), (0,)), ((), ()))
NN = (((1,), (0,)), ((), ()))
ROWS, D, TOPK, FFW, NEXP, CAP = 128, 2880, 4, 360, 16, 40
NZ, NY, NX = 8, 4, 4
NDP = NZ * NY
OWN = D // NDP
PAD = 96
WIDE = NDP * PAD
HALF = NEXP // 2
HSLOT = HALF * CAP
STEP = 768
HW = 384
COVER_PAD = 50_000_000_000
COVER_LOW = 10_000_000_000
COVER = 50_000_000_000
BLK = NY * PAD
CW = WIDE // 2
def spread_scratch(width):
    return [pltpu.VMEM((HSLOT, width), BF), pltpu.SemaphoreType.DMA((WIDE // STEP + 1,))]


VMEM = pl.BlockSpec(memory_space=pltpu.VMEM)
SMEM = pl.BlockSpec(memory_space=pltpu.SMEM)
ANY = pl.BlockSpec(memory_space=pltpu.HBM)


def call(body, name, ins, outs, scratch=(), mib=14, weight=None, where=None):
    outs = [(pltpu.HBM if where else jax.ShapeDtypeStruct)(*o) for o in outs]
    return pl.pallas_call(
        body,
        in_specs=list(ins),
        out_specs=[where or VMEM] * len(outs),
        out_shape=outs,
        scratch_shapes=list(scratch),
        compiler_params=pltpu.CompilerParams(vmem_limit_bytes=mib << 20),
        name=name,
        cost_estimate=weight and pl.CostEstimate(flops=weight, transcendentals=0, bytes_accessed=0),
    )


def expert_ids():
    row = lax.broadcasted_iota(I32, (NEXP, ROWS), 0)
    return ((row >> 1) & 3) * 4 + (row >> 3) * 2 + (row & 1)


def slot_onehot(place, n):
    c = lax.broadcasted_iota(I32, (n, CAP, ROWS), 1).astype(F32)
    return (place[:, None, :] == c).astype(F32).reshape(n * CAP, ROWS)


def prep_kernel(pos_ref, len_hbm, adv_hbm, g_hbm, r_hbm, low_ref, high_ref, pm_ref, *refs):
    g_ref, r_ref, len_ref, adv_ref, scr, sems = refs
    pairs = [(g_hbm, g_ref), (r_hbm, r_ref), (len_hbm, len_ref), (adv_hbm, adv_ref)]
    copies = [pltpu.make_async_copy(a, b, sems.at[i]) for i, (a, b) in enumerate(pairs)]
    for c in copies:
        c.start()
    for c in copies[1:]:
        c.wait()
    eid = expert_ids()
    hit = r_ref[0:1] == eid
    for k in range(1, TOPK):
        hit = hit | (r_ref[k : k + 1] == eid)
    a = lax.broadcasted_iota(I32, (ROWS, ROWS), 0)
    b = lax.broadcasted_iota(I32, (ROWS, ROWS), 1)
    before = (a < b).astype(F32).astype(BF)
    rank = lax.dot_general(hit.astype(F32).astype(BF), before, NN, preferred_element_type=F32)
    place = jnp.where(hit, rank, -1.0)
    pm_ref[...] = place
    other = jnp.where(pos_ref[2] == 0, place[HALF:], place[:HALF])
    low_ref[CW:] = jnp.concatenate([other, jnp.zeros((HALF, ROWS), F32)], axis=0).astype(BF)
    pos = lax.broadcasted_iota(I32, (8, ROWS), 1)
    start = jnp.int32(0)
    scale = jnp.zeros((8, ROWS), F32)
    for s in range(4):
        n = len_ref[0, s]
        ratio = jnp.full((8, ROWS), adv_ref[0, s], F32) / jnp.full((8, ROWS), n, I32).astype(F32)
        scale = jnp.where((pos >= start) & (pos < start + n), ratio, scale)
        start = start + n
    copies[0].wait()
    scr[0:D] = g_ref[...].astype(F32) * scale[0:1]
    scr[D:] = jnp.zeros((8, ROWS), F32)
    keep = lax.broadcasted_iota(I32, (PAD, ROWS), 0) < OWN
    for d in range(NDP):
        block = scr[d * OWN : d * OWN + PAD]
        cot_ref, at = (low_ref, d * PAD) if d < NDP // 2 else (high_ref, d * PAD - CW)
        cot_ref[at : at + PAD] = jnp.where(keep, block, 0.0).astype(BF)


def prep(pos, lens, adv, gt, rt):
    outs = [((CW + 16, ROWS), BF), ((CW, ROWS), BF), ((NEXP, ROWS), F32)]
    scratch = [
        pltpu.VMEM((D, ROWS), BF),
        pltpu.VMEM((TOPK, ROWS), I32),
        pltpu.SMEM((1, 4), I32),
        pltpu.SMEM((1, 4), F32),
        pltpu.VMEM((D + 8, ROWS), F32),
        pltpu.SemaphoreType.DMA((4,)),
    ]
    args = [pltpu.with_memory_space_constraint(v, pltpu.HBM) for v in (lens, adv, gt, rt)]
    return call(prep_kernel, "prep", [SMEM] + [ANY] * 4, outs, scratch)(pos, *args)


def send(copies, scr, out_hbm, at, n, sems):
    cols = pl.ds(at, n)
    copies.append(pltpu.make_async_copy(scr.at[:, cols], out_hbm.at[:, cols], sems.at[len(copies)]))
    copies[-1].start()


def spread(s, cots, scr, out_hbm, sems):
    copies = []
    for n, cot_ref in enumerate(cots):
        for i in range(0, CW, STEP):
            at = n * CW + i
            scr[:, at : at + STEP] = lax.dot_general(
                s, cot_ref[i : i + STEP], NT, preferred_element_type=F32
            ).astype(BF)
            send(copies, scr, out_hbm, at, STEP, sems)
    return copies


def hidden_rows(h_ref, gate_ref, r_ref, place, eid):
    n = place.shape[0]
    acc = jnp.zeros((n * CAP, HW), F32)
    for k in range(TOPK):
        s = slot_onehot(jnp.where(r_ref[k : k + 1] == eid, place, -1.0), n).astype(BF)
        rows = jnp.concatenate(
            [h_ref[k], gate_ref[k : k + 1], jnp.zeros((HW - FFW - 1, ROWS), BF)], axis=0
        )
        acc = acc + lax.dot_general(s, rows, NT, preferred_element_type=F32)
    return acc.astype(BF)


def other_kernel(pos_ref, h_ref, gate_ref, r_ref, pm_ref, out_ref):
    first = pos_ref[2] == 0
    eid = expert_ids()
    place = jnp.where(first, pm_ref[HALF:], pm_ref[:HALF])
    out_ref[...] = hidden_rows(h_ref, gate_ref, r_ref, place, jnp.where(first, eid[HALF:], eid[:HALF]))


def own_kernel(pos_ref, h_hbm, gate_hbm, r_hbm, pm_ref, low_ref, high_ref, out_hbm, *refs):
    h_ref, gate_ref, r_ref, sem_in, scr, sems = refs
    pairs = [(h_hbm, h_ref), (gate_hbm, gate_ref), (r_hbm, r_ref)]
    loads = [pltpu.make_async_copy(a, b, sem_in.at[i]) for i, (a, b) in enumerate(pairs)]
    for c in loads:
        c.start()
    first = pos_ref[2] == 0
    eid = expert_ids()
    place = jnp.where(first, pm_ref[:HALF], pm_ref[HALF:])
    copies = spread(slot_onehot(place, HALF).astype(BF), (low_ref, high_ref), scr, out_hbm, sems)
    for c in loads:
        c.wait()
    scr[:, WIDE:] = hidden_rows(
        h_ref, gate_ref, r_ref, place, jnp.where(first, eid[:HALF], eid[HALF:])
    )
    send(copies, scr, out_hbm, WIDE, HW, sems)
    for c in copies:
        c.wait()


def low_kernel(cot_ref, out_hbm, scr, sems):
    place = cot_ref[CW:].astype(F32)[:HALF]
    for c in spread(slot_onehot(place, HALF).astype(BF), (cot_ref,), scr, out_hbm, sems):
        c.wait()


def high_kernel(cot_ref, pm_ref, h_ref, out_hbm, scr, sems):
    place = pm_ref[CW:].astype(F32)[:HALF]
    copies = spread(slot_onehot(place, HALF).astype(BF), (cot_ref,), scr, out_hbm, sems)
    scr[:, CW:] = h_ref[...]
    send(copies, scr, out_hbm, CW, HW, sems)
    for c in copies:
        c.wait()


def term_kernel(own_ref, low_ref, high_ref, _, out_hbm, scr, sems):
    hid = [own_ref[:, WIDE:], high_ref[:, CW:]]
    gate = [h[:, FFW : FFW + 1].astype(F32) for h in hid]
    copies = []
    for z in range(NZ):
        acc = jnp.zeros((BLK, FFW), F32)
        at = z * BLK
        cots = [own_ref[:, at : at + BLK]]
        cots.append(low_ref[:, at : at + BLK] if at < CW else high_ref[:, at - CW : at - CW + BLK])
        for cot, h, g in zip(cots, hid, gate):
            gated = (cot.astype(F32) * g).astype(BF)
            acc = acc + lax.dot_general(gated, h[:, :FFW], TN, preferred_element_type=F32)
        rows = pl.ds(at, BLK)
        scr[rows] = acc.astype(BF)
        copies.append(pltpu.make_async_copy(scr.at[rows], out_hbm.at[rows], sems.at[z]))
        copies[-1].start()
    for c in copies:
        c.wait()


def sum_kernel(x_ref, _, out_ref):
    v = x_ref[0].astype(F32)
    for d in range(1, NDP):
        v = v + x_ref[d].astype(F32)
    out_ref[...] = v[:OWN]


def pad_kernel(w_ref, _, out_ref):
    out_ref[...] = jnp.zeros((PAD, HW), BF)
    out_ref[:OWN, :FFW] = w_ref[...]


def weight_kernel(pos_ref, *refs):
    out_ref = refs[NY]
    for j in range(NY):
        out_ref[(pos_ref[1] + NY - j) % NY] = refs[j][...]


def peer(pos_ref, r, sign):
    dx, dc = r // 2, r % 2
    return ((pos_ref[3] + NX + sign * dx) % NX) * 2 + (pos_ref[4] + dc) % 2


def back_kernel(pos_ref, own_ref, low_ref, high_ref, w_ref, *refs):
    outs, scr = refs[:HALF], refs[HALF]
    for i in range(2):
        parts = (own_ref[:, :CW], own_ref[:, CW:WIDE]) if i == 0 else (low_ref[...], high_ref[:, :CW])
        acc = lax.dot_general(parts[0], w_ref[:CW, :FFW], NN, preferred_element_type=F32)
        scr[...] = acc + lax.dot_general(
            parts[1], w_ref[CW:, :FFW], NN, preferred_element_type=F32
        )
        for r, out_ref in enumerate(outs):
            at = pl.multiple_of(peer(pos_ref, r, 1) * CAP, 8)
            out_ref[i] = scr[pl.ds(at, CAP)].astype(BF)


def stack_kernel(*refs):
    for r in range(HALF):
        refs[HALF][r] = refs[r][1]


def home_kernel(pos_ref, h_ref, gate_ref, pm_ref, r_ref, other_ref, *refs):
    owns, gh_ref, gg_ref = refs[:HALF], refs[HALF], refs[HALF + 1]
    gate = gate_ref[...].astype(F32)
    c = lax.broadcasted_iota(I32, (CAP, ROWS), 0).astype(F32)
    yh = pos_ref[2]
    pieces, places, ids = [], [], []
    for half in range(2):
        side = yh if half == 0 else 1 - yh
        for r in range(HALF):
            i = peer(pos_ref, r, -1)
            pieces.append((owns[r][0] if half == 0 else other_ref[r]).astype(F32))
            places.append(pm_ref[pl.ds(side * HALF + i, 1)])
            ids.append((i // 2) * 4 + side * 2 + i % 2)
    x = jnp.concatenate(pieces, axis=0).astype(BF)
    for k in range(TOPK):
        rk = r_ref[k : k + 1]
        rows = [
            (jnp.where(rk == e, p, -1.0) == c).astype(F32) for p, e in zip(places, ids)
        ]
        s = jnp.concatenate(rows, axis=0).astype(BF)
        back = lax.dot_general(x, s, TN, preferred_element_type=F32)
        gh_ref[k] = back * gate[k : k + 1]
        gg_ref[k : k + 1] = jnp.sum(back * h_ref[k].astype(F32), axis=0, keepdims=True)


def shift(x, axis, n, by):
    return lax.ppermute(x, axis, [(i, (i + by) % n) for i in range(n)])


def to_peer(x, r):
    dx, dc = r // 2, r % 2
    if r == 0:
        return x
    pairs = [(i, ((i // 2 + dx) % NX) * 2 + (i + dc) % 2) for i in range(HALF)]
    return lax.ppermute(x, ("x", "c"), pairs)


def exchange(x, axes):
    return lax.all_to_all(x, axes, split_axis=0, concat_axis=0, tiled=True)


def local(grad_out, hidden_act, gate_weights, routing, resp_lengths, advantage, w_down):
    pos = jnp.stack([lax.axis_index(a).astype(I32) for a in ("z", "yl", "yh", "x", "c")])
    gt = grad_out.T
    ht = jnp.transpose(hidden_act, (1, 2, 0))
    gates = gate_weights.T
    rt = routing.T

    low, high, pm = prep(pos, resp_lengths, advantage, gt, rt)
    low_par = shift(low, "yh", 2, 1)
    own = call(
        own_kernel,
        "send_own",
        [SMEM] + [ANY] * 3 + [VMEM] * 3,
        [((HSLOT, WIDE + HW), BF)],
        [
            pltpu.VMEM((TOPK, FFW, ROWS), BF),
            pltpu.VMEM((TOPK, ROWS), BF),
            pltpu.VMEM((TOPK, ROWS), I32),
            pltpu.SemaphoreType.DMA((3,)),
        ]
        + spread_scratch(WIDE + HW),
        where=ANY,
    )(pos, *(pltpu.with_memory_space_constraint(v, pltpu.HBM) for v in (ht, gates, rt)), pm, low, high)[0]


    ready = pltpu.with_memory_space_constraint(own, pltpu.HBM)
    wt = call(pad_kernel, "weight_pad", [VMEM, ANY], [((PAD, HW), BF)], weight=COVER_PAD)(
        w_down[0].T, ready
    )[0]
    parts = [wt] + [shift(wt, "yl", NY, j) for j in range(1, NY)]
    w4 = call(weight_kernel, "weight_part", [SMEM] + [VMEM] * NY, [((NY, PAD, HW), BF)])(
        pos, *parts
    )[0].reshape(NY * PAD, HW)
    weight = lax.all_gather(w4, "z", axis=0, tiled=True)

    high_out, pm_out, _, _ = lax.optimization_barrier((high, pm, low_par, w4))
    high_par = shift(high_out, "yh", 2, 1)
    hid_par = call(other_kernel, "send_other", [SMEM] + [VMEM] * 4, [((HSLOT, HW), BF)])(
        pos, ht, gates, rt, pm_out
    )[0]
    hid_par = shift(hid_par, "yh", 2, 1)
    own = exchange(own.reshape(HALF, CAP, WIDE + HW), ("x", "c")).reshape(HSLOT, WIDE + HW)

    def forward(x, after):
        width = x.shape[1]
        x, _ = lax.optimization_barrier((x, after))
        return exchange(x.reshape(HALF, CAP, width), ("x", "c")).reshape(HSLOT, width)

    par_low = call(
        low_kernel,
        "send_low",
        [VMEM],
        [((HSLOT, CW), BF)],
        spread_scratch(CW),
        where=ANY,
        weight=COVER_LOW,
    )(low_par)[0]
    par_low = forward(par_low, own)
    par_high = call(
        high_kernel,
        "send_high",
        [VMEM] * 3,
        [((HSLOT, CW + HW), BF)],
        spread_scratch(CW + HW),
        where=ANY,
        weight=COVER,
    )(high_par, low_par, hid_par)[0]
    par_high = forward(par_high, par_low)

    terms = call(
        term_kernel,
        "grad_term",
        [VMEM] * 3 + [ANY],
        [((WIDE, FFW), BF)],
        [pltpu.VMEM((WIDE, FFW), BF), pltpu.SemaphoreType.DMA((NZ,))],
        mib=20,
        where=ANY,
    )(own, par_low, par_high, pltpu.with_memory_space_constraint(weight, pltpu.HBM))[0]
    terms = exchange(terms.reshape(NDP, PAD, FFW), ("z", "yl"))

    backs = call(
        back_kernel,
        "back_product",
        [SMEM] + [VMEM] * 4,
        [((2, CAP, FFW), BF)] * HALF,
        [pltpu.VMEM((HSLOT, FFW), F32)],
        mib=20,
    )(pos, own, par_low, par_high, weight)
    backs = [to_peer(b, r) for r, b in enumerate(backs)]
    other = call(stack_kernel, "stack_other", [VMEM] * HALF, [((HALF, CAP, FFW), BF)])(*backs)[0]
    other = shift(other, "yh", 2, 1)
    gh, gg = call(
        home_kernel,
        "bring_home",
        [SMEM] + [VMEM] * (5 + HALF),
        [((TOPK, FFW, ROWS), F32), ((TOPK, ROWS), F32)],
    )(pos, ht, gates, pm, rt, other, *backs)
    gd = call(sum_kernel, "sum_terms", [VMEM, ANY], [((OWN, FFW), F32)])(terms, gg)[0]
    return gd.T[None], jnp.transpose(gh, (2, 0, 1)), gg.T


def solution(mesh):
    every = ("z", "yl", "x", "yh", "c")
    fine = Mesh(mesh.devices.reshape(NZ, NY, NX, 2, 2), every)
    rows2 = P(every, None)
    rows3 = P(every, None, None)
    cols = P(("x", "yh", "c"), None, ("z", "yl"))
    return jax.shard_map(
        local,
        mesh=fine,
        in_specs=(rows2, rows3, rows2, rows2, rows2, rows2, cols),
        out_specs=(cols, rows3, rows2),
        check_vma=False,
    )
```

```python
import jax
import jax.numpy as jnp
from jax import lax
from jax.experimental import pallas as pl
from jax.experimental.pallas import tpu as pltpu
from jax.sharding import Mesh, PartitionSpec as P

BF = jnp.bfloat16
F32 = jnp.float32
I32 = jnp.int32
NT = (((1,), (1,)), ((), ()))
TN = (((0,), (0,)), ((), ()))
NN = (((1,), (0,)), ((), ()))
ROWS, D, TOPK, FFW, NEXP, CAP = 128, 2880, 4, 360, 16, 40
NZ, NY, NX = 8, 4, 4
NDP = NZ * NY
OWN = D // NDP
PAD = 96
WIDE = NDP * PAD
HALF = NEXP // 2
HSLOT = HALF * CAP
STEP = 768
HW = 384
COVER_PAD = 50_000_000_000
COVER_LOW = 10_000_000_000
COVER = 50_000_000_000
BLK = NY * PAD
CW = WIDE // 2
def spread_scratch(width):
    return [pltpu.VMEM((HSLOT, width), BF), pltpu.SemaphoreType.DMA((WIDE // STEP + 1,))]


VMEM = pl.BlockSpec(memory_space=pltpu.VMEM)
SMEM = pl.BlockSpec(memory_space=pltpu.SMEM)
ANY = pl.BlockSpec(memory_space=pltpu.HBM)


def call(body, name, ins, outs, scratch=(), mib=14, weight=None, where=None):
    outs = [(pltpu.HBM if where else jax.ShapeDtypeStruct)(*o) for o in outs]
    return pl.pallas_call(
        body,
        in_specs=list(ins),
        out_specs=[where or VMEM] * len(outs),
        out_shape=outs,
        scratch_shapes=list(scratch),
        compiler_params=pltpu.CompilerParams(vmem_limit_bytes=mib << 20),
        name=name,
        cost_estimate=weight and pl.CostEstimate(flops=weight, transcendentals=0, bytes_accessed=0),
    )


def expert_ids():
    row = lax.broadcasted_iota(I32, (NEXP, ROWS), 0)
    return ((row >> 1) & 3) * 4 + (row >> 3) * 2 + (row & 1)


def slot_onehot(place, n):
    c = lax.broadcasted_iota(I32, (n, CAP, ROWS), 1).astype(F32)
    return (place[:, None, :] == c).astype(F32).reshape(n * CAP, ROWS)


def prep_kernel(pos_ref, len_hbm, adv_hbm, g_hbm, r_hbm, low_ref, high_ref, pm_ref, *refs):
    g_ref, r_ref, len_ref, adv_ref, scr, sems = refs
    pairs = [(g_hbm, g_ref), (r_hbm, r_ref), (len_hbm, len_ref), (adv_hbm, adv_ref)]
    copies = [pltpu.make_async_copy(a, b, sems.at[i]) for i, (a, b) in enumerate(pairs)]
    for c in copies:
        c.start()
    for c in copies[1:]:
        c.wait()
    eid = expert_ids()
    hit = r_ref[0:1] == eid
    for k in range(1, TOPK):
        hit = hit | (r_ref[k : k + 1] == eid)
    a = lax.broadcasted_iota(I32, (ROWS, ROWS), 0)
    b = lax.broadcasted_iota(I32, (ROWS, ROWS), 1)
    before = (a < b).astype(F32).astype(BF)
    rank = lax.dot_general(hit.astype(F32).astype(BF), before, NN, preferred_element_type=F32)
    place = jnp.where(hit, rank, -1.0)
    pm_ref[...] = place
    other = jnp.where(pos_ref[2] == 0, place[HALF:], place[:HALF])
    low_ref[CW:] = jnp.concatenate([other, jnp.zeros((HALF, ROWS), F32)], axis=0).astype(BF)
    pos = lax.broadcasted_iota(I32, (8, ROWS), 1)
    start = jnp.int32(0)
    scale = jnp.zeros((8, ROWS), F32)
    for s in range(4):
        n = len_ref[0, s]
        ratio = jnp.full((8, ROWS), adv_ref[0, s], F32) / jnp.full((8, ROWS), n, I32).astype(F32)
        scale = jnp.where((pos >= start) & (pos < start + n), ratio, scale)
        start = start + n
    copies[0].wait()
    scr[0:D] = g_ref[...].astype(F32) * scale[0:1]
    scr[D:] = jnp.zeros((8, ROWS), F32)
    keep = lax.broadcasted_iota(I32, (PAD, ROWS), 0) < OWN
    for d in range(NDP):
        block = scr[d * OWN : d * OWN + PAD]
        cot_ref, at = (low_ref, d * PAD) if d < NDP // 2 else (high_ref, d * PAD - CW)
        cot_ref[at : at + PAD] = jnp.where(keep, block, 0.0).astype(BF)


def prep(pos, lens, adv, gt, rt):
    outs = [((CW + 16, ROWS), BF), ((CW, ROWS), BF), ((NEXP, ROWS), F32)]
    scratch = [
        pltpu.VMEM((D, ROWS), BF),
        pltpu.VMEM((TOPK, ROWS), I32),
        pltpu.SMEM((1, 4), I32),
        pltpu.SMEM((1, 4), F32),
        pltpu.VMEM((D + 8, ROWS), F32),
        pltpu.SemaphoreType.DMA((4,)),
    ]
    args = [pltpu.with_memory_space_constraint(v, pltpu.HBM) for v in (lens, adv, gt, rt)]
    return call(prep_kernel, "prep", [SMEM] + [ANY] * 4, outs, scratch)(pos, *args)


def send(copies, scr, out_hbm, at, n, sems):
    cols = pl.ds(at, n)
    copies.append(pltpu.make_async_copy(scr.at[:, cols], out_hbm.at[:, cols], sems.at[len(copies)]))
    copies[-1].start()


def spread(s, cots, scr, out_hbm, sems):
    copies = []
    for n, cot_ref in enumerate(cots):
        for i in range(0, CW, STEP):
            at = n * CW + i
            scr[:, at : at + STEP] = lax.dot_general(
                s, cot_ref[i : i + STEP], NT, preferred_element_type=F32
            ).astype(BF)
            send(copies, scr, out_hbm, at, STEP, sems)
    return copies


def hidden_rows(h_ref, gate_ref, r_ref, place, eid):
    n = place.shape[0]
    acc = jnp.zeros((n * CAP, HW), F32)
    for k in range(TOPK):
        s = slot_onehot(jnp.where(r_ref[k : k + 1] == eid, place, -1.0), n).astype(BF)
        rows = jnp.concatenate(
            [h_ref[k], gate_ref[k : k + 1], jnp.zeros((HW - FFW - 1, ROWS), BF)], axis=0
        )
        acc = acc + lax.dot_general(s, rows, NT, preferred_element_type=F32)
    return acc.astype(BF)


def other_kernel(pos_ref, h_ref, gate_ref, r_ref, pm_ref, out_ref):
    first = pos_ref[2] == 0
    eid = expert_ids()
    place = jnp.where(first, pm_ref[HALF:], pm_ref[:HALF])
    out_ref[...] = hidden_rows(h_ref, gate_ref, r_ref, place, jnp.where(first, eid[HALF:], eid[:HALF]))


def own_kernel(pos_ref, h_hbm, gate_hbm, r_hbm, pm_ref, low_ref, high_ref, out_hbm, *refs):
    h_ref, gate_ref, r_ref, sem_in, scr, sems = refs
    pairs = [(h_hbm, h_ref), (gate_hbm, gate_ref), (r_hbm, r_ref)]
    loads = [pltpu.make_async_copy(a, b, sem_in.at[i]) for i, (a, b) in enumerate(pairs)]
    for c in loads:
        c.start()
    first = pos_ref[2] == 0
    eid = expert_ids()
    place = jnp.where(first, pm_ref[:HALF], pm_ref[HALF:])
    copies = spread(slot_onehot(place, HALF).astype(BF), (low_ref, high_ref), scr, out_hbm, sems)
    for c in loads:
        c.wait()
    scr[:, WIDE:] = hidden_rows(
        h_ref, gate_ref, r_ref, place, jnp.where(first, eid[:HALF], eid[HALF:])
    )
    send(copies, scr, out_hbm, WIDE, HW, sems)
    for c in copies:
        c.wait()


def low_kernel(cot_ref, out_hbm, scr, sems):
    place = cot_ref[CW:].astype(F32)[:HALF]
    for c in spread(slot_onehot(place, HALF).astype(BF), (cot_ref,), scr, out_hbm, sems):
        c.wait()


def high_kernel(cot_ref, pm_ref, h_ref, out_hbm, scr, sems):
    place = pm_ref[CW:].astype(F32)[:HALF]
    copies = spread(slot_onehot(place, HALF).astype(BF), (cot_ref,), scr, out_hbm, sems)
    scr[:, CW:] = h_ref[...]
    send(copies, scr, out_hbm, CW, HW, sems)
    for c in copies:
        c.wait()


def term_kernel(own_ref, low_hbm, high_ref, _, out_hbm, low_ref, scr, sems):
    load = pltpu.make_async_copy(low_hbm, low_ref, sems.at[NZ])
    load.start()
    hid = [own_ref[:, WIDE:], high_ref[:, CW:]]
    gate = [h[:, FFW : FFW + 1].astype(F32) for h in hid]
    copies = []
    for z in [*range(NZ // 2, NZ), *range(NZ // 2)]:
        if z == 0:
            load.wait()
        acc = jnp.zeros((BLK, FFW), F32)
        at = z * BLK
        cots = [own_ref[:, at : at + BLK]]
        cots.append(low_ref[:, at : at + BLK] if at < CW else high_ref[:, at - CW : at - CW + BLK])
        for cot, h, g in zip(cots, hid, gate):
            gated = (cot.astype(F32) * g).astype(BF)
            acc = acc + lax.dot_general(gated, h[:, :FFW], TN, preferred_element_type=F32)
        rows = pl.ds(at, BLK)
        scr[rows] = acc.astype(BF)
        copies.append(pltpu.make_async_copy(scr.at[rows], out_hbm.at[rows], sems.at[z]))
        copies[-1].start()
    for c in copies:
        c.wait()


def sum_kernel(x_ref, out_ref):
    v = x_ref[0].astype(F32)
    for d in range(1, NDP):
        v = v + x_ref[d].astype(F32)
    out_ref[...] = v[:OWN]


def pad_kernel(w_ref, _, out_ref):
    out_ref[...] = jnp.zeros((PAD, HW), BF)
    out_ref[:OWN, :FFW] = w_ref[...]


def weight_kernel(pos_ref, *refs):
    out_ref = refs[NY]
    for j in range(NY):
        out_ref[(pos_ref[1] + NY - j) % NY] = refs[j][...]


def peer(pos_ref, r, sign):
    dx, dc = r // 2, r % 2
    return ((pos_ref[3] + NX + sign * dx) % NX) * 2 + (pos_ref[4] + dc) % 2


def back_kernel(pos_ref, own_ref, low_ref, high_ref, w_ref, *refs):
    outs, scr = refs[:HALF], refs[HALF]
    for i in range(2):
        parts = (own_ref[:, :CW], own_ref[:, CW:WIDE]) if i == 0 else (low_ref[...], high_ref[:, :CW])
        acc = lax.dot_general(parts[0], w_ref[:CW, :FFW], NN, preferred_element_type=F32)
        scr[...] = acc + lax.dot_general(
            parts[1], w_ref[CW:, :FFW], NN, preferred_element_type=F32
        )
        for r, out_ref in enumerate(outs):
            at = pl.multiple_of(peer(pos_ref, r, 1) * CAP, 8)
            out_ref[i] = scr[pl.ds(at, CAP)].astype(BF)


def stack_kernel(*refs):
    for r in range(HALF):
        refs[HALF][r] = refs[r][1]


def home_kernel(pos_ref, h_ref, gate_ref, pm_ref, r_ref, other_ref, *refs):
    owns, gh_ref, gg_ref = refs[:HALF], refs[HALF], refs[HALF + 1]
    gate = gate_ref[...].astype(F32)
    c = lax.broadcasted_iota(I32, (CAP, ROWS), 0).astype(F32)
    yh = pos_ref[2]
    pieces, places, ids = [], [], []
    for half in range(2):
        side = yh if half == 0 else 1 - yh
        for r in range(HALF):
            i = peer(pos_ref, r, -1)
            pieces.append((owns[r][0] if half == 0 else other_ref[r]).astype(F32))
            places.append(pm_ref[pl.ds(side * HALF + i, 1)])
            ids.append((i // 2) * 4 + side * 2 + i % 2)
    x = jnp.concatenate(pieces, axis=0).astype(BF)
    for k in range(TOPK):
        rk = r_ref[k : k + 1]
        rows = [
            (jnp.where(rk == e, p, -1.0) == c).astype(F32) for p, e in zip(places, ids)
        ]
        s = jnp.concatenate(rows, axis=0).astype(BF)
        back = lax.dot_general(x, s, TN, preferred_element_type=F32)
        gh_ref[k] = back * gate[k : k + 1]
        gg_ref[k : k + 1] = jnp.sum(back * h_ref[k].astype(F32), axis=0, keepdims=True)


def shift(x, axis, n, by):
    return lax.ppermute(x, axis, [(i, (i + by) % n) for i in range(n)])


def held(x):
    return pltpu.with_memory_space_constraint(x, pltpu.HBM)


def to_peer(x, r):
    dx, dc = r // 2, r % 2
    if r == 0:
        return x
    pairs = [(i, ((i // 2 + dx) % NX) * 2 + (i + dc) % 2) for i in range(HALF)]
    return lax.ppermute(x, ("x", "c"), pairs)


def exchange(x, axes):
    return lax.all_to_all(x, axes, split_axis=0, concat_axis=0, tiled=True)


def local(grad_out, hidden_act, gate_weights, routing, resp_lengths, advantage, w_down):
    pos = jnp.stack([lax.axis_index(a).astype(I32) for a in ("z", "yl", "yh", "x", "c")])
    gt = grad_out.T
    ht = jnp.transpose(hidden_act, (1, 2, 0))
    gates = gate_weights.T
    rt = routing.T

    low, high, pm = prep(pos, resp_lengths, advantage, gt, rt)
    low_par = shift(low, "yh", 2, 1)
    own = call(
        own_kernel,
        "send_own",
        [SMEM] + [ANY] * 3 + [VMEM] * 3,
        [((HSLOT, WIDE + HW), BF)],
        [
            pltpu.VMEM((TOPK, FFW, ROWS), BF),
            pltpu.VMEM((TOPK, ROWS), BF),
            pltpu.VMEM((TOPK, ROWS), I32),
            pltpu.SemaphoreType.DMA((3,)),
        ]
        + spread_scratch(WIDE + HW),
        where=ANY,
    )(pos, *(pltpu.with_memory_space_constraint(v, pltpu.HBM) for v in (ht, gates, rt)), pm, low, high)[0]


    ready = pltpu.with_memory_space_constraint(own, pltpu.HBM)
    wt = call(pad_kernel, "weight_pad", [VMEM, ANY], [((PAD, HW), BF)], weight=COVER_PAD)(
        w_down[0].T, ready
    )[0]
    parts = [wt] + [shift(wt, "yl", NY, j) for j in range(1, NY)]
    w4 = call(weight_kernel, "weight_part", [SMEM] + [VMEM] * NY, [((NY, PAD, HW), BF)])(
        pos, *parts
    )[0].reshape(NY * PAD, HW)
    weight = lax.all_gather(w4, "z", axis=0, tiled=True)

    high_out, pm_out, _ = lax.optimization_barrier((high, pm, own))
    high_par = shift(high_out, "yh", 2, 1)
    hid_par = call(other_kernel, "send_other", [SMEM] + [VMEM] * 4, [((HSLOT, HW), BF)])(
        pos, ht, gates, rt, pm_out
    )[0]
    hid_par = shift(hid_par, "yh", 2, 1)
    own = exchange(own.reshape(HALF, CAP, WIDE + HW), ("x", "c")).reshape(HSLOT, WIDE + HW)

    def forward(x, after):
        width = x.shape[1]
        x, _ = lax.optimization_barrier((x, after))
        return exchange(x.reshape(HALF, CAP, width), ("x", "c")).reshape(HSLOT, width)

    par_low = call(
        low_kernel,
        "send_low",
        [VMEM],
        [((HSLOT, CW), BF)],
        spread_scratch(CW),
        where=ANY,
        weight=COVER_LOW,
    )(low_par)[0]
    par_low = forward(par_low, own)
    par_high = call(
        high_kernel,
        "send_high",
        [VMEM] * 3,
        [((HSLOT, CW + HW), BF)],
        spread_scratch(CW + HW),
        where=ANY,
        weight=COVER,
    )(high_par, low_par, hid_par)[0]
    par_high = forward(par_high, par_low)

    terms = call(
        term_kernel,
        "grad_term",
        [VMEM, ANY, VMEM, ANY],
        [((WIDE, FFW), BF)],
        [
            pltpu.VMEM((HSLOT, CW), BF),
            pltpu.VMEM((WIDE, FFW), BF),
            pltpu.SemaphoreType.DMA((NZ + 1,)),
        ],
        mib=20,
        where=ANY,
    )(own, held(par_low), par_high, held(weight))[0]
    terms = exchange(terms.reshape(NDP, PAD, FFW), ("z", "yl"))

    backs = call(
        back_kernel,
        "back_product",
        [SMEM] + [VMEM] * 4,
        [((2, CAP, FFW), BF)] * HALF,
        [pltpu.VMEM((HSLOT, FFW), F32)],
        mib=20,
    )(pos, own, par_low, par_high, weight)
    backs = [to_peer(b, r) for r, b in enumerate(backs)]
    other = call(stack_kernel, "stack_other", [VMEM] * HALF, [((HALF, CAP, FFW), BF)])(*backs)[0]
    other = shift(other, "yh", 2, 1)
    gh, gg = call(
        home_kernel,
        "bring_home",
        [SMEM] + [VMEM] * (5 + HALF),
        [((TOPK, FFW, ROWS), F32), ((TOPK, ROWS), F32)],
    )(pos, ht, gates, pm, rt, other, *backs)
    terms, gg = lax.optimization_barrier((terms, gg))
    gd = call(sum_kernel, "sum_terms", [VMEM], [((OWN, FFW), F32)])(terms)[0]
    return gd.T[None], jnp.transpose(gh, (2, 0, 1)), gg.T


def solution(mesh):
    every = ("z", "yl", "x", "yh", "c")
    fine = Mesh(mesh.devices.reshape(NZ, NY, NX, 2, 2), every)
    rows2 = P(every, None)
    rows3 = P(every, None, None)
    cols = P(("x", "yh", "c"), None, ("z", "yl"))
    return jax.shard_map(
        local,
        mesh=fine,
        in_specs=(rows2, rows3, rows2, rows2, rows2, rows2, cols),
        out_specs=(cols, rows3, rows2),
        check_vma=False,
    )
```

```python
import jax
import jax.numpy as jnp
from jax import lax
from jax.experimental import pallas as pl
from jax.experimental.pallas import tpu as pltpu
from jax.sharding import Mesh, PartitionSpec as P

BF = jnp.bfloat16
F32 = jnp.float32
I32 = jnp.int32
NT = (((1,), (1,)), ((), ()))
TN = (((0,), (0,)), ((), ()))
NN = (((1,), (0,)), ((), ()))
ROWS, D, TOPK, FFW, NEXP, CAP = 128, 2880, 4, 360, 16, 40
NZ, NY, NX = 8, 4, 4
NDP = NZ * NY
OWN = D // NDP
PAD = 96
WIDE = NDP * PAD
HALF = NEXP // 2
HSLOT = HALF * CAP
STEP = 768
HW = 384
COVER_PAD = 50_000_000_000
COVER_LOW = 10_000_000_000
COVER = 50_000_000_000
BLK = NY * PAD
CW = WIDE // 2
def spread_scratch(width):
    return [pltpu.VMEM((HSLOT, width), BF), pltpu.SemaphoreType.DMA((WIDE // STEP + 1,))]


VMEM = pl.BlockSpec(memory_space=pltpu.VMEM)
SMEM = pl.BlockSpec(memory_space=pltpu.SMEM)
ANY = pl.BlockSpec(memory_space=pltpu.HBM)


def call(body, name, ins, outs, scratch=(), mib=14, weight=None, where=None):
    outs = [(pltpu.HBM if where else jax.ShapeDtypeStruct)(*o) for o in outs]
    return pl.pallas_call(
        body,
        in_specs=list(ins),
        out_specs=[where or VMEM] * len(outs),
        out_shape=outs,
        scratch_shapes=list(scratch),
        compiler_params=pltpu.CompilerParams(vmem_limit_bytes=mib << 20),
        name=name,
        cost_estimate=weight and pl.CostEstimate(flops=weight, transcendentals=0, bytes_accessed=0),
    )


def expert_ids():
    row = lax.broadcasted_iota(I32, (NEXP, ROWS), 0)
    return ((row >> 1) & 3) * 4 + (row >> 3) * 2 + (row & 1)


def slot_onehot(place, n):
    c = lax.broadcasted_iota(I32, (n, CAP, ROWS), 1).astype(F32)
    return (place[:, None, :] == c).astype(F32).reshape(n * CAP, ROWS)


def prep_kernel(pos_ref, len_hbm, adv_hbm, g_hbm, r_hbm, low_ref, high_ref, pm_ref, *refs):
    g_ref, r_ref, len_ref, adv_ref, scr, sems = refs
    pairs = [(g_hbm, g_ref), (r_hbm, r_ref), (len_hbm, len_ref), (adv_hbm, adv_ref)]
    copies = [pltpu.make_async_copy(a, b, sems.at[i]) for i, (a, b) in enumerate(pairs)]
    for c in copies:
        c.start()
    for c in copies[1:]:
        c.wait()
    eid = expert_ids()
    hit = r_ref[0:1] == eid
    for k in range(1, TOPK):
        hit = hit | (r_ref[k : k + 1] == eid)
    a = lax.broadcasted_iota(I32, (ROWS, ROWS), 0)
    b = lax.broadcasted_iota(I32, (ROWS, ROWS), 1)
    before = (a < b).astype(F32).astype(BF)
    rank = lax.dot_general(hit.astype(F32).astype(BF), before, NN, preferred_element_type=F32)
    place = jnp.where(hit, rank, -1.0)
    pm_ref[...] = place
    other = jnp.where(pos_ref[2] == 0, place[HALF:], place[:HALF])
    low_ref[CW:] = jnp.concatenate([other, jnp.zeros((HALF, ROWS), F32)], axis=0).astype(BF)
    pos = lax.broadcasted_iota(I32, (8, ROWS), 1)
    start = jnp.int32(0)
    scale = jnp.zeros((8, ROWS), F32)
    for s in range(4):
        n = len_ref[0, s]
        ratio = jnp.full((8, ROWS), adv_ref[0, s], F32) / jnp.full((8, ROWS), n, I32).astype(F32)
        scale = jnp.where((pos >= start) & (pos < start + n), ratio, scale)
        start = start + n
    copies[0].wait()
    scr[0:D] = g_ref[...].astype(F32) * scale[0:1]
    scr[D:] = jnp.zeros((8, ROWS), F32)
    keep = lax.broadcasted_iota(I32, (PAD, ROWS), 0) < OWN
    for d in range(NDP):
        block = scr[d * OWN : d * OWN + PAD]
        cot_ref, at = (low_ref, d * PAD) if d < NDP // 2 else (high_ref, d * PAD - CW)
        cot_ref[at : at + PAD] = jnp.where(keep, block, 0.0).astype(BF)


def prep(pos, lens, adv, gt, rt):
    outs = [((CW + 16, ROWS), BF), ((CW, ROWS), BF), ((NEXP, ROWS), F32)]
    scratch = [
        pltpu.VMEM((D, ROWS), BF),
        pltpu.VMEM((TOPK, ROWS), I32),
        pltpu.SMEM((1, 4), I32),
        pltpu.SMEM((1, 4), F32),
        pltpu.VMEM((D + 8, ROWS), F32),
        pltpu.SemaphoreType.DMA((4,)),
    ]
    args = [pltpu.with_memory_space_constraint(v, pltpu.HBM) for v in (lens, adv, gt, rt)]
    return call(prep_kernel, "prep", [SMEM] + [ANY] * 4, outs, scratch)(pos, *args)


def send(copies, scr, out_hbm, at, n, sems):
    cols = pl.ds(at, n)
    copies.append(pltpu.make_async_copy(scr.at[:, cols], out_hbm.at[:, cols], sems.at[len(copies)]))
    copies[-1].start()


def spread(s, cots, scr, out_hbm, sems):
    copies = []
    for n, cot_ref in enumerate(cots):
        for i in range(0, CW, STEP):
            at = n * CW + i
            scr[:, at : at + STEP] = lax.dot_general(
                s, cot_ref[i : i + STEP], NT, preferred_element_type=F32
            ).astype(BF)
            send(copies, scr, out_hbm, at, STEP, sems)
    return copies


def hidden_rows(h_ref, gate_ref, r_ref, place, eid):
    n = place.shape[0]
    acc = jnp.zeros((n * CAP, HW), F32)
    for k in range(TOPK):
        s = slot_onehot(jnp.where(r_ref[k : k + 1] == eid, place, -1.0), n).astype(BF)
        rows = jnp.concatenate(
            [h_ref[k], gate_ref[k : k + 1], jnp.zeros((HW - FFW - 1, ROWS), BF)], axis=0
        )
        acc = acc + lax.dot_general(s, rows, NT, preferred_element_type=F32)
    return acc.astype(BF)


def other_kernel(pos_ref, h_ref, gate_ref, r_ref, pm_ref, out_ref):
    first = pos_ref[2] == 0
    eid = expert_ids()
    place = jnp.where(first, pm_ref[HALF:], pm_ref[:HALF])
    out_ref[...] = hidden_rows(h_ref, gate_ref, r_ref, place, jnp.where(first, eid[HALF:], eid[:HALF]))


def own_kernel(pos_ref, h_hbm, gate_hbm, r_hbm, pm_ref, low_ref, high_ref, out_hbm, *refs):
    h_ref, gate_ref, r_ref, sem_in, scr, sems = refs
    pairs = [(h_hbm, h_ref), (gate_hbm, gate_ref), (r_hbm, r_ref)]
    loads = [pltpu.make_async_copy(a, b, sem_in.at[i]) for i, (a, b) in enumerate(pairs)]
    for c in loads:
        c.start()
    first = pos_ref[2] == 0
    eid = expert_ids()
    place = jnp.where(first, pm_ref[:HALF], pm_ref[HALF:])
    copies = spread(slot_onehot(place, HALF).astype(BF), (low_ref, high_ref), scr, out_hbm, sems)
    for c in loads:
        c.wait()
    scr[:, WIDE:] = hidden_rows(
        h_ref, gate_ref, r_ref, place, jnp.where(first, eid[:HALF], eid[HALF:])
    )
    send(copies, scr, out_hbm, WIDE, HW, sems)
    for c in copies:
        c.wait()


def low_kernel(cot_ref, out_hbm, scr, sems):
    place = cot_ref[CW:].astype(F32)[:HALF]
    for c in spread(slot_onehot(place, HALF).astype(BF), (cot_ref,), scr, out_hbm, sems):
        c.wait()


def high_kernel(cot_ref, pm_ref, h_ref, out_hbm, scr, sems):
    place = pm_ref[CW:].astype(F32)[:HALF]
    copies = spread(slot_onehot(place, HALF).astype(BF), (cot_ref,), scr, out_hbm, sems)
    scr[:, CW:] = h_ref[...]
    send(copies, scr, out_hbm, CW, HW, sems)
    for c in copies:
        c.wait()


def term_kernel(own_ref, low_hbm, high_ref, out_hbm, low_ref, scr, sems):
    load = pltpu.make_async_copy(low_hbm, low_ref, sems.at[NZ])
    load.start()
    hid = [own_ref[:, WIDE:], high_ref[:, CW:]]
    gate = [h[:, FFW : FFW + 1].astype(F32) for h in hid]
    copies = []
    for z in [*range(NZ // 2, NZ), *range(NZ // 2)]:
        if z == 0:
            load.wait()
        acc = jnp.zeros((BLK, FFW), F32)
        at = z * BLK
        cots = [own_ref[:, at : at + BLK]]
        cots.append(low_ref[:, at : at + BLK] if at < CW else high_ref[:, at - CW : at - CW + BLK])
        for cot, h, g in zip(cots, hid, gate):
            gated = (cot.astype(F32) * g).astype(BF)
            acc = acc + lax.dot_general(gated, h[:, :FFW], TN, preferred_element_type=F32)
        rows = pl.ds(at, BLK)
        scr[rows] = acc.astype(BF)
        copies.append(pltpu.make_async_copy(scr.at[rows], out_hbm.at[rows], sems.at[z]))
        copies[-1].start()
    for c in copies:
        c.wait()


def sum_kernel(x_ref, out_ref):
    v = x_ref[0].astype(F32)
    for d in range(1, NDP):
        v = v + x_ref[d].astype(F32)
    out_ref[...] = v[:OWN]


def pad_kernel(w_ref, _, out_ref):
    out_ref[...] = jnp.zeros((PAD, HW), BF)
    out_ref[:OWN, :FFW] = w_ref[...]


def weight_kernel(pos_ref, *refs):
    out_ref = refs[NY]
    for j in range(NY):
        out_ref[(pos_ref[1] + NY - j) % NY] = refs[j][...]


def peer(pos_ref, r, sign):
    dx, dc = r // 2, r % 2
    return ((pos_ref[3] + NX + sign * dx) % NX) * 2 + (pos_ref[4] + dc) % 2


def back_kernel(pos_ref, own_ref, low_ref, high_ref, w_ref, *refs):
    outs, scr = refs[:HALF], refs[HALF]
    for i in range(2):
        parts = (own_ref[:, :CW], own_ref[:, CW:WIDE]) if i == 0 else (low_ref[...], high_ref[:, :CW])
        acc = lax.dot_general(parts[0], w_ref[:CW, :FFW], NN, preferred_element_type=F32)
        scr[...] = acc + lax.dot_general(
            parts[1], w_ref[CW:, :FFW], NN, preferred_element_type=F32
        )
        for r, out_ref in enumerate(outs):
            at = pl.multiple_of(peer(pos_ref, r, 1) * CAP, 8)
            out_ref[i] = scr[pl.ds(at, CAP)].astype(BF)


def stack_kernel(*refs):
    for r in range(HALF):
        refs[HALF][r] = refs[r][1]


def home_kernel(pos_ref, h_ref, gate_ref, pm_ref, r_ref, other_ref, *refs):
    owns, gh_ref, gg_ref = refs[:HALF], refs[HALF], refs[HALF + 1]
    gate = gate_ref[...].astype(F32)
    c = lax.broadcasted_iota(I32, (CAP, ROWS), 0).astype(F32)
    yh = pos_ref[2]
    pieces, places, ids = [], [], []
    for half in range(2):
        side = yh if half == 0 else 1 - yh
        for r in range(HALF):
            i = peer(pos_ref, r, -1)
            pieces.append((owns[r][0] if half == 0 else other_ref[r]).astype(F32))
            places.append(pm_ref[pl.ds(side * HALF + i, 1)])
            ids.append((i // 2) * 4 + side * 2 + i % 2)
    x = jnp.concatenate(pieces, axis=0).astype(BF)
    for k in range(TOPK):
        rk = r_ref[k : k + 1]
        rows = [
            (jnp.where(rk == e, p, -1.0) == c).astype(F32) for p, e in zip(places, ids)
        ]
        s = jnp.concatenate(rows, axis=0).astype(BF)
        back = lax.dot_general(x, s, TN, preferred_element_type=F32)
        gh_ref[k] = back * gate[k : k + 1]
        gg_ref[k : k + 1] = jnp.sum(back * h_ref[k].astype(F32), axis=0, keepdims=True)


def shift(x, axis, n, by):
    return lax.ppermute(x, axis, [(i, (i + by) % n) for i in range(n)])


def held(x):
    return pltpu.with_memory_space_constraint(x, pltpu.HBM)


def to_peer(x, r):
    dx, dc = r // 2, r % 2
    if r == 0:
        return x
    pairs = [(i, ((i // 2 + dx) % NX) * 2 + (i + dc) % 2) for i in range(HALF)]
    return lax.ppermute(x, ("x", "c"), pairs)


def exchange(x, axes):
    return lax.all_to_all(x, axes, split_axis=0, concat_axis=0, tiled=True)


def local(grad_out, hidden_act, gate_weights, routing, resp_lengths, advantage, w_down):
    pos = jnp.stack([lax.axis_index(a).astype(I32) for a in ("z", "yl", "yh", "x", "c")])
    gt = grad_out.T
    ht = jnp.transpose(hidden_act, (1, 2, 0))
    gates = gate_weights.T
    rt = routing.T

    low, high, pm = prep(pos, resp_lengths, advantage, gt, rt)
    low_par = shift(low, "yh", 2, 1)
    own = call(
        own_kernel,
        "send_own",
        [SMEM] + [ANY] * 3 + [VMEM] * 3,
        [((HSLOT, WIDE + HW), BF)],
        [
            pltpu.VMEM((TOPK, FFW, ROWS), BF),
            pltpu.VMEM((TOPK, ROWS), BF),
            pltpu.VMEM((TOPK, ROWS), I32),
            pltpu.SemaphoreType.DMA((3,)),
        ]
        + spread_scratch(WIDE + HW),
        where=ANY,
    )(pos, *(pltpu.with_memory_space_constraint(v, pltpu.HBM) for v in (ht, gates, rt)), pm, low, high)[0]


    ready = pltpu.with_memory_space_constraint(own, pltpu.HBM)
    wt = call(pad_kernel, "weight_pad", [VMEM, ANY], [((PAD, HW), BF)], weight=COVER_PAD)(
        w_down[0].T, ready
    )[0]
    parts = [wt] + [shift(wt, "yl", NY, j) for j in range(1, NY)]
    w4 = call(weight_kernel, "weight_part", [SMEM] + [VMEM] * NY, [((NY, PAD, HW), BF)])(
        pos, *parts
    )[0].reshape(NY * PAD, HW)
    weight = lax.all_gather(w4, "z", axis=0, tiled=True)

    high_out, pm_out, _ = lax.optimization_barrier((high, pm, own))
    high_par = shift(high_out, "yh", 2, 1)
    hid_par = call(other_kernel, "send_other", [SMEM] + [VMEM] * 4, [((HSLOT, HW), BF)])(
        pos, ht, gates, rt, pm_out
    )[0]
    hid_par = shift(hid_par, "yh", 2, 1)
    own = exchange(own.reshape(HALF, CAP, WIDE + HW), ("x", "c")).reshape(HSLOT, WIDE + HW)

    def forward(x, after):
        width = x.shape[1]
        x, _ = lax.optimization_barrier((x, after))
        return exchange(x.reshape(HALF, CAP, width), ("x", "c")).reshape(HSLOT, width)

    par_low = call(
        low_kernel,
        "send_low",
        [VMEM],
        [((HSLOT, CW), BF)],
        spread_scratch(CW),
        where=ANY,
        weight=COVER_LOW,
    )(low_par)[0]
    par_low = forward(par_low, own)
    par_high = call(
        high_kernel,
        "send_high",
        [VMEM] * 3,
        [((HSLOT, CW + HW), BF)],
        spread_scratch(CW + HW),
        where=ANY,
        weight=COVER,
    )(high_par, low_par, hid_par)[0]
    par_high = forward(par_high, par_low)

    terms = call(
        term_kernel,
        "grad_term",
        [VMEM, ANY, VMEM],
        [((WIDE, FFW), BF)],
        [
            pltpu.VMEM((HSLOT, CW), BF),
            pltpu.VMEM((WIDE, FFW), BF),
            pltpu.SemaphoreType.DMA((NZ + 1,)),
        ],
        mib=20,
        where=ANY,
    )(own, held(par_low), par_high)[0]
    terms, weight = lax.optimization_barrier((terms, weight))
    terms = exchange(terms.reshape(NDP, PAD, FFW), ("z", "yl"))

    backs = call(
        back_kernel,
        "back_product",
        [SMEM] + [VMEM] * 4,
        [((2, CAP, FFW), BF)] * HALF,
        [pltpu.VMEM((HSLOT, FFW), F32)],
        mib=20,
    )(pos, own, par_low, par_high, weight)
    backs = [to_peer(b, r) for r, b in enumerate(backs)]
    other = call(stack_kernel, "stack_other", [VMEM] * HALF, [((HALF, CAP, FFW), BF)])(*backs)[0]
    other = shift(other, "yh", 2, 1)
    gh, gg = call(
        home_kernel,
        "bring_home",
        [SMEM] + [VMEM] * (5 + HALF),
        [((TOPK, FFW, ROWS), F32), ((TOPK, ROWS), F32)],
    )(pos, ht, gates, pm, rt, other, *backs)
    terms, gg = lax.optimization_barrier((terms, gg))
    gd = call(sum_kernel, "sum_terms", [VMEM], [((OWN, FFW), F32)])(terms)[0]
    return gd.T[None], jnp.transpose(gh, (2, 0, 1)), gg.T


def solution(mesh):
    every = ("z", "yl", "x", "yh", "c")
    fine = Mesh(mesh.devices.reshape(NZ, NY, NX, 2, 2), every)
    rows2 = P(every, None)
    rows3 = P(every, None, None)
    cols = P(("x", "yh", "c"), None, ("z", "yl"))
    return jax.shard_map(
        local,
        mesh=fine,
        in_specs=(rows2, rows3, rows2, rows2, rows2, rows2, cols),
        out_specs=(cols, rows3, rows2),
        check_vma=False,
    )
```

```python
import jax
import jax.numpy as jnp
from jax import lax
from jax.experimental import pallas as pl
from jax.experimental.pallas import tpu as pltpu
from jax.sharding import Mesh, PartitionSpec as P

BF = jnp.bfloat16
F32 = jnp.float32
I32 = jnp.int32
NT = (((1,), (1,)), ((), ()))
TN = (((0,), (0,)), ((), ()))
NN = (((1,), (0,)), ((), ()))
ROWS, D, TOPK, FFW, NEXP, CAP = 128, 2880, 4, 360, 16, 40
NZ, NY, NX = 8, 4, 4
NDP = NZ * NY
OWN = D // NDP
PAD = 96
WIDE = NDP * PAD
SLABS = ((0, 128), (128, 256), (256, FFW))
SENT = 272
HALF = NEXP // 2
HSLOT = HALF * CAP
STEP = 768
HW = 384
COVER_PAD = 50_000_000_000
COVER_LOW = 10_000_000_000
COVER = 50_000_000_000
BLK = NY * PAD
CW = WIDE // 2
def spread_scratch(width):
    return [pltpu.VMEM((HSLOT, width), BF), pltpu.SemaphoreType.DMA((WIDE // STEP + 1,))]


VMEM = pl.BlockSpec(memory_space=pltpu.VMEM)
SMEM = pl.BlockSpec(memory_space=pltpu.SMEM)
ANY = pl.BlockSpec(memory_space=pltpu.HBM)


def call(body, name, ins, outs, scratch=(), mib=14, weight=None, where=None):
    outs = [(pltpu.HBM if where else jax.ShapeDtypeStruct)(*o) for o in outs]
    return pl.pallas_call(
        body,
        in_specs=list(ins),
        out_specs=[where or VMEM] * len(outs),
        out_shape=outs,
        scratch_shapes=list(scratch),
        compiler_params=pltpu.CompilerParams(vmem_limit_bytes=mib << 20),
        name=name,
        cost_estimate=weight and pl.CostEstimate(flops=weight, transcendentals=0, bytes_accessed=0),
    )


def expert_ids():
    row = lax.broadcasted_iota(I32, (NEXP, ROWS), 0)
    return ((row >> 1) & 3) * 4 + (row >> 3) * 2 + (row & 1)


def slot_onehot(place, n):
    c = lax.broadcasted_iota(I32, (n, CAP, ROWS), 1).astype(F32)
    return (place[:, None, :] == c).astype(F32).reshape(n * CAP, ROWS)


def prep_kernel(pos_ref, len_hbm, adv_hbm, g_hbm, r_hbm, low_ref, high_ref, pm_ref, *refs):
    g_ref, r_ref, len_ref, adv_ref, scr, sems = refs
    pairs = [(g_hbm, g_ref), (r_hbm, r_ref), (len_hbm, len_ref), (adv_hbm, adv_ref)]
    copies = [pltpu.make_async_copy(a, b, sems.at[i]) for i, (a, b) in enumerate(pairs)]
    for c in copies:
        c.start()
    for c in copies[1:]:
        c.wait()
    eid = expert_ids()
    hit = r_ref[0:1] == eid
    for k in range(1, TOPK):
        hit = hit | (r_ref[k : k + 1] == eid)
    a = lax.broadcasted_iota(I32, (ROWS, ROWS), 0)
    b = lax.broadcasted_iota(I32, (ROWS, ROWS), 1)
    before = (a < b).astype(F32).astype(BF)
    rank = lax.dot_general(hit.astype(F32).astype(BF), before, NN, preferred_element_type=F32)
    place = jnp.where(hit, rank, -1.0)
    pm_ref[...] = place
    other = jnp.where(pos_ref[2] == 0, place[HALF:], place[:HALF])
    low_ref[CW:] = jnp.concatenate([other, jnp.zeros((HALF, ROWS), F32)], axis=0).astype(BF)
    pos = lax.broadcasted_iota(I32, (8, ROWS), 1)
    start = jnp.int32(0)
    scale = jnp.zeros((8, ROWS), F32)
    for s in range(4):
        n = len_ref[0, s]
        ratio = jnp.full((8, ROWS), adv_ref[0, s], F32) / jnp.full((8, ROWS), n, I32).astype(F32)
        scale = jnp.where((pos >= start) & (pos < start + n), ratio, scale)
        start = start + n
    copies[0].wait()
    scr[0:D] = g_ref[...].astype(F32) * scale[0:1]
    scr[D:] = jnp.zeros((8, ROWS), F32)
    keep = lax.broadcasted_iota(I32, (PAD, ROWS), 0) < OWN
    for d in range(NDP):
        block = scr[d * OWN : d * OWN + PAD]
        cot_ref, at = (low_ref, d * PAD) if d < NDP // 2 else (high_ref, d * PAD - CW)
        cot_ref[at : at + PAD] = jnp.where(keep, block, 0.0).astype(BF)


def prep(pos, lens, adv, gt, rt):
    outs = [((CW + 16, ROWS), BF), ((CW, ROWS), BF), ((NEXP, ROWS), F32)]
    scratch = [
        pltpu.VMEM((D, ROWS), BF),
        pltpu.VMEM((TOPK, ROWS), I32),
        pltpu.SMEM((1, 4), I32),
        pltpu.SMEM((1, 4), F32),
        pltpu.VMEM((D + 8, ROWS), F32),
        pltpu.SemaphoreType.DMA((4,)),
    ]
    args = [pltpu.with_memory_space_constraint(v, pltpu.HBM) for v in (lens, adv, gt, rt)]
    return call(prep_kernel, "prep", [SMEM] + [ANY] * 4, outs, scratch)(pos, *args)


def send(copies, scr, out_hbm, at, n, sems):
    cols = pl.ds(at, n)
    copies.append(pltpu.make_async_copy(scr.at[:, cols], out_hbm.at[:, cols], sems.at[len(copies)]))
    copies[-1].start()


def spread(s, cots, scr, out_hbm, sems):
    copies = []
    for n, cot_ref in enumerate(cots):
        for i in range(0, CW, STEP):
            at = n * CW + i
            scr[:, at : at + STEP] = lax.dot_general(
                s, cot_ref[i : i + STEP], NT, preferred_element_type=F32
            ).astype(BF)
            send(copies, scr, out_hbm, at, STEP, sems)
    return copies


def hidden_rows(h_ref, gate_ref, r_ref, place, eid):
    n = place.shape[0]
    acc = jnp.zeros((n * CAP, HW), F32)
    for k in range(TOPK):
        s = slot_onehot(jnp.where(r_ref[k : k + 1] == eid, place, -1.0), n).astype(BF)
        rows = jnp.concatenate(
            [h_ref[k], gate_ref[k : k + 1], jnp.zeros((HW - FFW - 1, ROWS), BF)], axis=0
        )
        acc = acc + lax.dot_general(s, rows, NT, preferred_element_type=F32)
    return acc.astype(BF)


def other_kernel(pos_ref, h_ref, gate_ref, r_ref, pm_ref, out_ref):
    first = pos_ref[2] == 0
    eid = expert_ids()
    place = jnp.where(first, pm_ref[HALF:], pm_ref[:HALF])
    out_ref[...] = hidden_rows(h_ref, gate_ref, r_ref, place, jnp.where(first, eid[HALF:], eid[:HALF]))


def own_kernel(pos_ref, h_hbm, gate_hbm, r_hbm, pm_ref, low_ref, high_ref, out_hbm, *refs):
    h_ref, gate_ref, r_ref, sem_in, scr, sems = refs
    pairs = [(h_hbm, h_ref), (gate_hbm, gate_ref), (r_hbm, r_ref)]
    loads = [pltpu.make_async_copy(a, b, sem_in.at[i]) for i, (a, b) in enumerate(pairs)]
    for c in loads:
        c.start()
    first = pos_ref[2] == 0
    eid = expert_ids()
    place = jnp.where(first, pm_ref[:HALF], pm_ref[HALF:])
    copies = spread(slot_onehot(place, HALF).astype(BF), (low_ref, high_ref), scr, out_hbm, sems)
    for c in loads:
        c.wait()
    scr[:, WIDE:] = hidden_rows(
        h_ref, gate_ref, r_ref, place, jnp.where(first, eid[:HALF], eid[HALF:])
    )
    send(copies, scr, out_hbm, WIDE, HW, sems)
    for c in copies:
        c.wait()


def low_kernel(cot_ref, out_hbm, scr, sems):
    place = cot_ref[CW:].astype(F32)[:HALF]
    for c in spread(slot_onehot(place, HALF).astype(BF), (cot_ref,), scr, out_hbm, sems):
        c.wait()


def high_kernel(cot_ref, pm_ref, h_ref, out_hbm, scr, sems):
    place = pm_ref[CW:].astype(F32)[:HALF]
    copies = spread(slot_onehot(place, HALF).astype(BF), (cot_ref,), scr, out_hbm, sems)
    scr[:, CW:] = h_ref[...]
    send(copies, scr, out_hbm, CW, HW, sems)
    for c in copies:
        c.wait()


def term_kernel(own_ref, low_hbm, high_ref, out_hbm, low_ref, pack, scr, sems):
    load = pltpu.make_async_copy(low_hbm, low_ref, sems.at[NZ])
    load.start()
    pack[...] = jnp.zeros((NY, SENT, 128), F32)
    hid = [own_ref[:, WIDE:], high_ref[:, CW:]]
    gate = [h[:, FFW : FFW + 1].astype(F32) for h in hid]
    copies = []
    for z in [*range(NZ // 2, NZ), *range(NZ // 2)]:
        if z == 0:
            load.wait()
        acc = jnp.zeros((BLK, FFW), F32)
        at = z * BLK
        cots = [own_ref[:, at : at + BLK]]
        cots.append(low_ref[:, at : at + BLK] if at < CW else high_ref[:, at - CW : at - CW + BLK])
        for cot, h, g in zip(cots, hid, gate):
            gated = (cot.astype(F32) * g).astype(BF)
            acc = acc + lax.dot_general(gated, h[:, :FFW], TN, preferred_element_type=F32)
        for y in range(NY):
            v = acc[y * PAD : y * PAD + OWN]
            for n, (a, b) in enumerate(SLABS):
                pack[y, n * OWN : (n + 1) * OWN, : b - a] = v[:, a:b]
            at = (z * NY + y) * SENT
            scr[at : at + SENT] = pack[y].astype(BF)
        rows = pl.ds(z * NY * SENT, NY * SENT)
        copies.append(pltpu.make_async_copy(scr.at[rows], out_hbm.at[rows], sems.at[z]))
        copies[-1].start()
    for c in copies:
        c.wait()


def sum_kernel(x_ref, out_ref, scr):
    v = x_ref[0].astype(F32)
    for d in range(1, NDP):
        v = v + x_ref[d].astype(F32)
    scr[...] = v
    for n, (a, b) in enumerate(SLABS):
        out_ref[:, a:b] = scr[n * OWN : (n + 1) * OWN, : b - a]


def pad_kernel(w_ref, _, out_ref):
    out_ref[...] = jnp.zeros((PAD, HW), BF)
    out_ref[:OWN, :FFW] = w_ref[...]


def weight_kernel(pos_ref, *refs):
    out_ref = refs[NY]
    for j in range(NY):
        out_ref[(pos_ref[1] + NY - j) % NY] = refs[j][...]


def peer(pos_ref, r, sign):
    dx, dc = r // 2, r % 2
    return ((pos_ref[3] + NX + sign * dx) % NX) * 2 + (pos_ref[4] + dc) % 2


def back_kernel(pos_ref, own_ref, low_ref, high_ref, w_ref, *refs):
    outs, scr = refs[:HALF], refs[HALF]
    for i in range(2):
        parts = (own_ref[:, :CW], own_ref[:, CW:WIDE]) if i == 0 else (low_ref[...], high_ref[:, :CW])
        acc = lax.dot_general(parts[0], w_ref[:CW, :FFW], NN, preferred_element_type=F32)
        scr[...] = acc + lax.dot_general(
            parts[1], w_ref[CW:, :FFW], NN, preferred_element_type=F32
        )
        for r, out_ref in enumerate(outs):
            at = pl.multiple_of(peer(pos_ref, r, 1) * CAP, 8)
            out_ref[i] = scr[pl.ds(at, CAP)].astype(BF)


def stack_kernel(*refs):
    for r in range(HALF):
        refs[HALF][r] = refs[r][1]


def home_kernel(pos_ref, h_ref, gate_ref, pm_ref, r_ref, other_ref, *refs):
    owns, gh_ref, gg_ref = refs[:HALF], refs[HALF], refs[HALF + 1]
    gate = gate_ref[...].astype(F32)
    c = lax.broadcasted_iota(I32, (CAP, ROWS), 0).astype(F32)
    yh = pos_ref[2]
    pieces, places, ids = [], [], []
    for half in range(2):
        side = yh if half == 0 else 1 - yh
        for r in range(HALF):
            i = peer(pos_ref, r, -1)
            pieces.append((owns[r][0] if half == 0 else other_ref[r]).astype(F32))
            places.append(pm_ref[pl.ds(side * HALF + i, 1)])
            ids.append((i // 2) * 4 + side * 2 + i % 2)
    x = jnp.concatenate(pieces, axis=0).astype(BF)
    for k in range(TOPK):
        rk = r_ref[k : k + 1]
        rows = [
            (jnp.where(rk == e, p, -1.0) == c).astype(F32) for p, e in zip(places, ids)
        ]
        s = jnp.concatenate(rows, axis=0).astype(BF)
        back = lax.dot_general(x, s, TN, preferred_element_type=F32)
        gh_ref[k] = back * gate[k : k + 1]
        gg_ref[k : k + 1] = jnp.sum(back * h_ref[k].astype(F32), axis=0, keepdims=True)


def shift(x, axis, n, by):
    return lax.ppermute(x, axis, [(i, (i + by) % n) for i in range(n)])


def held(x):
    return pltpu.with_memory_space_constraint(x, pltpu.HBM)


def to_peer(x, r):
    dx, dc = r // 2, r % 2
    if r == 0:
        return x
    pairs = [(i, ((i // 2 + dx) % NX) * 2 + (i + dc) % 2) for i in range(HALF)]
    return lax.ppermute(x, ("x", "c"), pairs)


def exchange(x, axes):
    return lax.all_to_all(x, axes, split_axis=0, concat_axis=0, tiled=True)


def local(grad_out, hidden_act, gate_weights, routing, resp_lengths, advantage, w_down):
    pos = jnp.stack([lax.axis_index(a).astype(I32) for a in ("z", "yl", "yh", "x", "c")])
    gt = grad_out.T
    ht = jnp.transpose(hidden_act, (1, 2, 0))
    gates = gate_weights.T
    rt = routing.T

    low, high, pm = prep(pos, resp_lengths, advantage, gt, rt)
    low_par = shift(low, "yh", 2, 1)
    own = call(
        own_kernel,
        "send_own",
        [SMEM] + [ANY] * 3 + [VMEM] * 3,
        [((HSLOT, WIDE + HW), BF)],
        [
            pltpu.VMEM((TOPK, FFW, ROWS), BF),
            pltpu.VMEM((TOPK, ROWS), BF),
            pltpu.VMEM((TOPK, ROWS), I32),
            pltpu.SemaphoreType.DMA((3,)),
        ]
        + spread_scratch(WIDE + HW),
        where=ANY,
    )(pos, *(pltpu.with_memory_space_constraint(v, pltpu.HBM) for v in (ht, gates, rt)), pm, low, high)[0]


    ready = pltpu.with_memory_space_constraint(own, pltpu.HBM)
    wt = call(pad_kernel, "weight_pad", [VMEM, ANY], [((PAD, HW), BF)], weight=COVER_PAD)(
        w_down[0].T, ready
    )[0]
    parts = [wt] + [shift(wt, "yl", NY, j) for j in range(1, NY)]
    w4 = call(weight_kernel, "weight_part", [SMEM] + [VMEM] * NY, [((NY, PAD, HW), BF)])(
        pos, *parts
    )[0].reshape(NY * PAD, HW)
    weight = lax.all_gather(w4, "z", axis=0, tiled=True)

    high_out, pm_out, _ = lax.optimization_barrier((high, pm, own))
    high_par = shift(high_out, "yh", 2, 1)
    hid_par = call(other_kernel, "send_other", [SMEM] + [VMEM] * 4, [((HSLOT, HW), BF)])(
        pos, ht, gates, rt, pm_out
    )[0]
    hid_par = shift(hid_par, "yh", 2, 1)
    own = exchange(own.reshape(HALF, CAP, WIDE + HW), ("x", "c")).reshape(HSLOT, WIDE + HW)

    def forward(x, after):
        width = x.shape[1]
        x, _ = lax.optimization_barrier((x, after))
        return exchange(x.reshape(HALF, CAP, width), ("x", "c")).reshape(HSLOT, width)

    par_low = call(
        low_kernel,
        "send_low",
        [VMEM],
        [((HSLOT, CW), BF)],
        spread_scratch(CW),
        where=ANY,
        weight=COVER_LOW,
    )(low_par)[0]
    par_low = forward(par_low, own)
    par_high = call(
        high_kernel,
        "send_high",
        [VMEM] * 3,
        [((HSLOT, CW + HW), BF)],
        spread_scratch(CW + HW),
        where=ANY,
        weight=COVER,
    )(high_par, low_par, hid_par)[0]
    par_high = forward(par_high, par_low)

    terms = call(
        term_kernel,
        "grad_term",
        [VMEM, ANY, VMEM],
        [((NDP * SENT, 128), BF)],
        [
            pltpu.VMEM((HSLOT, CW), BF),
            pltpu.VMEM((NY, SENT, 128), F32),
            pltpu.VMEM((NDP * SENT, 128), BF),
            pltpu.SemaphoreType.DMA((NZ + 1,)),
        ],
        mib=20,
        where=ANY,
    )(own, held(par_low), par_high)[0]
    terms, weight = lax.optimization_barrier((terms, weight))
    terms = exchange(terms.reshape(NDP, SENT, 128), ("z", "yl"))

    backs = call(
        back_kernel,
        "back_product",
        [SMEM] + [VMEM] * 4,
        [((2, CAP, FFW), BF)] * HALF,
        [pltpu.VMEM((HSLOT, FFW), F32)],
        mib=20,
    )(pos, own, par_low, par_high, weight)
    backs = [to_peer(b, r) for r, b in enumerate(backs)]
    other = call(stack_kernel, "stack_other", [VMEM] * HALF, [((HALF, CAP, FFW), BF)])(*backs)[0]
    other = shift(other, "yh", 2, 1)
    gh, gg = call(
        home_kernel,
        "bring_home",
        [SMEM] + [VMEM] * (5 + HALF),
        [((TOPK, FFW, ROWS), F32), ((TOPK, ROWS), F32)],
    )(pos, ht, gates, pm, rt, other, *backs)
    terms, gg = lax.optimization_barrier((terms, gg))
    gd = call(sum_kernel, "sum_terms", [VMEM], [((OWN, FFW), F32)], [pltpu.VMEM((SENT, 128), F32)])(terms)[0]
    return gd.T[None], jnp.transpose(gh, (2, 0, 1)), gg.T


def solution(mesh):
    every = ("z", "yl", "x", "yh", "c")
    fine = Mesh(mesh.devices.reshape(NZ, NY, NX, 2, 2), every)
    rows2 = P(every, None)
    rows3 = P(every, None, None)
    cols = P(("x", "yh", "c"), None, ("z", "yl"))
    return jax.shard_map(
        local,
        mesh=fine,
        in_specs=(rows2, rows3, rows2, rows2, rows2, rows2, cols),
        out_specs=(cols, rows3, rows2),
        check_vma=False,
    )
```

```python
import jax
import jax.numpy as jnp
from jax import lax
from jax.experimental import pallas as pl
from jax.experimental.pallas import tpu as pltpu
from jax.sharding import Mesh, PartitionSpec as P

BF = jnp.bfloat16
F32 = jnp.float32
I32 = jnp.int32
NT = (((1,), (1,)), ((), ()))
TN = (((0,), (0,)), ((), ()))
NN = (((1,), (0,)), ((), ()))
ROWS, D, TOPK, FFW, NEXP, CAP = 128, 2880, 4, 360, 16, 40
NZ, NY, NX = 8, 4, 4
NDP = NZ * NY
OWN = D // NDP
PAD = 96
WIDE = NDP * PAD
SLABS = ((0, 128), (128, 256), (256, FFW))
SENT = 272
HALF = NEXP // 2
HSLOT = HALF * CAP
STEP = 768
HW = 384
COVER_PAD = 50_000_000_000
COVER_LOW = 10_000_000_000
COVER = 50_000_000_000
BLK = NY * PAD
CW = WIDE // 2
def spread_scratch(width):
    return [pltpu.VMEM((HSLOT, width), BF), pltpu.SemaphoreType.DMA((WIDE // STEP + 1,))]


VMEM = pl.BlockSpec(memory_space=pltpu.VMEM)
SMEM = pl.BlockSpec(memory_space=pltpu.SMEM)
ANY = pl.BlockSpec(memory_space=pltpu.HBM)


def call(body, name, ins, outs, scratch=(), mib=14, weight=None, where=None):
    outs = [(pltpu.HBM if where else jax.ShapeDtypeStruct)(*o) for o in outs]
    return pl.pallas_call(
        body,
        in_specs=list(ins),
        out_specs=[where or VMEM] * len(outs),
        out_shape=outs,
        scratch_shapes=list(scratch),
        compiler_params=pltpu.CompilerParams(vmem_limit_bytes=mib << 20),
        name=name,
        cost_estimate=weight and pl.CostEstimate(flops=weight, transcendentals=0, bytes_accessed=0),
    )


def expert_ids():
    row = lax.broadcasted_iota(I32, (NEXP, ROWS), 0)
    return ((row >> 1) & 3) * 4 + (row >> 3) * 2 + (row & 1)


def slot_onehot(place, n):
    c = lax.broadcasted_iota(I32, (n, CAP, ROWS), 1).astype(F32)
    return (place[:, None, :] == c).astype(F32).reshape(n * CAP, ROWS)


def prep_kernel(pos_ref, len_hbm, adv_hbm, g_hbm, r_hbm, low_ref, high_ref, pm_ref, *refs):
    g_ref, r_ref, len_ref, adv_ref, scr, sems = refs
    pairs = [(g_hbm, g_ref), (r_hbm, r_ref), (len_hbm, len_ref), (adv_hbm, adv_ref)]
    copies = [pltpu.make_async_copy(a, b, sems.at[i]) for i, (a, b) in enumerate(pairs)]
    for c in copies:
        c.start()
    for c in copies[1:]:
        c.wait()
    eid = expert_ids()
    hit = r_ref[0:1] == eid
    for k in range(1, TOPK):
        hit = hit | (r_ref[k : k + 1] == eid)
    a = lax.broadcasted_iota(I32, (ROWS, ROWS), 0)
    b = lax.broadcasted_iota(I32, (ROWS, ROWS), 1)
    before = (a < b).astype(F32).astype(BF)
    rank = lax.dot_general(hit.astype(F32).astype(BF), before, NN, preferred_element_type=F32)
    place = jnp.where(hit, rank, -1.0)
    pm_ref[...] = place
    other = jnp.where(pos_ref[2] == 0, place[HALF:], place[:HALF])
    low_ref[CW:] = jnp.concatenate([other, jnp.zeros((HALF, ROWS), F32)], axis=0).astype(BF)
    pos = lax.broadcasted_iota(I32, (8, ROWS), 1)
    start = jnp.int32(0)
    scale = jnp.zeros((8, ROWS), F32)
    for s in range(4):
        n = len_ref[0, s]
        ratio = jnp.full((8, ROWS), adv_ref[0, s], F32) / jnp.full((8, ROWS), n, I32).astype(F32)
        scale = jnp.where((pos >= start) & (pos < start + n), ratio, scale)
        start = start + n
    copies[0].wait()
    scr[0:D] = g_ref[...].astype(F32) * scale[0:1]
    scr[D:] = jnp.zeros((8, ROWS), F32)
    keep = lax.broadcasted_iota(I32, (PAD, ROWS), 0) < OWN
    for d in range(NDP):
        block = scr[d * OWN : d * OWN + PAD]
        cot_ref, at = (low_ref, d * PAD) if d < NDP // 2 else (high_ref, d * PAD - CW)
        cot_ref[at : at + PAD] = jnp.where(keep, block, 0.0).astype(BF)


def prep(pos, lens, adv, gt, rt):
    outs = [((CW + 16, ROWS), BF), ((CW, ROWS), BF), ((NEXP, ROWS), F32)]
    scratch = [
        pltpu.VMEM((D, ROWS), BF),
        pltpu.VMEM((TOPK, ROWS), I32),
        pltpu.SMEM((1, 4), I32),
        pltpu.SMEM((1, 4), F32),
        pltpu.VMEM((D + 8, ROWS), F32),
        pltpu.SemaphoreType.DMA((4,)),
    ]
    args = [pltpu.with_memory_space_constraint(v, pltpu.HBM) for v in (lens, adv, gt, rt)]
    return call(prep_kernel, "prep", [SMEM] + [ANY] * 4, outs, scratch)(pos, *args)


def send(copies, scr, out_hbm, at, n, sems):
    cols = pl.ds(at, n)
    copies.append(pltpu.make_async_copy(scr.at[:, cols], out_hbm.at[:, cols], sems.at[len(copies)]))
    copies[-1].start()


def spread(s, cots, scr, out_hbm, sems):
    copies = []
    for n, cot_ref in enumerate(cots):
        for i in range(0, CW, STEP):
            at = n * CW + i
            scr[:, at : at + STEP] = lax.dot_general(
                s, cot_ref[i : i + STEP], NT, preferred_element_type=F32
            ).astype(BF)
            send(copies, scr, out_hbm, at, STEP, sems)
    return copies


def hidden_rows(h_ref, gate_ref, r_ref, place, eid):
    n = place.shape[0]
    acc = jnp.zeros((n * CAP, HW), F32)
    for k in range(TOPK):
        s = slot_onehot(jnp.where(r_ref[k : k + 1] == eid, place, -1.0), n).astype(BF)
        rows = jnp.concatenate(
            [h_ref[k], gate_ref[k : k + 1], jnp.zeros((HW - FFW - 1, ROWS), BF)], axis=0
        )
        acc = acc + lax.dot_general(s, rows, NT, preferred_element_type=F32)
    return acc.astype(BF)


def other_kernel(pos_ref, h_ref, gate_ref, r_ref, pm_ref, out_ref):
    first = pos_ref[2] == 0
    eid = expert_ids()
    place = jnp.where(first, pm_ref[HALF:], pm_ref[:HALF])
    out_ref[...] = hidden_rows(h_ref, gate_ref, r_ref, place, jnp.where(first, eid[HALF:], eid[:HALF]))


def own_kernel(pos_ref, h_hbm, gate_hbm, r_hbm, pm_ref, low_ref, high_ref, out_hbm, *refs):
    h_ref, gate_ref, r_ref, sem_in, scr, sems = refs
    pairs = [(h_hbm, h_ref), (gate_hbm, gate_ref), (r_hbm, r_ref)]
    loads = [pltpu.make_async_copy(a, b, sem_in.at[i]) for i, (a, b) in enumerate(pairs)]
    for c in loads:
        c.start()
    first = pos_ref[2] == 0
    eid = expert_ids()
    place = jnp.where(first, pm_ref[:HALF], pm_ref[HALF:])
    copies = spread(slot_onehot(place, HALF).astype(BF), (low_ref, high_ref), scr, out_hbm, sems)
    for c in loads:
        c.wait()
    scr[:, WIDE:] = hidden_rows(
        h_ref, gate_ref, r_ref, place, jnp.where(first, eid[:HALF], eid[HALF:])
    )
    send(copies, scr, out_hbm, WIDE, HW, sems)
    for c in copies:
        c.wait()


def low_kernel(cot_ref, out_hbm, scr, sems):
    place = cot_ref[CW:].astype(F32)[:HALF]
    for c in spread(slot_onehot(place, HALF).astype(BF), (cot_ref,), scr, out_hbm, sems):
        c.wait()


def high_kernel(cot_ref, pm_ref, h_ref, out_hbm, scr, sems):
    place = pm_ref[CW:].astype(F32)[:HALF]
    copies = spread(slot_onehot(place, HALF).astype(BF), (cot_ref,), scr, out_hbm, sems)
    scr[:, CW:] = h_ref[...]
    send(copies, scr, out_hbm, CW, HW, sems)
    for c in copies:
        c.wait()


def term_kernel(own_ref, low_hbm, high_ref, out_hbm, low_ref, pack, scr, sems):
    load = pltpu.make_async_copy(low_hbm, low_ref, sems.at[NZ])
    load.start()
    pack[...] = jnp.zeros((NY, SENT, 128), F32)
    hid = [own_ref[:, WIDE:], high_ref[:, CW:]]
    gate = [h[:, FFW : FFW + 1].astype(F32) for h in hid]
    copies = []
    for z in [*range(NZ // 2, NZ), *range(NZ // 2)]:
        if z == 0:
            load.wait()
        acc = jnp.zeros((BLK, FFW), F32)
        at = z * BLK
        cots = [own_ref[:, at : at + BLK]]
        cots.append(low_ref[:, at : at + BLK] if at < CW else high_ref[:, at - CW : at - CW + BLK])
        for cot, h, g in zip(cots, hid, gate):
            gated = (cot.astype(F32) * g).astype(BF)
            acc = acc + lax.dot_general(gated, h[:, :FFW], TN, preferred_element_type=F32)
        for y in range(NY):
            v = acc[y * PAD : y * PAD + OWN]
            for n, (a, b) in enumerate(SLABS):
                pack[y, n * OWN : (n + 1) * OWN, : b - a] = v[:, a:b]
            at = (z * NY + y) * SENT
            scr[at : at + SENT] = pack[y].astype(BF)
        rows = pl.ds(z * NY * SENT, NY * SENT)
        copies.append(pltpu.make_async_copy(scr.at[rows], out_hbm.at[rows], sems.at[z]))
        copies[-1].start()
    for c in copies:
        c.wait()


def sum_kernel(x_ref, out_ref, scr):
    v = x_ref[0].astype(F32)
    for d in range(1, NDP):
        v = v + x_ref[d].astype(F32)
    scr[...] = v
    for n, (a, b) in enumerate(SLABS):
        out_ref[:, 0, a:b] = scr[n * OWN : (n + 1) * OWN, : b - a]


def pad_kernel(w_ref, _, out_ref):
    out_ref[...] = jnp.zeros((PAD, HW), BF)
    out_ref[:OWN, :FFW] = w_ref[...]


def weight_kernel(pos_ref, *refs):
    out_ref = refs[NY]
    for j in range(NY):
        out_ref[(pos_ref[1] + NY - j) % NY] = refs[j][...]


def peer(pos_ref, r, sign):
    dx, dc = r // 2, r % 2
    return ((pos_ref[3] + NX + sign * dx) % NX) * 2 + (pos_ref[4] + dc) % 2


def back_kernel(pos_ref, own_ref, low_ref, high_ref, w_ref, *refs):
    outs, scr = refs[:HALF], refs[HALF]
    for i in range(2):
        parts = (own_ref[:, :CW], own_ref[:, CW:WIDE]) if i == 0 else (low_ref[...], high_ref[:, :CW])
        acc = lax.dot_general(parts[0], w_ref[:CW, :FFW], NN, preferred_element_type=F32)
        scr[...] = acc + lax.dot_general(
            parts[1], w_ref[CW:, :FFW], NN, preferred_element_type=F32
        )
        for r, out_ref in enumerate(outs):
            at = pl.multiple_of(peer(pos_ref, r, 1) * CAP, 8)
            out_ref[i] = scr[pl.ds(at, CAP)].astype(BF)


def stack_kernel(*refs):
    for r in range(HALF):
        refs[HALF][r] = refs[r][1]


def home_kernel(pos_ref, h_ref, gate_ref, pm_ref, r_ref, other_ref, *refs):
    owns, gh_ref, gg_ref = refs[:HALF], refs[HALF], refs[HALF + 1]
    gate = gate_ref[...].astype(F32)
    c = lax.broadcasted_iota(I32, (CAP, ROWS), 0).astype(F32)
    yh = pos_ref[2]
    pieces, places, ids = [], [], []
    for half in range(2):
        side = yh if half == 0 else 1 - yh
        for r in range(HALF):
            i = peer(pos_ref, r, -1)
            pieces.append((owns[r][0] if half == 0 else other_ref[r]).astype(F32))
            places.append(pm_ref[pl.ds(side * HALF + i, 1)])
            ids.append((i // 2) * 4 + side * 2 + i % 2)
    x = jnp.concatenate(pieces, axis=0).astype(BF)
    for k in range(TOPK):
        rk = r_ref[k : k + 1]
        rows = [
            (jnp.where(rk == e, p, -1.0) == c).astype(F32) for p, e in zip(places, ids)
        ]
        s = jnp.concatenate(rows, axis=0).astype(BF)
        back = lax.dot_general(x, s, TN, preferred_element_type=F32)
        gh_ref[k] = back * gate[k : k + 1]
        gg_ref[k : k + 1] = jnp.sum(back * h_ref[k].astype(F32), axis=0, keepdims=True)


def shift(x, axis, n, by):
    return lax.ppermute(x, axis, [(i, (i + by) % n) for i in range(n)])


def held(x):
    return pltpu.with_memory_space_constraint(x, pltpu.HBM)


def to_peer(x, r):
    dx, dc = r // 2, r % 2
    if r == 0:
        return x
    pairs = [(i, ((i // 2 + dx) % NX) * 2 + (i + dc) % 2) for i in range(HALF)]
    return lax.ppermute(x, ("x", "c"), pairs)


def exchange(x, axes):
    return lax.all_to_all(x, axes, split_axis=0, concat_axis=0, tiled=True)


def local(grad_out, hidden_act, gate_weights, routing, resp_lengths, advantage, w_down):
    pos = jnp.stack([lax.axis_index(a).astype(I32) for a in ("z", "yl", "yh", "x", "c")])
    gt = grad_out.T
    ht = jnp.transpose(hidden_act, (1, 2, 0))
    gates = gate_weights.T
    rt = routing.T

    low, high, pm = prep(pos, resp_lengths, advantage, gt, rt)
    low_par = shift(low, "yh", 2, 1)
    own = call(
        own_kernel,
        "send_own",
        [SMEM] + [ANY] * 3 + [VMEM] * 3,
        [((HSLOT, WIDE + HW), BF)],
        [
            pltpu.VMEM((TOPK, FFW, ROWS), BF),
            pltpu.VMEM((TOPK, ROWS), BF),
            pltpu.VMEM((TOPK, ROWS), I32),
            pltpu.SemaphoreType.DMA((3,)),
        ]
        + spread_scratch(WIDE + HW),
        where=ANY,
    )(pos, *(pltpu.with_memory_space_constraint(v, pltpu.HBM) for v in (ht, gates, rt)), pm, low, high)[0]


    ready = pltpu.with_memory_space_constraint(own, pltpu.HBM)
    wt = call(pad_kernel, "weight_pad", [VMEM, ANY], [((PAD, HW), BF)], weight=COVER_PAD)(
        w_down[0].T, ready
    )[0]
    parts = [wt] + [shift(wt, "yl", NY, j) for j in range(1, NY)]
    w4 = call(weight_kernel, "weight_part", [SMEM] + [VMEM] * NY, [((NY, PAD, HW), BF)])(
        pos, *parts
    )[0].reshape(NY * PAD, HW)
    weight = lax.all_gather(w4, "z", axis=0, tiled=True)

    high_out, pm_out, _ = lax.optimization_barrier((high, pm, own))
    high_par = shift(high_out, "yh", 2, 1)
    hid_par = call(other_kernel, "send_other", [SMEM] + [VMEM] * 4, [((HSLOT, HW), BF)])(
        pos, ht, gates, rt, pm_out
    )[0]
    hid_par = shift(hid_par, "yh", 2, 1)
    own = exchange(own.reshape(HALF, CAP, WIDE + HW), ("x", "c")).reshape(HSLOT, WIDE + HW)

    def forward(x, after):
        width = x.shape[1]
        x, _ = lax.optimization_barrier((x, after))
        return exchange(x.reshape(HALF, CAP, width), ("x", "c")).reshape(HSLOT, width)

    par_low = call(
        low_kernel,
        "send_low",
        [VMEM],
        [((HSLOT, CW), BF)],
        spread_scratch(CW),
        where=ANY,
        weight=COVER_LOW,
    )(low_par)[0]
    par_low = forward(par_low, own)
    par_high = call(
        high_kernel,
        "send_high",
        [VMEM] * 3,
        [((HSLOT, CW + HW), BF)],
        spread_scratch(CW + HW),
        where=ANY,
        weight=COVER,
    )(high_par, low_par, hid_par)[0]
    par_high = forward(par_high, par_low)

    terms = call(
        term_kernel,
        "grad_term",
        [VMEM, ANY, VMEM],
        [((NDP * SENT, 128), BF)],
        [
            pltpu.VMEM((HSLOT, CW), BF),
            pltpu.VMEM((NY, SENT, 128), F32),
            pltpu.VMEM((NDP * SENT, 128), BF),
            pltpu.SemaphoreType.DMA((NZ + 1,)),
        ],
        mib=20,
        where=ANY,
    )(own, held(par_low), par_high)[0]
    terms, weight = lax.optimization_barrier((terms, weight))
    terms = exchange(terms.reshape(NDP, SENT, 128), ("z", "yl"))

    backs = call(
        back_kernel,
        "back_product",
        [SMEM] + [VMEM] * 4,
        [((2, CAP, FFW), BF)] * HALF,
        [pltpu.VMEM((HSLOT, FFW), F32)],
        mib=20,
    )(pos, own, par_low, par_high, weight)
    backs = [to_peer(b, r) for r, b in enumerate(backs)]
    other = call(stack_kernel, "stack_other", [VMEM] * HALF, [((HALF, CAP, FFW), BF)])(*backs)[0]
    other = shift(other, "yh", 2, 1)
    gh, gg = call(
        home_kernel,
        "bring_home",
        [SMEM] + [VMEM] * (5 + HALF),
        [((TOPK, FFW, ROWS), F32), ((TOPK, ROWS), F32)],
    )(pos, ht, gates, pm, rt, other, *backs)
    terms, gg = lax.optimization_barrier((terms, gg))
    gd = call(sum_kernel, "sum_terms", [VMEM], [((OWN, 1, FFW), F32)], [pltpu.VMEM((SENT, 128), F32)])(terms)[0]
    return jnp.transpose(gd, (1, 2, 0)), jnp.transpose(gh, (2, 0, 1)), gg.T


def solution(mesh):
    every = ("z", "yl", "x", "yh", "c")
    fine = Mesh(mesh.devices.reshape(NZ, NY, NX, 2, 2), every)
    rows2 = P(every, None)
    rows3 = P(every, None, None)
    cols = P(("x", "yh", "c"), None, ("z", "yl"))
    return jax.shard_map(
        local,
        mesh=fine,
        in_specs=(rows2, rows3, rows2, rows2, rows2, rows2, cols),
        out_specs=(cols, rows3, rows2),
        check_vma=False,
    )
```
